32 devices in a mesh: dp: 8 (over z, x), mp: 4 (over y, core).
Axes of the slice: x: 2, y: 2, z: 4, core: 2. Of those that a mesh axis runs over, the one named last changes fastest.
Arguments:
- tokens: bfloat16 [8192, 2048], P('dp'), may hold values from -8 to 8
- segment_ids: int32 [8192], P('dp'), may hold values from 0 to 3, as said below
- out_grad: bfloat16 [8192, 2048], P('dp'), may hold values from -8 to 8
- query_weight: float32 [2048, 2048], P('dp', 'mp'), may hold values from -0.125 to 0.125
- keyval_weight: float32 [2, 2048, 512], P(None, ('dp', 'mp')), may hold values from -0.125 to 0.125
- output_weight: float32 [2048, 2048], P('mp', 'dp'), may hold values from -1 to 1
- gateup_weight: float32 [2, 2048, 5632], P(None, 'dp', 'mp'), may hold values from -0.125 to 0.125
- down_weight: float32 [5632, 2048], P('mp', 'dp'), may hold values from -0.078125 to 0.078125
- norm_gains: float32 [2, 2048], P(None, 'dp'), may hold values from 0.5 to 1.5
- query_moment: float32 [2048, 2048], P('dp', 'mp'), may hold values from -9.1552734e-05 to 9.1552734e-05
- keyval_moment: float32 [2, 2048, 512], P(None, ('dp', 'mp')), may hold values from -9.1552734e-05 to 9.1552734e-05
- output_moment: float32 [2048, 2048], P('mp', 'dp'), may hold values from -5.340576e-05 to 5.340576e-05
- gateup_moment: float32 [2, 2048, 5632], P(None, 'dp', 'mp'), may hold values from -9.1552734e-05 to 9.1552734e-05
- down_moment: float32 [5632, 2048], P('mp', 'dp'), may hold values from -9.1552734e-05 to 9.1552734e-05
- gains_moment: float32 [2, 2048], P(None, 'dp'), may hold values from -0.00030517578 to 0.00030517578
- query_square: float32 [2048, 2048], P('dp', 'mp'), may hold values from 1.1753523e-09 to 4.657056e-09
- keyval_square: float32 [2, 2048, 512], P(None, ('dp', 'mp')), may hold values from 1.1753523e-09 to 4.657056e-09
- output_square: float32 [2048, 2048], P('mp', 'dp'), may hold values from 2.2176458e-10 to 8.870583e-10
- gateup_square: float32 [2, 2048, 5632], P(None, 'dp', 'mp'), may hold values from 1.1753523e-09 to 4.657056e-09
- down_square: float32 [5632, 2048], P('mp', 'dp'), may hold values from 1.1753523e-09 to 4.657056e-09
- gains_square: float32 [2, 2048], P(None, 'dp'), may hold values from 1.0422935e-08 to 4.213527e-08
Outputs:
- layer_out: bfloat16 [8192, 2048], P('dp')
- input_grad: float32 [8192, 2048], P('dp')
- grad_norm: float32 [], replicated
- query_next: float32 [2048, 2048], P('dp', 'mp')
- keyval_next: float32 [2, 2048, 512], P(None, ('dp', 'mp'))
- output_next: float32 [2048, 2048], P('mp', 'dp')
- gateup_next: float32 [2, 2048, 5632], P(None, 'dp', 'mp')
- down_next: float32 [5632, 2048], P('mp', 'dp')
- gains_next: float32 [2, 2048], P(None, 'dp')
- moment_query: float32 [2048, 2048], P('dp', 'mp')
- moment_keyval: float32 [2, 2048, 512], P(None, ('dp', 'mp'))
- moment_output: float32 [2048, 2048], P('mp', 'dp')
- moment_gateup: float32 [2, 2048, 5632], P(None, 'dp', 'mp')
- moment_down: float32 [5632, 2048], P('mp', 'dp')
- moment_gains: float32 [2, 2048], P(None, 'dp')
- square_query: float32 [2048, 2048], P('dp', 'mp')
- square_keyval: float32 [2, 2048, 512], P(None, ('dp', 'mp'))
- square_output: float32 [2048, 2048], P('mp', 'dp')
- square_gateup: float32 [2, 2048, 5632], P(None, 'dp', 'mp')
- square_down: float32 [5632, 2048], P('mp', 'dp')
- square_gains: float32 [2, 2048], P(None, 'dp')
The draws below stay inside these ranges and needn't reach their ends.
Inputs may be any that keep to these rules, and one draw needn't show every extreme that they name: `segment_ids`: in each block of 1024 rows the ids start at 0 and never fall; a block holds 1, 2 or 4 whole sequences of equal length; the first block holds one sequence and the second holds four.
All inputs are finite; a program needn't handle non-finite values.
Results may differ from the reference program's by a relative error of at most 0.015.
Values may be sent and summed in bfloat16 or wider, within the bound.
A program may use at most 320 MiB of HBM per device.

```python
import math
import jax
import jax.numpy as jnp
from jax import lax

D = 2048
H = 16
KV = 4
HD = 128
FF = 5632
TOK_DEV = 1024
ADAM_STEP = 10
TOKENS = 8192
NPARAM = 45092864
N_DP = 8
N_MP = 4


def draw_segment_ids(key, part):
    blocks = TOKENS // TOK_DEV
    power_two = jax.random.randint(key, (blocks,), 0, 3)
    block_index = jnp.arange(blocks, dtype=jnp.int32)
    power_two = jnp.where(block_index == 0, 0, jnp.where(block_index == 1, 2, power_two))
    length = TOK_DEV // jnp.left_shift(jnp.ones_like(power_two), power_two)
    position = jnp.arange(TOK_DEV, dtype=jnp.int32)
    return (position[None, :] // length[:, None]).reshape(-1).astype(jnp.int32)


def ramped_rows(key, salt):
    own_key = jax.random.fold_in(key, salt)
    value_key, column_key = jax.random.split(own_key)
    place = jnp.arange(D, dtype=jnp.float32) / (D - 1.0)
    jitter = jax.random.uniform(column_key, (D,), jnp.float32, 0.7, 1.4)
    ramp = 3.0 ** place
    values = jnp.clip(jax.random.normal(value_key, (TOKENS, D), jnp.float32), -4.0, 4.0)
    column_scale = ramp * jitter
    column_scale = column_scale / jnp.sqrt(jnp.mean(column_scale * column_scale))
    return (values * column_scale[None, :]).astype(jnp.bfloat16)


def draw_tokens(key, part):
    return ramped_rows(key, 101)


def draw_out_grad(key, part):
    return ramped_rows(key, 202)


def shard_levels(stream_key, shape, cuts, least, top_value):
    def one(axis_at, shards_of):
        steps = jax.random.uniform(jax.random.fold_in(jax.random.fold_in(stream_key, 6), axis_at), (shards_of,), jnp.float32, least / len(cuts), top_value / len(cuts))
        return jnp.repeat(jnp.exp(steps), shape[axis_at] // shards_of).reshape((-1,) + (1,) * (len(shape) - axis_at - 1))

    factor_of = one(*cuts[0])
    for cut in cuts[1:]:
        factor_of = factor_of * one(*cut)
    return factor_of


def scatter_about(key, dims, spread, limit, cuts=(), kind=jnp.bfloat16):
    level = shard_levels(key, dims, cuts, -0.22, 0.18) if cuts else 1.0
    values = jax.random.normal(key, dims, jnp.float32) * spread * level
    return jnp.minimum(jnp.maximum(values, -limit), limit).astype(kind)


def setup_inputs(seed: int = 0) -> dict:
    splits = jax.random.split(jax.random.key(seed), 22)
    return {
        "tokens": draw_tokens(jax.random.fold_in(splits[21], 71), 0),
        "segment_ids": draw_segment_ids(jax.random.fold_in(splits[21], 71), 0),
        "out_grad": draw_out_grad(jax.random.fold_in(splits[21], 71), 0),
        "query_weight": scatter_about(splits[3], (D, H * HD), D ** -0.5, 0.125, ((0, 8), (1, 4)), jnp.float32),
        "keyval_weight": scatter_about(splits[4], (2, D, KV * HD), D ** -0.5, 0.125, ((1, 32),), jnp.float32),
        "output_weight": scatter_about(splits[5], (H * HD, D), (H * HD * 16 // TOK_DEV) ** -0.5, 1.0, ((0, 4), (1, 8)), jnp.float32),
        "gateup_weight": scatter_about(splits[6], (2, D, FF), D ** -0.5, 0.125, ((1, 8), (2, 4)), jnp.float32),
        "down_weight": scatter_about(splits[7], (FF, D), FF ** -0.5, 0.078125, ((0, 4), (1, 8)), jnp.float32),
        "norm_gains": jnp.clip(1.0 + 0.1 * jax.random.normal(splits[8], (2, D), jnp.float32), 0.5, 1.5),
        "query_moment": scatter_about(splits[9], (D, H * HD), (0.11 / NPARAM ** 0.5), 9.1552734375e-05, ((0, 8), (1, 4)), jnp.float32),
        "keyval_moment": scatter_about(splits[10], (2, D, KV * HD), (0.11 / NPARAM ** 0.5), 9.1552734375e-05, ((1, 32),), jnp.float32),
        "output_moment": scatter_about(splits[11], (H * HD, D), (0.06 / NPARAM ** 0.5), 5.340576171875e-05, ((0, 4), (1, 8)), jnp.float32),
        "gateup_moment": scatter_about(splits[12], (2, D, FF), (0.11 / NPARAM ** 0.5), 9.1552734375e-05, ((1, 8), (2, 4)), jnp.float32),
        "down_moment": scatter_about(splits[13], (FF, D), (0.11 / NPARAM ** 0.5), 9.1552734375e-05, ((0, 4), (1, 8)), jnp.float32),
        "gains_moment": scatter_about(splits[14], (2, D), (0.33 / NPARAM ** 0.5), 0.00030517578, ((1, 8),), jnp.float32),
        "query_square": jnp.clip(jnp.exp(math.log(4.657056074108823e-09) - 1.3768156 * jax.random.uniform(splits[15], (D, H * HD), jnp.float32) ** shard_levels(splits[15], (D, H * HD), ((0, 8), (1, 4)), -0.2, 0.2)), 1.175352259963347e-09, 4.657056074108823e-09),
        "keyval_square": jnp.clip(jnp.exp(math.log(4.657056074108823e-09) - 1.3768156 * jax.random.uniform(splits[16], (2, D, KV * HD), jnp.float32) ** shard_levels(splits[16], (2, D, KV * HD), ((1, 32),), -0.2, 0.2)), 1.175352259963347e-09, 4.657056074108823e-09),
        "output_square": jnp.clip(jnp.exp(math.log(8.870583156905809e-10) - 1.3862944 * jax.random.uniform(splits[17], (H * HD, D), jnp.float32) ** shard_levels(splits[17], (H * HD, D), ((0, 4), (1, 8)), -0.2, 0.2)), 2.2176457892264523e-10, 8.870583156905809e-10),
        "gateup_square": jnp.clip(jnp.exp(math.log(4.657056074108823e-09) - 1.3768156 * jax.random.uniform(splits[18], (2, D, FF), jnp.float32) ** shard_levels(splits[18], (2, D, FF), ((1, 8), (2, 4)), -0.2, 0.2)), 1.175352259963347e-09, 4.657056074108823e-09),
        "down_square": jnp.clip(jnp.exp(math.log(4.657056074108823e-09) - 1.3768156 * jax.random.uniform(splits[19], (FF, D), jnp.float32) ** shard_levels(splits[19], (FF, D), ((0, 4), (1, 8)), -0.2, 0.2)), 1.175352259963347e-09, 4.657056074108823e-09),
        "gains_square": jnp.clip(jnp.exp(math.log(4.213526949570223e-08) - 1.3968764 * jax.random.uniform(splits[20], (2, D), jnp.float32) ** shard_levels(splits[20], (2, D), ((1, 8),), -0.2, 0.2)), 1.0422935403653355e-08, 4.213526949570223e-08),
    }


@jax.custom_vjp
def low(v):
    return lax.optimization_barrier(v.astype(jnp.bfloat16)).astype(jnp.float32)

@jax.custom_vjp
def low_back(v):
    return v

def low_keep(v):
    return (low(v), None)

def low_pass(kept, grad):
    return (grad,)

def back_keep(v):
    return (v, None)

def back_low(kept, grad):
    return (low(grad),)
low.defvjp(low_keep, low_pass)
low_back.defvjp(back_keep, back_low)
norm_eps = 1e-05
rope_base = 10000.0
clip_limit = 1.0
beta_first = 0.9
beta_second = 0.95
adam_eps = 1e-08
weight_decay = 0.1
matrix_rate = 0.02
gain_rate = 0.6

def positions(segment):
    row_count = segment.shape[0]
    row_index = jnp.arange(row_count, dtype=jnp.int32)
    fresh_start = jnp.concatenate([jnp.ones((1,), dtype=jnp.bool_), segment[1:] != segment[:-1]])
    seg_start = lax.cummax(jnp.where(fresh_start, row_index, jnp.zeros_like(row_index)), axis=0)
    return row_index - seg_start

def rope_tables(segment, width):
    half_width = width // 2
    angle_rate = rope_base ** (-(jnp.arange(half_width, dtype=jnp.float32) * 2.0 / width))
    angles = positions(segment).astype(jnp.float32)[:, None] * angle_rate[None, :]
    return (jnp.cos(angles), jnp.sin(angles))

def rotate(tensor_in, cosine_table, sine_table):
    half_width = tensor_in.shape[-1] // 2
    lower_half = tensor_in[..., :half_width]
    upper_half = tensor_in[..., half_width:]
    return jnp.concatenate([lower_half * cosine_table - upper_half * sine_table, upper_half * cosine_table + lower_half * sine_table], axis=-1)

def rms_norm(values_in, gain_vec):
    inv_rms = lax.rsqrt(lax.optimization_barrier(jnp.mean(values_in * values_in, axis=-1, keepdims=True)) + norm_eps)
    return values_in * inv_rms * gain_vec

def layer_block(inputs, segment, query_weight, keyval_weight, output_weight, gateup_weight, down_weight, norm_gains):
    highest = lax.Precision.HIGHEST
    row_count = inputs.shape[0]
    local_heads = H // N_MP
    act_one = low(rms_norm(inputs, norm_gains[0]))
    query_raw = low_back(jnp.dot(act_one, query_weight, precision=highest)).reshape(row_count, H, HD)
    kv_owner = jnp.arange(N_MP, dtype=jnp.int32) * local_heads // (H // KV)
    key_cols = jnp.take(keyval_weight[0].reshape(D, KV, HD), kv_owner, axis=1).reshape(D, N_MP * HD)
    value_cols = jnp.take(keyval_weight[1].reshape(D, KV, HD), kv_owner, axis=1).reshape(D, N_MP * HD)
    key_raw = low_back(jnp.dot(act_one, key_cols, precision=highest)).reshape(row_count, N_MP, HD)
    value_low = low(low_back(jnp.dot(act_one, value_cols, precision=highest))).reshape(row_count, N_MP, HD)
    cosine_table, sine_table = rope_tables(segment, HD)
    cos_heads = cosine_table[:, None, :]
    sin_heads = sine_table[:, None, :]
    query_rot = low(rotate(query_raw, cos_heads, sin_heads)).reshape(row_count, N_MP, local_heads, HD)
    key_rot = low(rotate(key_raw, cos_heads, sin_heads))
    raw_scores = jnp.einsum('tmgd,smd->mgts', query_rot, key_rot, precision=highest)
    scores = low_back(raw_scores * HD ** (-0.5))
    row_index = jnp.arange(row_count, dtype=jnp.int32)
    allowed = (segment[:, None] == segment[None, :]) & (row_index[:, None] >= row_index[None, :])
    masked = jnp.where(allowed[None, None], scores, -1e+30)
    row_max = lax.optimization_barrier(jnp.max(masked, axis=-1, keepdims=True))
    exp_scores = jnp.exp(masked - row_max)
    weights_soft = exp_scores / lax.optimization_barrier(jnp.sum(exp_scores, axis=-1, keepdims=True))
    mixed_heads = jnp.einsum('mgts,smd->tmgd', low(weights_soft), value_low, precision=highest).reshape(row_count, H * HD)
    attn_low = low(low_back(mixed_heads))
    attn_out = low_back(jnp.dot(attn_low, output_weight, precision=highest))
    hidden_in = inputs + attn_out
    act_two = low(rms_norm(hidden_in, norm_gains[1]))
    gate_pre = low_back(jnp.dot(act_two, gateup_weight[0], precision=highest))
    up_proj = low_back(jnp.dot(act_two, gateup_weight[1], precision=highest))
    inner_act = low(jax.nn.silu(gate_pre) * up_proj)
    return hidden_in + low_back(jnp.dot(inner_act, down_weight, precision=highest))

def adam_update(weight, moment, square, gradient, factor, step_rate, decay_rate):
    clipped = gradient * factor
    moment_new = beta_first * moment + (1.0 - beta_first) * clipped
    square_new = beta_second * square + (1.0 - beta_second) * clipped * clipped
    first_fix = 1.0 - beta_first ** ADAM_STEP
    second_fix = 1.0 - beta_second ** ADAM_STEP
    step_dir = moment_new / first_fix / (jnp.sqrt(square_new / second_fix) + adam_eps)
    return (weight - step_rate * (step_dir + decay_rate * weight), moment_new, square_new)

def reference(tokens, segment_ids, out_grad, query_weight, keyval_weight, output_weight, gateup_weight, down_weight, norm_gains, query_moment, keyval_moment, output_moment, gateup_moment, down_moment, gains_moment, query_square, keyval_square, output_square, gateup_square, down_square, gains_square):
    weights = (query_weight, keyval_weight, output_weight, gateup_weight, down_weight, norm_gains)
    blocks = tokens.astype(jnp.float32).reshape(N_DP, TOK_DEV, D)
    segments = segment_ids.reshape(N_DP, TOK_DEV)

    def forward(inputs, params):
        rounded = tuple((low(tensor_part) for tensor_part in params))

        def one_block(scan_item):
            return jax.checkpoint(layer_block)(scan_item[0], scan_item[1], *rounded)
        return lax.map(one_block, (inputs, segments))
    outputs, pullback = jax.vjp(forward, blocks, weights)
    input_grads, gradients = pullback(out_grad.astype(jnp.float32).reshape(N_DP, TOK_DEV, D))
    square_total = jnp.float32(0.0)
    for tensor_part in gradients:
        square_total = square_total + jnp.sum(tensor_part * tensor_part)
    grad_norm = jnp.sqrt(square_total)
    factor = jnp.minimum(1.0, clip_limit / (grad_norm + 1e-06))
    moments = (query_moment, keyval_moment, output_moment, gateup_moment, down_moment, gains_moment)
    squares = (query_square, keyval_square, output_square, gateup_square, down_square, gains_square)
    output_rate = matrix_rate * (TOK_DEV * D / (16.0 * H * HD)) ** 0.5
    step_rates = (matrix_rate, matrix_rate, output_rate, matrix_rate, matrix_rate, gain_rate)
    updated = []
    for slot in range(6):
        decay_rate = 0.0 if slot == 5 else weight_decay
        updated.append(adam_update(weights[slot], moments[slot], squares[slot], gradients[slot], factor, step_rates[slot], decay_rate))
    layer_out = outputs.reshape(TOKENS, D).astype(jnp.bfloat16)
    input_grad = input_grads.reshape(TOKENS, D)
    return (layer_out, input_grad, grad_norm, updated[0][0], updated[1][0], updated[2][0], updated[3][0], updated[4][0], updated[5][0], updated[0][1], updated[1][1], updated[2][1], updated[3][1], updated[4][1], updated[5][1], updated[0][2], updated[1][2], updated[2][2], updated[3][2], updated[4][2], updated[5][2])
```

```python
import jax
import jax.numpy as jnp
from jax import lax
from jax.sharding import PartitionSpec as P

D = 2048
H = 16
KV = 4
HD = 128
TOK_DEV = 1024
ADAM_STEP = 10


norm_eps = 1e-05
rope_base = 10000.0
clip_limit = 1.0
beta_first = 0.9
beta_second = 0.95
adam_eps = 1e-08
weight_decay = 0.1
matrix_rate = 0.02
gain_rate = 0.6

low_type = jnp.bfloat16
f32 = jnp.float32


def positions(segment):
    row_count = segment.shape[0]
    row_index = jnp.arange(row_count, dtype=jnp.int32)
    fresh_start = jnp.concatenate([jnp.ones((1,), dtype=jnp.bool_), segment[1:] != segment[:-1]])
    seg_start = lax.cummax(jnp.where(fresh_start, row_index, jnp.zeros_like(row_index)), axis=0)
    return row_index - seg_start


def rope_tables(segment, width):
    half_width = width // 2
    angle_rate = rope_base ** (-(jnp.arange(half_width, dtype=jnp.float32) * 2.0 / width))
    angles = positions(segment).astype(jnp.float32)[:, None] * angle_rate[None, :]
    return (jnp.cos(angles), jnp.sin(angles))


def rotate(tensor_in, cosine_table, sine_table):
    half_width = tensor_in.shape[-1] // 2
    lower_half = tensor_in[..., :half_width]
    upper_half = tensor_in[..., half_width:]
    return jnp.concatenate(
        [
            lower_half * cosine_table - upper_half * sine_table,
            upper_half * cosine_table + lower_half * sine_table,
        ],
        axis=-1,
    )


def unrotate(gradient, cosine_table, sine_table):
    return rotate(gradient, cosine_table, -sine_table)


def adam_update(weight, moment, square, gradient, factor, step_rate, decay_rate):
    clipped = gradient * factor
    moment_new = beta_first * moment + (1.0 - beta_first) * clipped
    square_new = beta_second * square + (1.0 - beta_second) * clipped * clipped
    first_fix = 1.0 - beta_first**ADAM_STEP
    second_fix = 1.0 - beta_second**ADAM_STEP
    step_dir = moment_new / first_fix / (jnp.sqrt(square_new / second_fix) + adam_eps)
    return (weight - step_rate * (step_dir + decay_rate * weight), moment_new, square_new)


class Ring:
    def __init__(self, count):
        lo = 1
        while lo * lo * 4 <= count:
            lo *= 2
        self.count, self.lo, self.hi = count, lo, count // lo
        me = lax.axis_index("dp")
        self.h, self.l = me // lo, me % lo

    def hi_perm(self, k):
        hi, lo = self.hi, self.lo
        return [(h * lo + l, ((h + k) % hi) * lo + l) for h in range(hi) for l in range(lo)]

    def lo_perm(self, j):
        hi, lo = self.hi, self.lo
        return [(h * lo + l, h * lo + (l + j) % lo) for h in range(hi) for l in range(lo)]

    def owners(self):
        return [
            lax.rem(self.h - k + self.hi, self.hi) * self.lo
            + lax.rem(self.l - j + self.lo, self.lo)
            for j in range(self.lo)
            for k in range(self.hi)
        ]

    def relative(self, x):
        width = x.shape[-1] // self.count
        return jnp.concatenate(
            [lax.dynamic_slice_in_dim(x, o * width, width, x.ndim - 1) for o in self.owners()], -1
        )

    def natural(self, x):
        width = x.shape[-1] // self.count
        out = []
        for b in range(self.count):
            k = lax.rem(self.h - b // self.lo + self.hi, self.hi)
            j = lax.rem(self.l - b % self.lo + self.lo, self.lo)
            out.append(lax.dynamic_slice_in_dim(x, (j * self.hi + k) * width, width, x.ndim - 1))
        return jnp.concatenate(out, -1)

    def spread_hi(self, shard):
        return jnp.stack(
            [shard] + [lax.ppermute(shard, "dp", self.hi_perm(k)) for k in range(1, self.hi)]
        )

    def spread_lo(self, stack):
        return [stack] + [lax.ppermute(stack, "dp", self.lo_perm(j)) for j in range(1, self.lo)]

    def fold_lo(self, grad):
        grad = grad.reshape((self.lo, self.hi) + grad.shape[1:])
        total = grad[0].astype(f32)
        for j in range(1, self.lo):
            total = total + lax.ppermute(grad[j], "dp", self.lo_perm(-j)).astype(f32)
        return total

    def fold_hi(self, part):
        total = part[0]
        for k in range(1, self.hi):
            total = total + lax.ppermute(
                part[k].astype(low_type), "dp", self.hi_perm(-k)
            ).astype(f32)
        return total


def body(
    tokens,
    segment_ids,
    out_grad,
    query_weight,
    keyval_weight,
    output_weight,
    gateup_weight,
    down_weight,
    norm_gains,
    query_moment,
    keyval_moment,
    output_moment,
    gateup_moment,
    down_moment,
    gains_moment,
    query_square,
    keyval_square,
    output_square,
    gateup_square,
    down_square,
    gains_square,
):
    groups_dp = lax.axis_size("dp")
    groups_mp = lax.axis_size("mp")
    local_heads = H // groups_mp
    row_count = tokens.shape[0]
    quarter = row_count // groups_mp
    ring = Ring(groups_dp)
    mp_me = lax.axis_index("mp")
    block = D // groups_dp
    kv_rows = block // groups_mp
    qcols = query_weight.shape[1]
    ff = down_weight.shape[0]

    def mp_perm(s):
        return [(m, (m + s) % groups_mp) for m in range(groups_mp)]

    def head_of(m):
        return m * local_heads // (H // KV)

    kv_low = keyval_weight.astype(low_type)
    kv_block = jnp.zeros((2, block, HD), low_type)
    for s in range(groups_mp):
        target = lax.rem(mp_me + s, groups_mp)
        piece = lax.dynamic_slice_in_dim(kv_low, head_of(target) * HD, HD, 2)
        if s:
            piece = lax.ppermute(piece, "mp", mp_perm(s))
        source = lax.rem(mp_me - s + groups_mp, groups_mp)
        kv_block = lax.dynamic_update_slice_in_dim(kv_block, piece, source * kv_rows, 1)
    gain_rows = jnp.pad(
        norm_gains.astype(low_type), ((0, 14), (0, qcols + 2 * HD - block))
    )
    shard_first = jnp.concatenate(
        [
            jnp.concatenate([query_weight.astype(low_type), kv_block[0], kv_block[1]], axis=1),
            gain_rows,
        ],
        axis=0,
    )
    half_ff = ff // 2
    down_low = down_weight.astype(low_type)
    shards = [
        shard_first,
        output_weight.astype(low_type),
        gateup_weight[0].astype(low_type),
        gateup_weight[1].astype(low_type),
        down_low[:half_ff],
        down_low[half_ff:],
    ]
    axes = [0, 1, 0, 0, 1, 1]
    gathered = []
    stack = None
    for i, shard in enumerate(shards):
        if stack is not None:
            shard, stack = lax.optimization_barrier((shard, stack))
        new_stack = ring.spread_hi(shard)
        if stack is not None:
            gathered.append(ring.spread_lo(stack))
        stack = new_stack
    gathered.append(ring.spread_lo(stack))

    def join(pieces, axis):
        return jnp.concatenate(
            [p[k] for p in pieces for k in range(ring.hi)], axis=axis
        )

    first = jnp.concatenate(gathered[0], axis=0)
    qkv_full = first[:, :block].reshape(D, qcols + 2 * HD)
    gains = jnp.moveaxis(first[:, block : block + 2, :block], 0, 1).reshape(2, D).astype(f32)
    output_full = join(gathered[1], 1)
    gate_full = join(gathered[2], 0)
    up_full = join(gathered[3], 0)
    down_full = jnp.concatenate([join(gathered[4], 1), join(gathered[5], 1)], axis=0)

    def rows_sum(part):
        return lax.psum_scatter(
            part.astype(low_type), "mp", scatter_dimension=0, tiled=True
        ).astype(f32)

    def rows_all(own):
        return lax.all_gather(own, "mp", axis=0, tiled=True)

    def own_rows(x):
        return lax.dynamic_slice_in_dim(x, mp_me * quarter, quarter, 0)

    cosine_table, sine_table = rope_tables(segment_ids, HD)
    cos_heads = cosine_table[:, None, :]
    sin_heads = sine_table[:, None, :]
    score_scale = HD ** (-0.5)
    tokens_rel = ring.relative(tokens)
    grad_rel = ring.relative(out_grad)
    inputs = tokens_rel.astype(f32)
    inv_one = lax.rsqrt(jnp.mean(inputs * inputs, axis=-1, keepdims=True) + norm_eps)
    act_one = (inputs * inv_one * gains[0]).astype(low_type)
    qkv_raw = jnp.dot(act_one, qkv_full, preferred_element_type=f32)
    query_raw = qkv_raw[:, :qcols].reshape(row_count, local_heads, HD)
    query_rot = rotate(query_raw, cos_heads, sin_heads).astype(low_type)
    key_rot = rotate(qkv_raw[:, qcols : qcols + HD], cosine_table, sine_table).astype(low_type)
    value_low = qkv_raw[:, qcols + HD :].astype(low_type)
    block_size = min(512, row_count)
    starts = jnp.arange(row_count // block_size, dtype=jnp.int32) * block_size
    row_index = jnp.arange(row_count, dtype=jnp.int32)

    def scores_at(block_start):
        query_block = lax.dynamic_slice_in_dim(query_rot, block_start, block_size, 0)
        seg_block = lax.dynamic_slice_in_dim(segment_ids, block_start, block_size, 0)
        query_rows = block_start + jnp.arange(block_size, dtype=jnp.int32)
        allowed = (seg_block[:, None] == segment_ids[None, :]) & (
            query_rows[:, None] >= row_index[None, :]
        )
        raw_scores = (
            jnp.einsum("thd,sd->hts", query_block, key_rot, preferred_element_type=f32)
            * score_scale
        )
        return (query_block, allowed, raw_scores)

    def attend(block_start):
        query_block, allowed, raw_scores = scores_at(block_start)
        masked = jnp.where(allowed[None], raw_scores, -1e30)
        row_max = jnp.max(masked, axis=-1, keepdims=True)
        exp_scores = jnp.exp(masked - row_max)
        exp_total = jnp.sum(exp_scores, axis=-1, keepdims=True)
        weights_soft = (exp_scores / exp_total).astype(low_type)
        mixed_heads = jnp.einsum("hts,sd->thd", weights_soft, value_low, preferred_element_type=f32)
        return (mixed_heads, (row_max + jnp.log(exp_total))[..., 0])

    mixed_blocks, log_totals = lax.map(attend, starts)
    attn_low = mixed_blocks.reshape(row_count, local_heads * HD).astype(low_type)
    attn_part = jnp.dot(attn_low, output_full, preferred_element_type=f32)
    inputs_own = own_rows(inputs)
    hidden_own = inputs_own + rows_sum(attn_part)
    inv_two = lax.rsqrt(jnp.mean(hidden_own * hidden_own, axis=-1, keepdims=True) + norm_eps)
    act_two = rows_all((hidden_own * inv_two * gains[1]).astype(low_type))
    gate_pre = jnp.dot(act_two, gate_full, preferred_element_type=f32)
    up_proj = jnp.dot(act_two, up_full, preferred_element_type=f32)
    sigmoid_gate = jax.nn.sigmoid(gate_pre)
    swish_gate = gate_pre * sigmoid_gate
    inner_act = (swish_gate * up_proj).astype(low_type)

    down_grad = jnp.einsum("td,tf->df", grad_rel, inner_act, preferred_element_type=f32)
    down_fold = ring.fold_lo(down_grad.astype(low_type).reshape(groups_dp, block, ff))
    inner_grad = jnp.einsum("td,fd->tf", grad_rel, down_full, preferred_element_type=f32)
    gate_grad = inner_grad * up_proj * sigmoid_gate * (1.0 + gate_pre * (1.0 - sigmoid_gate))
    up_grad = (inner_grad * swish_gate).astype(low_type)
    gate_grad = gate_grad.astype(low_type)
    normed_two_part = jnp.einsum("tf,df->td", gate_grad, gate_full, preferred_element_type=f32)
    normed_two_part += jnp.einsum("tf,df->td", up_grad, up_full, preferred_element_type=f32)
    gate_wgrad = jnp.einsum("td,tf->df", act_two, gate_grad, preferred_element_type=f32)
    up_wgrad = jnp.einsum("td,tf->df", act_two, up_grad, preferred_element_type=f32)
    gate_fold = ring.fold_lo(gate_wgrad.astype(low_type).reshape(groups_dp, block, ff))
    up_fold = ring.fold_lo(up_wgrad.astype(low_type).reshape(groups_dp, block, ff))
    down_share = ring.fold_hi(down_fold)
    gate_share = ring.fold_hi(gate_fold)
    up_share = ring.fold_hi(up_fold)

    dn2 = rows_sum(normed_two_part)
    gain_two_grad = jnp.sum(dn2 * hidden_own * inv_two, axis=0)
    weighted = dn2 * gains[1]
    hidden_grad = (
        own_rows(grad_rel).astype(f32)
        + inv_two * weighted
        - hidden_own * inv_two**3 * jnp.mean(weighted * hidden_own, axis=-1, keepdims=True)
    )
    hidden_low = rows_all(hidden_grad.astype(low_type))
    output_grad = jnp.einsum("td,te->de", hidden_low, attn_low, preferred_element_type=f32)
    output_fold = ring.fold_lo(output_grad.astype(low_type).reshape(groups_dp, block, qcols))
    mixed_grad = (
        jnp.einsum("td,ed->te", hidden_low, output_full, preferred_element_type=f32)
        .astype(low_type)
        .reshape(row_count, local_heads, HD)
    )

    def attend_back(carried, scan_item):
        key_acc, value_acc = carried
        block_start, log_total = scan_item
        query_block, allowed, raw_scores = scores_at(block_start)
        weights_soft = jnp.where(allowed[None], jnp.exp(raw_scores - log_total[..., None]), 0.0)
        grad_block = lax.dynamic_slice_in_dim(mixed_grad, block_start, block_size, 0)
        prob_grad = jnp.einsum("thd,sd->hts", grad_block, value_low, preferred_element_type=f32)
        centre = jnp.sum(weights_soft * prob_grad, axis=-1, keepdims=True)
        score_low = (weights_soft * (prob_grad - centre)).astype(low_type)
        query_grad_block = (
            jnp.einsum("hts,sd->thd", score_low, key_rot, preferred_element_type=f32) * score_scale
        )
        key_acc = (
            key_acc
            + jnp.einsum("hts,thd->sd", score_low, query_block, preferred_element_type=f32)
            * score_scale
        )
        value_acc = value_acc + jnp.einsum(
            "hts,thd->sd", weights_soft.astype(low_type), grad_block, preferred_element_type=f32
        )
        return ((key_acc, value_acc), query_grad_block)

    zero_rows = jnp.zeros((row_count, HD), f32)
    (key_grad, value_grad), query_blocks = lax.scan(
        attend_back, (zero_rows, zero_rows), (starts, log_totals)
    )
    query_low = (
        unrotate(query_blocks.reshape(row_count, local_heads, HD), cos_heads, sin_heads)
        .astype(low_type)
        .reshape(row_count, local_heads * HD)
    )
    qkv_low = jnp.concatenate(
        [
            query_low,
            unrotate(key_grad, cosine_table, sine_table).astype(low_type),
            value_grad.astype(low_type),
        ],
        axis=1,
    )
    qkv_grad = jnp.einsum("td,te->de", act_one, qkv_low, preferred_element_type=f32)
    qkv_fold = ring.fold_lo(qkv_grad.astype(low_type).reshape(groups_dp, block, qcols + 2 * HD))
    normed_one_part = jnp.einsum("te,de->td", qkv_low, qkv_full, preferred_element_type=f32)
    output_share = ring.fold_hi(output_fold)
    qkv_share = ring.fold_hi(qkv_fold)

    ffn_part = jnp.dot(inner_act, down_full, preferred_element_type=f32)
    ffn_own = rows_sum(ffn_part)
    layer_out = ring.natural(rows_all((hidden_own + ffn_own).astype(low_type)))

    dn1 = rows_sum(normed_one_part)
    inv_own = own_rows(inv_one)
    gain_one_grad = jnp.sum(dn1 * inputs_own * inv_own, axis=0)
    weighted = dn1 * gains[0]
    input_own = (
        hidden_grad
        + inv_own * weighted
        - inputs_own * inv_own**3 * jnp.mean(weighted * inputs_own, axis=-1, keepdims=True)
    )
    input_grad = ring.natural(rows_all(input_own.astype(low_type))).astype(f32)

    gains_part = ring.natural(jnp.stack([gain_one_grad, gain_two_grad]))
    gains_sum = lax.psum(gains_part, ("dp", "mp"))
    gains_share = lax.dynamic_slice_in_dim(gains_sum, lax.axis_index("dp") * block, block, 1)
    query_share = qkv_share[:, :qcols]
    kv_mine = qkv_share[:, qcols:]
    kv_share = jnp.zeros((2, kv_rows, KV * HD), f32)
    for s in range(groups_mp):
        target = lax.rem(mp_me + s, groups_mp)
        piece = lax.dynamic_slice_in_dim(kv_mine, target * kv_rows, kv_rows, 0)
        if s:
            piece = lax.ppermute(piece, "mp", mp_perm(s))
        source = lax.rem(mp_me - s + groups_mp, groups_mp)
        start = head_of(source) * HD
        both = jnp.stack([piece[:, :HD], piece[:, HD:]])
        old = lax.dynamic_slice_in_dim(kv_share, start, HD, 2)
        kv_share = lax.dynamic_update_slice_in_dim(kv_share, old + both, start, 2)
    output_share = output_share.T
    down_share = down_share.T
    gateup_share = jnp.stack([gate_share, up_share])

    own_squares = (
        jnp.sum(query_share * query_share)
        + jnp.sum(kv_share * kv_share)
        + jnp.sum(output_share * output_share)
    )
    own_squares = (
        own_squares + jnp.sum(gateup_share * gateup_share) + jnp.sum(down_share * down_share)
    )
    gains_own = jnp.where(mp_me == 0, jnp.sum(gains_share * gains_share), 0.0)
    grad_norm = jnp.sqrt(lax.psum(own_squares + gains_own, ("dp", "mp")))
    factor = jnp.minimum(1.0, clip_limit / (grad_norm + 1e-06))
    output_rate = matrix_rate * (TOK_DEV * D / (16.0 * H * HD)) ** 0.5
    news = [
        adam_update(*args, factor, rate, decay)
        for args, rate, decay in (
            ((query_weight, query_moment, query_square, query_share), matrix_rate, weight_decay),
            ((keyval_weight, keyval_moment, keyval_square, kv_share), matrix_rate, weight_decay),
            ((output_weight, output_moment, output_square, output_share), output_rate, weight_decay),
            ((gateup_weight, gateup_moment, gateup_square, gateup_share), matrix_rate, weight_decay),
            ((down_weight, down_moment, down_square, down_share), matrix_rate, weight_decay),
            ((norm_gains, gains_moment, gains_square, gains_share), gain_rate, 0.0),
        )
    ]
    return (
        (layer_out, input_grad, grad_norm)
        + tuple(n[0] for n in news)
        + tuple(n[1] for n in news)
        + tuple(n[2] for n in news)
    )


def solution(mesh):
    params = (
        P("dp", "mp"),
        P(None, ("dp", "mp"), None),
        P("mp", "dp"),
        P(None, "dp", "mp"),
        P("mp", "dp"),
        P(None, "dp"),
    )
    rows = P("dp", None)
    return jax.shard_map(
        body,
        mesh=mesh,
        in_specs=(rows, P("dp"), rows) + params * 3,
        out_specs=(rows, rows, P()) + params * 3,
        check_vma=False,
    )
```

```python
import jax
import jax.numpy as jnp
from jax import lax
from jax.experimental import pallas as pl
from jax.experimental.pallas import tpu as pltpu
from jax.sharding import PartitionSpec as P

MESH_ID = pl.DeviceIdType.MESH
low_type = jnp.bfloat16
f32 = jnp.float32
HBM = pl.BlockSpec(memory_space=pl.ANY)
VM = pl.BlockSpec(memory_space=pltpu.VMEM)
DMA = pltpu.SemaphoreType.DMA
NT = (((1,), (1,)), ((), ()))
TN = (((0,), (0,)), ((), ()))


D = 2048
H = 16
KV = 4
HD = 128
TOK_DEV = 1024
ADAM_STEP = 10


norm_eps = 1e-05
rope_base = 10000.0
clip_limit = 1.0
beta_first = 0.9
beta_second = 0.95
adam_eps = 1e-08
weight_decay = 0.1
matrix_rate = 0.02
gain_rate = 0.6


def positions(segment):
    row_count = segment.shape[0]
    row_index = jnp.arange(row_count, dtype=jnp.int32)
    fresh_start = jnp.concatenate([jnp.ones((1,), dtype=jnp.bool_), segment[1:] != segment[:-1]])
    seg_start = lax.cummax(jnp.where(fresh_start, row_index, jnp.zeros_like(row_index)), axis=0)
    return row_index - seg_start


def rope_tables(segment, width):
    half_width = width // 2
    angle_rate = rope_base ** (-(jnp.arange(half_width, dtype=jnp.float32) * 2.0 / width))
    angles = positions(segment).astype(jnp.float32)[:, None] * angle_rate[None, :]
    return (jnp.cos(angles), jnp.sin(angles))


def adam_update(weight, moment, square, gradient, factor, step_rate, decay_rate):
    clipped = gradient * factor
    moment_new = beta_first * moment + (1.0 - beta_first) * clipped
    square_new = beta_second * square + (1.0 - beta_second) * clipped * clipped
    first_fix = 1.0 - beta_first**ADAM_STEP
    second_fix = 1.0 - beta_second**ADAM_STEP
    step_dir = moment_new / first_fix / (jnp.sqrt(square_new / second_fix) + adam_eps)
    return (weight - step_rate * (step_dir + decay_rate * weight), moment_new, square_new)


def split_dp(count):
    lo = 1
    while lo * lo * 4 <= count:
        lo *= 2
    return count // lo, lo


class Place:
    def __init__(self, dp, mp):
        self.dp, self.mp = dp, mp
        self.hi, self.lo = split_dp(dp)
        self.mlo = 2 if mp % 2 == 0 else 1
        self.mhi = mp // self.mlo
        me = lax.axis_index("dp")
        self.h, self.l = me // self.lo, lax.rem(me, self.lo)
        self.m = lax.axis_index("mp")
        self.y, self.c = self.m // self.mlo, lax.rem(self.m, self.mlo)

    def z(self, k):
        return {"dp": lax.rem(self.h + (k + self.hi) % self.hi, self.hi) * self.lo + self.l}

    def x(self, j):
        return {"dp": self.h * self.lo + lax.rem(self.l + (j + self.lo) % self.lo, self.lo)}

    def part(self, k, i):
        return lax.rem(self.y + k, self.mhi) * self.mlo + lax.rem(self.c + i, self.mlo)

    def barrier(self, dp=True, mp=True):
        peers = []
        if dp:
            peers += [self.z(k) for k in range(1, self.hi)]
            peers += [self.x(j) for j in range(1, self.lo)]
        if mp:
            peers += [{"mp": self.part(k, 0)} for k in range(1, self.mhi)]
            peers += [{"mp": self.part(0, i)} for i in range(1, self.mlo)]
        bar = pltpu.get_barrier_semaphore()
        for p in peers:
            pl.semaphore_signal(bar, inc=1, device_id=p, device_id_type=MESH_ID)
        pl.semaphore_wait(bar, len(peers))


def remote(src, dst, send, recv, to):
    return pltpu.make_async_remote_copy(src, dst, send, recv, to, MESH_ID)


class Gather:
    def __init__(self, shapes, axes, splits, dp):
        self.hi, self.lo = split_dp(dp)
        self.shapes, self.axes = shapes, axes
        self.chunks = []
        for i, s in enumerate(shapes):
            step = s[0] // splits[i]
            self.chunks += [(i, n * step, step) for n in range(splits[i])]
        self.count = len(self.chunks)

    def out_shapes(self):
        n = self.hi * self.lo
        return [
            jax.ShapeDtypeStruct((s[0] * n, s[1]) if a == 0 else (s[0], s[1] * n), low_type)
            for s, a in zip(self.shapes, self.axes)
        ]

    def scratch(self):
        c, hi, lo = self.count, self.hi, self.lo
        return [
            DMA((c, hi - 1)),
            DMA((c, hi - 1)),
            DMA((c, hi, max(lo - 1, 1))),
            DMA((c, hi, max(lo - 1, 1))),
            DMA((c,)),
        ]

    def bind(self, place, ins, outs, sems):
        zs, zr, xs, xr, ls = sems
        hi, lo = self.hi, self.lo

        def dst(c, r):
            i, at, step = self.chunks[c]
            rows, cols = self.shapes[i]
            if self.axes[i] == 0:
                return outs[i].at[pl.ds(r * rows + at, step), :]
            return outs[i].at[pl.ds(at, step), pl.ds(r * cols, cols)]

        def src(c):
            i, at, step = self.chunks[c]
            return ins[i].at[pl.ds(at, step), :]

        self.zc = {
            (c, k): remote(src(c), dst(c, k), zs.at[c, k - 1], zr.at[c, k - 1], place.z(k))
            for c in range(self.count)
            for k in range(1, hi)
        }
        self.xc = {
            (c, k, j): remote(
                src(c) if k == 0 else dst(c, k),
                dst(c, j * hi + k),
                xs.at[c, k, j - 1],
                xr.at[c, k, j - 1],
                place.x(j),
            )
            for c in range(self.count)
            for k in range(hi)
            for j in range(1, lo)
        }
        self.lc = [pltpu.make_async_copy(src(c), dst(c, 0), ls.at[c]) for c in range(self.count)]
        self.items = []
        self.started = 0
        self.window = 2
        for c in range(self.count):
            for k in range(1, hi):
                self.items.append((c, k))
        self.arrived = [False] * self.count

    def start_z(self, c):
        for k in range(1, self.hi):
            self.zc[c, k].start()

    def begin(self):
        for c in range(self.count):
            if c < self.window:
                self.start_z(c)
            for j in range(1, self.lo):
                self.xc[c, 0, j].start()
            self.lc[c].start()
        self.started = min(self.window, self.count)

    def step(self, n=1):
        for _ in range(n):
            if not self.items:
                return
            c, k = self.items.pop(0)
            self.zc[c, k].wait_recv()
            for j in range(1, self.lo):
                self.xc[c, k, j].start()
            if k == self.hi - 1 and self.started < self.count:
                self.start_z(self.started)
                self.started += 1

    def arrive(self, c):
        if self.arrived[c]:
            return
        while any(i[0] <= c for i in self.items):
            self.step()
        self.lc[c].wait()
        for k in range(self.hi):
            for j in range(1, self.lo):
                self.xc[c, k, j].wait_recv()
        self.arrived[c] = True

    def finish(self):
        for c in range(self.count):
            self.arrive(c)
        for c in range(self.count):
            for k in range(1, self.hi):
                self.zc[c, k].wait_send()
            for k in range(self.hi):
                for j in range(1, self.lo):
                    self.xc[c, k, j].wait_send()


class RowSum:
    def __init__(self, rows, width, mp, parts):
        self.mlo = 2 if mp % 2 == 0 else 1
        self.mhi = mp // self.mlo
        self.mp, self.parts = mp, parts
        self.share = rows // mp
        self.step = self.share // parts
        self.width = width
        self.tile = min(512, width)
        self.tiles = width // self.tile

    def scratch(self):
        h, p, t = self.mhi, self.parts, self.tiles
        g = max(h - 1, 1)
        return [
            pltpu.VMEM((h, self.share, self.width), low_type),
            pltpu.VMEM((h, self.share, self.width), low_type),
            pltpu.VMEM((g, self.share, self.width), low_type),
            pltpu.VMEM((g, self.share, self.width), low_type),
            pltpu.VMEM((self.share, self.width), f32),
            DMA((h, t)),
            DMA((h, t)),
            DMA((g, t)),
            DMA((g, t)),
            DMA((g, p)),
            DMA((g, p)),
            DMA((h, p)),
            DMA((h, p)),
        ]

    def bind(self, place, refs, full):
        self.place, self.full = place, full
        (self.cs, self.cr, self.ys, self.yr, self.acc) = refs[:5]
        css, crs, yss, yrs, gys, gyr, gcs, gcr = refs[5:]
        h, p, step = self.mhi, self.parts, self.step

        def sl(ref, k, t):
            return ref.at[k, :, pl.ds(t * self.tile, self.tile)]

        other = {"mp": place.part(0, 1)}
        self.cc = {
            (k, r): remote(sl(self.cs, k, r), sl(self.cr, k, r), css.at[k, r], crs.at[k, r], other)
            for k in range(h)
            for r in range(self.tiles)
        }
        self.yc = {
            (k, r): remote(
                sl(self.ys, k - 1, r),
                sl(self.yr, k - 1, r),
                yss.at[k - 1, r],
                yrs.at[k - 1, r],
                {"mp": place.part(k, 0)},
            )
            for k in range(1, h)
            for r in range(self.tiles)
        }

        def rows_at(m, r):
            return full.at[pl.ds(pl.multiple_of(m * self.share + r * step, 8), step), :]

        self.rows_at = rows_at
        self.gy = {
            (k, r): remote(
                rows_at(place.m, r),
                rows_at(place.m, r),
                gys.at[k - 1, r],
                gyr.at[k - 1, r],
                {"mp": place.part(k, 0)},
            )
            for k in range(1, h)
            for r in range(p)
        }
        self.gc = {
            (k, r): remote(
                rows_at(place.part((h - k) % h, 0), r),
                rows_at(place.part((h - k) % h, 0), r),
                gcs.at[k, r],
                gcr.at[k, r],
                other,
            )
            for k in range(h)
            for r in range(p)
        }

    def start_of(self, k, i):
        return pl.multiple_of(self.place.part(k, i) * self.share, 8)

    def scatter(self, partial, before=lambda t: None, between=lambda: None):
        order = list(range(1, self.mhi)) + [0]
        for t in range(self.tiles):
            before(t)
            cols = pl.ds(t * self.tile, self.tile)
            if self.mlo > 1:
                for k in order:
                    v = partial(self.start_of(k, 1), self.share, t, self.tile)
                    self.cs[k, :, cols] = v.astype(low_type)
                    self.cc[k, t].start()
            for k in order:
                v = partial(self.start_of(k, 0), self.share, t, self.tile)
                if self.mlo > 1:
                    self.cc[k, t].wait_recv()
                    v += self.cr[k, :, cols].astype(f32)
                if k:
                    self.ys[k - 1, :, cols] = v.astype(low_type)
                    self.yc[k, t].start()
                else:
                    self.acc[:, cols] = v
            between()

    def arrive(self):
        for t in range(self.tiles):
            for k in range(1, self.mhi):
                self.yc[k, t].wait_recv()

        def read(at, count):
            v = self.acc[pl.ds(at, count), :]
            for k in range(1, self.mhi):
                v += self.yr[k - 1, pl.ds(at, count), :].astype(f32)
            return v

        return read

    def spread(self, r):
        for k in range(1, self.mhi):
            self.gy[k, r].start()
        if self.mlo > 1:
            self.gc[0, r].start()

    def forward(self, r):
        for k in range(1, self.mhi):
            self.gy[k, r].wait_recv()
            if self.mlo > 1:
                self.gc[k, r].start()

    def finish(self):
        for t in range(self.tiles):
            if self.mlo > 1:
                for k in range(self.mhi):
                    self.cc[k, t].wait_send()
            for k in range(1, self.mhi):
                self.yc[k, t].wait_send()
        for r in range(self.parts):
            if self.mlo > 1:
                for k in range(self.mhi):
                    self.gc[k, r].wait()
            for k in range(1, self.mhi):
                self.gy[k, r].wait_send()


def small_rows(total, step, fn):
    @pl.loop(0, total // step)
    def _(t):
        fn(pl.multiple_of(t * step, step))


def gather_call(shards, axes, splits, dp, mp, cid):
    gather = Gather([s.shape for s in shards], axes, splits, dp)
    n = len(shards)

    def kernel(*refs):
        place = Place(dp, mp)
        place.barrier(mp=False)
        gather.bind(place, refs[:n], refs[n : 2 * n], refs[2 * n :])
        gather.begin()
        gather.finish()

    return pl.pallas_call(
        kernel,
        name="gather_dp",
        out_shape=gather.out_shapes(),
        in_specs=[HBM] * n,
        out_specs=[HBM] * n,
        scratch_shapes=gather.scratch(),
        compiler_params=pltpu.CompilerParams(collective_id=cid, has_side_effects=True),
    )(*shards)


def forward_call(attn, wo, x_own, gain, gate, up, down, dp, mp, cid, eps):
    rows, width = attn.shape[0], x_own.shape[1]
    ff = gate.shape[1]
    gather = Gather([gate.shape, up.shape, down.shape], (0, 0, 1), (2, 2, 4), dp)
    rsum = RowSum(rows, width, mp, 2)
    share = rsum.share
    n_g, n_r = len(gather.scratch()), len(rsum.scratch())
    tile = 128

    def kernel(attn_r, wo_r, x_r, gain_r, gate_r, up_r, down_r, *refs):
        wg_o, wu_o, wd_o, h_o, inv_o, act_o, hid_o, ht_o, ga_o, ub_o = refs[:10]
        wg_v, wu_v, wsem = refs[10:13]
        g_s = refs[13 : 13 + n_g]
        r_s = refs[13 + n_g :]
        place = Place(dp, mp)
        place.barrier()
        gather.bind(place, (gate_r, up_r, down_r), (wg_o, wu_o, wd_o), g_s)
        rsum.bind(place, r_s, act_o)
        gather.begin()

        def partial(start, count, t, n):
            return jnp.dot(
                attn_r[pl.ds(start, count), :],
                wo_r[:, pl.ds(t * n, n)],
                preferred_element_type=f32,
            )

        rsum.scatter(partial)
        gather.step(2)
        read = rsum.arrive()
        for r in range(rsum.parts):
            base = r * rsum.step
            own = place.m * share

            def norm(at):
                v = x_r[pl.ds(base + at, 32), :].astype(f32) + read(base + at, 32)
                h_o[pl.ds(base + at, 32), :] = v
                inv = lax.rsqrt(jnp.mean(v * v, axis=-1, keepdims=True) + eps)
                inv_o[pl.ds(base + at, 32), :] = jnp.broadcast_to(inv, (32, 128))
                act_o[pl.ds(pl.multiple_of(own + base + at, 32), 32), :] = (
                    v * inv * gain_r[...]
                ).astype(low_type)

            small_rows(rsum.step, 32, norm)
            rsum.spread(r)
            gather.step(1)
        for r in range(rsum.parts):
            rsum.forward(r)
            gather.step(1)
        rsum.finish()
        for c in range(2):
            gather.arrive(c)
        cg = pltpu.make_async_copy(wg_o, wg_v, wsem.at[0])
        cg.start()
        for c in range(2, 4):
            gather.arrive(c)
        cu = pltpu.make_async_copy(wu_o, wu_v, wsem.at[1])
        cu.start()
        cg.wait()
        cu.wait()
        groups = 4
        per = rows // tile // groups
        for q in range(groups):

            @pl.loop(q * per, (q + 1) * per)
            def _(t):
                rs = pl.ds(pl.multiple_of(t * tile, tile), tile)
                a = act_o[rs, :]
                gp = jnp.dot(a, wg_v[...], preferred_element_type=f32)
                upv = jnp.dot(a, wu_v[...], preferred_element_type=f32)
                sg = jax.nn.sigmoid(gp)
                sw = gp * sg
                hid = (sw * upv).astype(low_type)
                hid_o[rs, :] = hid
                ht_o[:, rs] = hid.T
                ga_o[rs, :] = (upv * sg * (1.0 + gp * (1.0 - sg))).astype(low_type)
                ub_o[rs, :] = sw.astype(low_type)

            gather.step(3)
        gather.finish()

    sds = jax.ShapeDtypeStruct
    act_shape = sds((rows, ff), low_type)
    return pl.pallas_call(
        kernel,
        name="forward_mlp",
        out_shape=gather.out_shapes()
        + [
            sds((share, width), f32),
            sds((share, 128), f32),
            sds((rows, width), low_type),
            act_shape,
            sds((ff, rows), low_type),
            act_shape,
            act_shape,
        ],
        in_specs=[VM] * 4 + [HBM] * 3,
        out_specs=[HBM] * 3 + [VM] * 7,
        scratch_shapes=[
            pltpu.VMEM((width, ff), low_type),
            pltpu.VMEM((width, ff), low_type),
            DMA((2,)),
        ]
        + gather.scratch()
        + rsum.scratch(),
        compiler_params=pltpu.CompilerParams(
            collective_id=cid, has_side_effects=True, vmem_limit_bytes=60 * 2**20
        ),
        cost_estimate=pl.CostEstimate(flops=2 * 10**10, bytes_accessed=10**8, transcendentals=10**6),
    )(attn, wo, x_own, gain, gate, up, down)


def fold_order(hi):
    return sorted(range(1, hi), key=lambda k: -min(k, hi - k)) + [0]


class Fold:
    def __init__(self, rows, cols, dp, sub):
        self.hi, self.lo = split_dp(dp)
        self.rows, self.cols, self.sub = rows, cols, sub
        self.step = rows // sub
        self.order = fold_order(self.hi)

    def scratch(self):
        hi, lo, s = self.hi, self.lo, self.sub
        j = max(lo - 1, 1)
        return [
            pltpu.VMEM((lo * hi, self.rows, self.cols), low_type),
            pltpu.VMEM((j * hi, self.rows, self.cols), low_type),
            pltpu.VMEM((hi - 1, self.rows, self.cols), low_type),
            DMA((j, hi, s)),
            DMA((j, hi, s)),
            DMA((hi - 1, s)),
            DMA((hi - 1, s)),
        ]

    def out_shapes(self):
        return [
            jax.ShapeDtypeStruct((self.rows, self.cols), f32),
            jax.ShapeDtypeStruct((8, self.cols), f32),
        ]

    def bind(self, place, refs):
        self.g, self.xb, self.zb, xs, xr, zs, zr = refs
        hi, lo = self.hi, self.lo

        def part(s):
            return pl.ds(s * self.step, self.step)

        self.part = part
        self.xc = {
            (k, j, s): remote(
                self.g.at[j * hi + k, part(s), :],
                self.xb.at[(j - 1) * hi + k, part(s), :],
                xs.at[j - 1, k, s],
                xr.at[j - 1, k, s],
                place.x(-j),
            )
            for k in range(hi)
            for j in range(1, lo)
            for s in range(self.sub)
        }
        self.zc = {
            (k, s): remote(
                self.g.at[k, part(s), :],
                self.zb.at[k - 1, part(s), :],
                zs.at[k - 1, s],
                zr.at[k - 1, s],
                place.z(-k),
            )
            for k in range(1, hi)
            for s in range(self.sub)
        }
        self.items = [(k, s) for k in self.order for s in range(self.sub)]
        self.blocks = [(j, k) for j in range(1, lo) for k in self.order]
        self.blocks += [(0, k) for k in self.order]
        self.small = next(n for n in (64, 32, 16, 8) if self.step % n == 0)

    def ready(self, j, k):
        if j:
            for s in range(self.sub):
                self.xc[k, j, s].start()

    def tiles(self, s, fn):
        @pl.loop(0, self.step // self.small)
        def _(t):
            fn(pl.ds(pl.multiple_of(s * self.step + t * self.small, self.small), self.small))

    def step_once(self):
        if not self.items:
            return
        k, s = self.items.pop(0)
        for j in range(1, self.lo):
            self.xc[k, j, s].wait_recv()
        if k:

            def add(rs):
                v = self.g[k, rs, :].astype(f32)
                for j in range(1, self.lo):
                    v += self.xb[(j - 1) * self.hi + k, rs, :].astype(f32)
                self.g[k, rs, :] = v.astype(low_type)

            self.tiles(s, add)
            self.zc[k, s].start()

    def finish(self, out, squares):
        while self.items:
            self.step_once()
        squares[...] = jnp.zeros_like(squares)
        for s in range(self.sub):
            for k in range(1, self.hi):
                self.zc[k, s].wait_recv()

            def add(rs):
                v = self.g[0, rs, :].astype(f32)
                for j in range(1, self.lo):
                    v += self.xb[(j - 1) * self.hi, rs, :].astype(f32)
                for k in range(1, self.hi):
                    v += self.zb[k - 1, rs, :].astype(f32)
                out[rs, :] = v
                squares[...] += jnp.sum((v * v).reshape(self.small // 8, 8, self.cols), axis=0)

            self.tiles(s, add)
        for c in self.xc.values():
            c.wait_send()
        for c in self.zc.values():
            c.wait_send()


def big(cid, remote_kernel=True):
    extra = {"collective_id": cid, "has_side_effects": True} if remote_kernel else {}
    return pltpu.CompilerParams(vmem_limit_bytes=61 * 2**20, **extra)


def cost(flops, bytes_accessed):
    return pl.CostEstimate(
        flops=int(flops), bytes_accessed=int(bytes_accessed), transcendentals=10**6
    )


def attention_call(x, wqkv, gain, cosine, sine, seg_rows, seg_cols, heads, eps):
    rows, width = x.shape
    hd = cosine.shape[1]
    qcols = heads * hd
    block = min(256, rows)
    scale = hd**-0.5

    def kernel(x_r, w_r, g_r, c_r, s_r, sr_r, sc_r, a_o, inv_o, q_o, k_o, v_o, ob_o, lse_o, bias):
        @pl.loop(0, rows // 128)
        def _(t):
            rs = pl.ds(pl.multiple_of(t * 128, 128), 128)
            v = x_r[rs, :].astype(f32)
            inv = lax.rsqrt(jnp.mean(v * v, axis=-1, keepdims=True) + eps)
            inv_o[rs, :] = jnp.broadcast_to(inv, (128, 128))
            a = (v * inv * g_r[...]).astype(low_type)
            a_o[rs, :] = a
            raw = jnp.dot(a, w_r[...], preferred_element_type=f32)
            cs, sn = c_r[rs, :], s_r[rs, :]
            for n in range(heads):
                u = raw[:, n * hd : (n + 1) * hd]
                q_o[rs, n * hd : (n + 1) * hd] = (u * cs + pltpu.roll(u, hd // 2, 1) * sn).astype(
                    low_type
                )
            u = raw[:, qcols : qcols + hd]
            k_o[rs, :] = (u * cs + pltpu.roll(u, hd // 2, 1) * sn).astype(low_type)
            v_o[rs, :] = raw[:, qcols + hd :].astype(low_type)

        @pl.loop(0, rows // block)
        def _(t):
            at = pl.multiple_of(t * block, block)
            rs = pl.ds(at, block)
            row = at + lax.broadcasted_iota(jnp.int32, (block, rows), 0)
            col = lax.broadcasted_iota(jnp.int32, (block, rows), 1)
            same = sr_r[rs, :1] == sc_r[:1, :]
            bias[...] = jnp.where(same & (row >= col), 0.0, -1e30)
            lane = lax.broadcasted_iota(jnp.int32, (block, 128), 1)
            lse = jnp.zeros((block, 128), f32)
            for n in range(heads):
                hs = slice(n * hd, (n + 1) * hd)
                s = lax.dot_general(q_o[rs, hs], k_o[...], NT, preferred_element_type=f32)
                s = s * scale + bias[...]
                top = jnp.max(s, axis=-1, keepdims=True)
                e = jnp.exp(s - top)
                total = jnp.sum(e, axis=-1, keepdims=True)
                p = (e * (1.0 / total)).astype(low_type)
                ob_o[rs, hs] = jnp.dot(p, v_o[...], preferred_element_type=f32).astype(low_type)
                lse = jnp.where(lane == n, top + jnp.log(total), lse)
            lse_o[rs, :] = lse

    sds = jax.ShapeDtypeStruct
    return pl.pallas_call(
        kernel,
        name="attention_forward",
        out_shape=[
            sds((rows, width), low_type),
            sds((rows, 128), f32),
            sds((rows, qcols), low_type),
            sds((rows, hd), low_type),
            sds((rows, hd), low_type),
            sds((rows, qcols), low_type),
            sds((rows, 128), f32),
        ],
        in_specs=[VM] * 7,
        out_specs=[VM] * 7,
        scratch_shapes=[pltpu.VMEM((block, rows), f32)],
        compiler_params=big(0, False),
        cost_estimate=cost(6e9, 2e7),
    )(x, wqkv, gain, cosine, sine, seg_rows, seg_cols)


def attention_back_call(dhb, wo, q, k, v, lse, cosine, sine, seg_rows, seg_cols, heads):
    rows, width = dhb.shape
    hd = cosine.shape[1]
    qcols = heads * hd
    block = min(256, rows)
    scale = hd**-0.5

    def kernel(d_r, w_r, q_r, k_r, v_r, l_r, c_r, s_r, sr_r, sc_r, out, bias, dk, dv):
        dk[...] = jnp.zeros_like(dk)
        dv[...] = jnp.zeros_like(dv)

        @pl.loop(0, rows // block)
        def _(t):
            at = pl.multiple_of(t * block, block)
            rs = pl.ds(at, block)
            row = at + lax.broadcasted_iota(jnp.int32, (block, rows), 0)
            col = lax.broadcasted_iota(jnp.int32, (block, rows), 1)
            same = sr_r[rs, :1] == sc_r[:1, :]
            bias[...] = jnp.where(same & (row >= col), 0.0, -1e30)
            do = lax.dot_general(d_r[rs, :], w_r[...], NT, preferred_element_type=f32).astype(
                low_type
            )
            cs, sn = c_r[rs, :], s_r[rs, :]
            for n in range(heads):
                hs = slice(n * hd, (n + 1) * hd)
                qb = q_r[rs, hs]
                s = lax.dot_general(qb, k_r[...], NT, preferred_element_type=f32)
                p = jnp.exp(s * scale + bias[...] - l_r[rs, n : n + 1])
                dp_ = lax.dot_general(do[:, hs], v_r[...], NT, preferred_element_type=f32)
                centre = jnp.sum(p * dp_, axis=-1, keepdims=True)
                ds = (p * (dp_ - centre)).astype(low_type)
                u = jnp.dot(ds, k_r[...], preferred_element_type=f32) * scale
                out[rs, hs] = (u * cs - pltpu.roll(u, hd // 2, 1) * sn).astype(low_type)
                dk[...] += lax.dot_general(ds, qb, TN, preferred_element_type=f32)
                dv[...] += lax.dot_general(
                    p.astype(low_type), do[:, hs], TN, preferred_element_type=f32
                )

        u = dk[...] * scale
        out[:, qcols : qcols + hd] = (
            u * c_r[...] - pltpu.roll(u, hd // 2, 1) * s_r[...]
        ).astype(low_type)
        out[:, qcols + hd :] = dv[...].astype(low_type)

    return pl.pallas_call(
        kernel,
        name="attention_backward",
        out_shape=jax.ShapeDtypeStruct((rows, qcols + 2 * hd), low_type),
        in_specs=[VM] * 10,
        out_specs=VM,
        scratch_shapes=[
            pltpu.VMEM((block, rows), f32),
            pltpu.VMEM((rows, hd), f32),
            pltpu.VMEM((rows, hd), f32),
        ],
        compiler_params=big(0, False),
        cost_estimate=cost(1e10, 2e7),
    )(dhb, wo, q, k, v, lse, cosine, sine, seg_rows, seg_cols)


def mlp_back_call(hid_t, og, ga, ub, wd, wg, wu, h_own, inv_own, gain, dp, mp, cid):
    ff, rows = hid_t.shape
    width = og.shape[1]
    blk = width // dp
    fold = Fold(ff, blk, dp, 2)
    rsum = RowSum(rows, width, mp, 2)
    share = rsum.share
    n_f = len(fold.scratch())

    def kernel(
        ht_r, og_r, ga_r, ub_r, wd_r, wg_r, wu_r, h_r, inv_r, g_r, *refs
    ):
        share_o, sq_o, dg_o, du_o, dh_o, dhb_o, gg_o = refs[:7]
        dg, du, wbuf, ls, ws, os = refs[7:13]
        f_s = refs[13 : 13 + n_f]
        r_s = refs[13 + n_f :]
        loads = [
            pltpu.make_async_copy(ga_r, dg, ls.at[0]),
            pltpu.make_async_copy(ub_r, du, ls.at[1]),
        ]
        for c in loads:
            c.start()
        tile = rsum.tile

        def fetch(t):
            rs = pl.ds(t * tile, tile)
            return [
                pltpu.make_async_copy(w.at[rs, :], wbuf.at[t % 2, i], ws.at[t, i])
                for i, w in enumerate((wg_r, wu_r))
            ]

        place = Place(dp, mp)
        place.barrier()
        fold.bind(place, f_s)
        rsum.bind(place, r_s, dhb_o)
        for c in fetch(0):
            c.start()
        for j, k in fold.blocks:
            r = j * fold.hi + k
            fold.g[r] = jnp.dot(
                ht_r[...], og_r[:, r * blk : (r + 1) * blk], preferred_element_type=f32
            ).astype(low_type)
            fold.ready(j, k)
        for c in loads:
            c.wait()
        groups = 4
        per = rows // 128 // groups
        for q in range(groups):

            @pl.loop(q * per, (q + 1) * per)
            def _(t):
                rs = pl.ds(pl.multiple_of(t * 128, 128), 128)
                d = lax.dot_general(og_r[rs, :], wd_r[...], NT, preferred_element_type=f32)
                dg[rs, :] = (d * dg[rs, :].astype(f32)).astype(low_type)
                du[rs, :] = (d * du[rs, :].astype(f32)).astype(low_type)

            if q > 0:
                fold.step_once()
        stores = [
            pltpu.make_async_copy(dg, dg_o, os.at[0]),
            pltpu.make_async_copy(du, du_o, os.at[1]),
        ]
        for c in stores:
            c.start()

        def before(t):
            for c in fetch(t):
                c.wait()
            if t + 1 < rsum.tiles:
                for c in fetch(t + 1):
                    c.start()

        def partial(start, count, t, n):
            rs = pl.ds(start, count)
            return lax.dot_general(
                dg[rs, :], wbuf[t % 2, 0], NT, preferred_element_type=f32
            ) + lax.dot_general(du[rs, :], wbuf[t % 2, 1], NT, preferred_element_type=f32)

        rsum.scatter(partial, before, fold.step_once)
        read = rsum.arrive()
        gg_o[...] = jnp.zeros_like(gg_o)
        own = place.m * share
        for r in range(rsum.parts):

            def norm(at):
                rs = pl.ds(at, 32)
                v, h = read(at, 32), h_r[rs, :]
                inv = inv_r[rs, :1]
                weighted = v * g_r[...]
                mean = jnp.mean(weighted * h, axis=-1, keepdims=True)
                orow = pl.ds(pl.multiple_of(own + at, 32), 32)
                dh = og_r[orow, :].astype(f32) + inv * weighted - h * (inv * inv * inv * mean)
                dh_o[rs, :] = dh
                dhb_o[orow, :] = dh.astype(low_type)
                gg_o[...] += jnp.sum((v * h * inv).reshape(4, 8, width), axis=0)

            @pl.loop(0, rsum.step // 32)
            def _(t):
                norm(pl.multiple_of(r * rsum.step + t * 32, 32))

            rsum.spread(r)
            fold.step_once()
        for r in range(rsum.parts):
            rsum.forward(r)
        fold.finish(share_o, sq_o)
        rsum.finish()
        for c in stores:
            c.wait()

    sds = jax.ShapeDtypeStruct
    act = sds((rows, ff), low_type)
    return pl.pallas_call(
        kernel,
        name="mlp_backward",
        out_shape=fold.out_shapes()
        + [act, act, sds((share, width), f32), sds((rows, width), low_type), sds((8, width), f32)],
        in_specs=[VM, VM, HBM, HBM, VM, HBM, HBM, VM, VM, VM],
        out_specs=[VM, VM, HBM, HBM, VM, VM, VM],
        scratch_shapes=[
            pltpu.VMEM((rows, ff), low_type),
            pltpu.VMEM((rows, ff), low_type),
            pltpu.VMEM((2, 2, rsum.tile, ff), low_type),
            DMA((2,)),
            DMA((rsum.tiles, 2)),
            DMA((2,)),
        ]
        + fold.scratch()
        + rsum.scratch(),
        compiler_params=big(cid),
        cost_estimate=cost(3e10, 1e8),
    )(hid_t, og, ga, ub, wd, wg, wu, h_own, inv_own, gain)


def put_natural(place, ref, rows, value, blk):
    for j in range(place.lo):
        for k in range(place.hi):
            owner = lax.rem(place.h - k + place.hi, place.hi) * place.lo + lax.rem(
                place.l - j + place.lo, place.lo
            )
            r = j * place.hi + k
            ref[rows, pl.ds(pl.multiple_of(owner * blk, 128), blk)] = value[
                :, r * blk : (r + 1) * blk
            ]


def gateup_back_call(act, dg, du, hid, wd, h_own, dp, mp, cid):
    rows, width = act.shape
    ff = dg.shape[1]
    blk = width // dp
    folds = [Fold(blk, ff, dp, 2), Fold(blk, ff, dp, 2)]
    rsum = RowSum(rows, width, mp, 2)
    share = rsum.share
    n_f = len(folds[0].scratch())

    def kernel(a_r, dg_r, du_r, hid_r, wd_r, h_r, *refs):
        outs, sqs, y_o = refs[0:4:2], refs[1:4:2], refs[4]
        f_s = [refs[5 : 5 + n_f], refs[5 + n_f : 5 + 2 * n_f]]
        r_s = refs[5 + 2 * n_f :]
        place = Place(dp, mp)
        place.barrier()
        for f, s in zip(folds, f_s):
            f.bind(place, s)
        rsum.bind(place, r_s, y_o)
        for j, k in folds[0].blocks:
            r = j * folds[0].hi + k
            at = a_r[:, r * blk : (r + 1) * blk].T
            for f, d in zip(folds, (dg_r, du_r)):
                f.g[r] = jnp.dot(at, d[...], preferred_element_type=f32).astype(low_type)
                f.ready(j, k)

        def both():
            for f in folds:
                f.step_once()

        def partial(start, count, t, n):
            return jnp.dot(
                hid_r[pl.ds(start, count), :],
                wd_r[:, pl.ds(t * n, n)],
                preferred_element_type=f32,
            )

        both()
        rsum.scatter(partial, lambda t: None, both)
        read = rsum.arrive()
        own = place.m * share
        for r in range(rsum.parts):

            @pl.loop(0, rsum.step // 32)
            def _(t):
                at = pl.multiple_of(r * rsum.step + t * 32, 32)
                v = (h_r[pl.ds(at, 32), :] + read(at, 32)).astype(low_type)
                put_natural(place, y_o, pl.ds(pl.multiple_of(own + at, 32), 32), v, blk)

            rsum.spread(r)
            both()
        for r in range(rsum.parts):
            rsum.forward(r)
            both()
        for f, o, s in zip(folds, outs, sqs):
            f.finish(o, s)
        rsum.finish()

    return pl.pallas_call(
        kernel,
        name="gateup_backward",
        out_shape=folds[0].out_shapes()
        + folds[1].out_shapes()
        + [jax.ShapeDtypeStruct((rows, width), low_type)],
        in_specs=[VM] * 6,
        out_specs=[VM] * 5,
        scratch_shapes=folds[0].scratch() + folds[1].scratch() + rsum.scratch(),
        compiler_params=big(cid),
        cost_estimate=cost(2e10, 1e8),
    )(act, dg, du, hid, wd, h_own)


def inputs_back_call(dhb, ob, a1, dqkv, wqkv, x_own, inv_own, dh_own, gain, dp, mp, cid):
    rows, width = dhb.shape
    qcols, cols = ob.shape[1], dqkv.shape[1]
    blk = width // dp
    folds = [Fold(blk, cols, dp, 2), Fold(qcols, blk, dp, 2)]
    rsum = RowSum(rows, width, mp, 2)
    share = rsum.share
    n_f = len(folds[0].scratch())

    def kernel(dhb_r, ob_r, a_r, d_r, w_r, x_r, inv_r, dh_r, g_r, *refs):
        outs, sqs, in_o, gg_o = refs[0:4:2], refs[1:4:2], refs[4], refs[5]
        obt = refs[6]
        f_s = [refs[7 : 7 + n_f], refs[7 + n_f : 7 + 2 * n_f]]
        r_s = refs[7 + 2 * n_f :]
        place = Place(dp, mp)
        place.barrier()
        for f, s in zip(folds, f_s):
            f.bind(place, s)
        rsum.bind(place, r_s, in_o)

        def partial(start, count, t, n):
            return lax.dot_general(
                d_r[pl.ds(start, count), :],
                w_r[pl.ds(t * n, n), :],
                NT,
                preferred_element_type=f32,
            )

        rsum.scatter(partial)
        for n in range(qcols // 128):
            obt[n * 128 : (n + 1) * 128, :] = ob_r[:, n * 128 : (n + 1) * 128].T
        for j, k in folds[0].blocks:
            r = j * folds[0].hi + k
            bs = slice(r * blk, (r + 1) * blk)
            folds[0].g[r] = jnp.dot(
                a_r[:, bs].T, d_r[...], preferred_element_type=f32
            ).astype(low_type)
            folds[0].ready(j, k)
            folds[1].g[r] = jnp.dot(obt[...], dhb_r[:, bs], preferred_element_type=f32).astype(
                low_type
            )
            folds[1].ready(j, k)

        def both():
            for f in folds:
                f.step_once()

        both()
        both()
        read = rsum.arrive()
        gg_o[...] = jnp.zeros_like(gg_o)
        own = place.m * share
        for r in range(rsum.parts):

            @pl.loop(0, rsum.step // 32)
            def _(t):
                at = pl.multiple_of(r * rsum.step + t * 32, 32)
                rs = pl.ds(at, 32)
                v, x = read(at, 32), x_r[rs, :].astype(f32)
                inv = inv_r[rs, :1]
                weighted = v * g_r[...]
                mean = jnp.mean(weighted * x, axis=-1, keepdims=True)
                d = dh_r[rs, :] + inv * weighted - x * (inv * inv * inv * mean)
                put_natural(
                    place,
                    in_o,
                    pl.ds(pl.multiple_of(own + at, 32), 32),
                    d.astype(low_type),
                    blk,
                )
                gg_o[...] += jnp.sum((v * x * inv).reshape(4, 8, width), axis=0)

            rsum.spread(r)
            both()
        for r in range(rsum.parts):
            rsum.forward(r)
            both()
        for f, o, s in zip(folds, outs, sqs):
            f.finish(o, s)
        rsum.finish()

    sds = jax.ShapeDtypeStruct
    return pl.pallas_call(
        kernel,
        name="inputs_backward",
        out_shape=folds[0].out_shapes()
        + folds[1].out_shapes()
        + [sds((rows, width), low_type), sds((8, width), f32)],
        in_specs=[VM] * 9,
        out_specs=[VM] * 6,
        scratch_shapes=[pltpu.VMEM((qcols, rows), low_type)]
        + folds[0].scratch()
        + folds[1].scratch()
        + rsum.scratch(),
        compiler_params=big(cid),
        cost_estimate=cost(1e10, 5e7),
    )(dhb, ob, a1, dqkv, wqkv, x_own, inv_own, dh_own, gain)


def whole(v):
    return jnp.sum(jnp.sum(v, axis=0, keepdims=True), axis=1, keepdims=True)


def totals_call(gain_parts, kv, squares, dp, mp, kv_heads, cid):
    width = gain_parts.shape[2]
    blk = width // dp
    rows, cols = kv.shape[0] // mp, kv.shape[1]
    n_sq = len(squares)
    local = [m * kv_heads // mp for m in range(mp)]

    def kernel(gp_r, kv_r, *refs):
        sq_r = refs[:n_sq]
        gain_o, kv_o, tot_o = refs[n_sq : n_sq + 3]
        (mine, got, sent2, got2, t1, t2, sems) = refs[n_sq + 3 :]
        place = Place(dp, mp)
        me_dp, me_mp = lax.axis_index("dp"), place.m

        def mp_at(s):
            return lax.rem(me_mp + s, mp)

        def dp_peers():
            out = []
            for j in range(place.lo):
                for k in range(place.hi):
                    if j or k:
                        out.append((j * place.hi + k, j, k))
            return out

        def owner(j, k):
            return lax.rem(place.h + place.hi - k, place.hi) * place.lo + lax.rem(
                place.l + place.lo - j, place.lo
            )

        bar = pltpu.get_barrier_semaphore()
        for s in range(1, mp):
            pl.semaphore_signal(bar, inc=1, device_id={"mp": mp_at(s)}, device_id_type=MESH_ID)
        for r, j, k in dp_peers():
            pl.semaphore_signal(bar, inc=1, device_id={"dp": owner(j, k)}, device_id_type=MESH_ID)
        mine[...] = jnp.zeros_like(mine)
        for i in range(2):
            mine[i : i + 1, :] = jnp.sum(gp_r[i], axis=0, keepdims=True)
        pl.semaphore_wait(bar, mp - 1 + dp - 1)
        waits = []
        for s in range(1, mp):
            to = {"mp": mp_at(s)}
            a = remote(mine, got.at[me_mp], sems.at[0, s], sems.at[1, s], to)
            b = remote(
                kv_r.at[pl.ds(pl.multiple_of(mp_at(s) * rows, 8), rows), :],
                kv_o.at[me_mp],
                sems.at[2, s],
                sems.at[3, s],
                to,
            )
            a.start()
            b.start()
            waits.append((a, b))
        kv_o[me_mp] = kv_r[pl.ds(pl.multiple_of(me_mp * rows, 8), rows), :]
        got[me_mp] = mine[...]
        total = jnp.zeros((1, 1), f32)
        for q in sq_r:
            total += whole(q[...])
        for a, b in waits:
            a.wait()
        v = got[0]
        for s in range(1, mp):
            v += got[s]
        for r in range(dp):
            sent2[r] = v[:, r * blk : (r + 1) * blk]
        waits2 = []
        for r, j, k in dp_peers():
            c = remote(
                sent2.at[r], got2.at[r], sems.at[4, r], sems.at[5, r], {"dp": owner(j, k)}
            )
            c.start()
            waits2.append(c)
        for a, b in waits:
            b.wait()
        for c in range(kv_heads):
            own = [m for m in range(mp) if local[m] == c]
            v = kv_o[own[0]]
            for m in own[1:]:
                v += kv_o[m]
            total += whole(v * v)
        got2[0] = sent2[0]
        for c in waits2:
            c.wait()
        v = got2[0]
        for r in range(1, dp):
            v += got2[r]
        gain_o[...] = v
        total += jnp.where(me_mp == 0, whole(v * v), jnp.zeros((1, 1), f32))
        t1[me_mp] = jnp.broadcast_to(total, (8, 128))
        waits = []
        for s in range(1, mp):
            c = remote(
                t1.at[me_mp], t1.at[me_mp], sems.at[6, s], sems.at[7, s], {"mp": mp_at(s)}
            )
            c.start()
            waits.append(c)
        for c in waits:
            c.wait()
        v = t1[0]
        for s in range(1, mp):
            v += t1[s]
        t2[me_dp] = v
        waits = []
        for r, j, k in dp_peers():
            c = remote(
                t2.at[me_dp], t2.at[me_dp], sems.at[8, r], sems.at[9, r], {"dp": owner(j, k)}
            )
            c.start()
            waits.append(c)
        for c in waits:
            c.wait()
        v = t2[0]
        for s in range(1, dp):
            v += t2[s]
        tot_o[...] = v

    sds = jax.ShapeDtypeStruct
    top = max(dp, mp)
    return pl.pallas_call(
        kernel,
        name="totals",
        out_shape=[sds((8, blk), f32), sds((mp, rows, cols), f32), sds((8, 128), f32)],
        in_specs=[VM] * (2 + n_sq),
        out_specs=[VM] * 3,
        scratch_shapes=[
            pltpu.VMEM((8, width), f32),
            pltpu.VMEM((mp, 8, width), f32),
            pltpu.VMEM((dp, 8, blk), f32),
            pltpu.VMEM((dp, 8, blk), f32),
            pltpu.VMEM((mp, 8, 128), f32),
            pltpu.VMEM((dp, 8, 128), f32),
            DMA((10, top)),
        ],
        compiler_params=pltpu.CompilerParams(collective_id=cid, has_side_effects=True),
        cost_estimate=cost(1e6, 1e6),
    )(gain_parts, kv, *squares)


def relative_columns(x, dp):
    hi, lo = split_dp(dp)
    me = lax.axis_index("dp")
    h, l = me // lo, me % lo
    width = x.shape[-1] // dp
    blocks = []
    for j in range(lo):
        for k in range(hi):
            o = lax.rem(h - k + hi, hi) * lo + lax.rem(l - j + lo, lo)
            blocks.append(lax.dynamic_slice_in_dim(x, o * width, width, x.ndim - 1))
    return jnp.concatenate(blocks, -1)


def body(
    tokens,
    segment_ids,
    out_grad,
    query_weight,
    keyval_weight,
    output_weight,
    gateup_weight,
    down_weight,
    norm_gains,
    query_moment,
    keyval_moment,
    output_moment,
    gateup_moment,
    down_moment,
    gains_moment,
    query_square,
    keyval_square,
    output_square,
    gateup_square,
    down_square,
    gains_square,
):
    dp = lax.axis_size("dp")
    mp = lax.axis_size("mp")
    heads = H // mp
    rows = tokens.shape[0]
    share = rows // mp
    mp_me = lax.axis_index("mp")
    blk = D // dp
    kv_rows = blk // mp
    qcols = query_weight.shape[1]

    def head_of(m):
        return m * heads // (H // KV)

    kv_low = keyval_weight.astype(low_type)
    kv_block = jnp.zeros((2, blk, HD), low_type)
    for s in range(mp):
        target = lax.rem(mp_me + s, mp)
        piece = lax.dynamic_slice_in_dim(kv_low, head_of(target) * HD, HD, 2)
        if s:
            piece = lax.ppermute(piece, "mp", [(m, (m + s) % mp) for m in range(mp)])
        source = lax.rem(mp_me - s + mp, mp)
        kv_block = lax.dynamic_update_slice_in_dim(kv_block, piece, source * kv_rows, 1)
    gain_rows = jnp.pad(norm_gains.astype(low_type), ((0, 14), (0, qcols + 2 * HD - blk)))
    first_shard = jnp.concatenate(
        [
            jnp.concatenate([query_weight.astype(low_type), kv_block[0], kv_block[1]], axis=1),
            gain_rows,
        ],
        axis=0,
    )
    first, wo = gather_call(
        [first_shard, output_weight.astype(low_type)], (0, 1), (2, 2), dp, mp, 0
    )
    first = first.reshape(dp, blk + 16, qcols + 2 * HD)
    wqkv = first[:, :blk].reshape(D, qcols + 2 * HD)
    gains = jnp.moveaxis(first[:, blk : blk + 2, :blk], 0, 1).reshape(2, 1, D).astype(f32)

    cos_half, sin_half = rope_tables(segment_ids, HD)
    cosine = jnp.concatenate([cos_half, cos_half], axis=-1)
    sine = jnp.concatenate([-sin_half, sin_half], axis=-1)
    seg_rows = jnp.broadcast_to(segment_ids[:, None], (rows, 128))
    seg_cols = jnp.broadcast_to(segment_ids[None, :], (8, rows))
    x = relative_columns(tokens, dp)
    og = relative_columns(out_grad, dp)
    act_one, inv_one, q, k, v, attn, lse = attention_call(
        x, wqkv, gains[0], cosine, sine, seg_rows, seg_cols, heads, norm_eps
    )

    def own_rows(a):
        return lax.dynamic_slice_in_dim(a, mp_me * share, share, 0)

    x_own = own_rows(x)
    gate_low, up_low = gateup_weight[0].astype(low_type), gateup_weight[1].astype(low_type)
    wg, wu, wd, h_own, inv_two, act_two, hid, hid_t, ga, ub = forward_call(
        attn, wo, x_own, gains[1], gate_low, up_low, down_weight.astype(low_type), dp, mp, 1, norm_eps
    )
    down_share, down_sq, dg, du, dh_own, dhb, gain_two = mlp_back_call(
        hid_t, og, ga, ub, wd, wg, wu, h_own, inv_two, gains[1], dp, mp, 2
    )
    dqkv = attention_back_call(
        dhb, wo, q, k, v, lse, cosine, sine, seg_rows, seg_cols, heads
    )
    gate_share, gate_sq, up_share, up_sq, layer_out = gateup_back_call(
        act_two, dg, du, hid, wd, h_own, dp, mp, 3
    )
    qkv_share, qkv_sq, output_share, output_sq, in_low, gain_one = inputs_back_call(
        dhb, attn, act_one, dqkv, wqkv, x_own, own_rows(inv_one), dh_own, gains[0], dp, mp, 4
    )
    input_grad = in_low.astype(f32)
    gain_rows8, kv_parts, total = totals_call(
        jnp.stack([gain_one, gain_two]),
        qkv_share[:, qcols:],
        [down_sq, gate_sq, up_sq, output_sq, qkv_sq[:, :qcols]],
        dp,
        mp,
        KV,
        5,
    )
    gains_share = gain_rows8[:2]
    query_share = qkv_share[:, :qcols]
    kv_heads = []
    for c in range(KV):
        parts = [kv_parts[m] for m in range(mp) if head_of(m) == c]
        one = parts[0]
        for p in parts[1:]:
            one = one + p
        kv_heads.append(jnp.stack([one[:, :HD], one[:, HD:]]))
    kv_share = jnp.concatenate(kv_heads, axis=-1)
    gateup_share = jnp.stack([gate_share, up_share])

    grad_norm = jnp.sqrt(total[0, 0])
    factor = jnp.minimum(1.0, clip_limit / (grad_norm + 1e-06))
    output_rate = matrix_rate * (TOK_DEV * D / (16.0 * H * HD)) ** 0.5
    news = [
        adam_update(*args, factor, rate, decay)
        for args, rate, decay in (
            ((query_weight, query_moment, query_square, query_share), matrix_rate, weight_decay),
            ((keyval_weight, keyval_moment, keyval_square, kv_share), matrix_rate, weight_decay),
            ((output_weight, output_moment, output_square, output_share), output_rate, weight_decay),
            ((gateup_weight, gateup_moment, gateup_square, gateup_share), matrix_rate, weight_decay),
            ((down_weight, down_moment, down_square, down_share), matrix_rate, weight_decay),
            ((norm_gains, gains_moment, gains_square, gains_share), gain_rate, 0.0),
        )
    ]
    return (
        (layer_out, input_grad, grad_norm)
        + tuple(n[0] for n in news)
        + tuple(n[1] for n in news)
        + tuple(n[2] for n in news)
    )


def solution(mesh):
    params = (
        P("dp", "mp"),
        P(None, ("dp", "mp"), None),
        P("mp", "dp"),
        P(None, "dp", "mp"),
        P("mp", "dp"),
        P(None, "dp"),
    )
    rows = P("dp", None)
    return jax.shard_map(
        body,
        mesh=mesh,
        in_specs=(rows, P("dp"), rows) + params * 3,
        out_specs=(rows, rows, P()) + params * 3,
        check_vma=False,
    )
```

```python
import jax
import jax.numpy as jnp
import numpy as np
from jax import lax
from jax.experimental import pallas as pl
from jax.experimental.pallas import tpu as pltpu
from jax.sharding import PartitionSpec as P

MESH_ID = pl.DeviceIdType.MESH
low_type = jnp.bfloat16
f32 = jnp.float32
HBM = pl.BlockSpec(memory_space=pl.ANY)
VM = pl.BlockSpec(memory_space=pltpu.VMEM)
DMA = pltpu.SemaphoreType.DMA
NT = (((1,), (1,)), ((), ()))
TN = (((0,), (0,)), ((), ()))


D = 2048
H = 16
KV = 4
HD = 128
TOK_DEV = 1024
ADAM_STEP = 10


norm_eps = 1e-05
rope_base = 10000.0
clip_limit = 1.0
beta_first = 0.9
beta_second = 0.95
adam_eps = 1e-08
weight_decay = 0.1
matrix_rate = 0.02
gain_rate = 0.6


def adam_update(weight, moment, square, gradient, factor, step_rate, decay_rate):
    clipped = gradient * factor
    moment_new = beta_first * moment + (1.0 - beta_first) * clipped
    square_new = beta_second * square + (1.0 - beta_second) * clipped * clipped
    first_fix = 1.0 - beta_first**ADAM_STEP
    second_fix = 1.0 - beta_second**ADAM_STEP
    step_dir = moment_new / first_fix / (jnp.sqrt(square_new / second_fix) + adam_eps)
    return (weight - step_rate * (step_dir + decay_rate * weight), moment_new, square_new)


def split_dp(count):
    lo = 1
    while lo * lo * 4 <= count:
        lo *= 2
    return count // lo, lo


class Place:
    def __init__(self, dp, mp):
        self.dp, self.mp = dp, mp
        self.hi, self.lo = split_dp(dp)
        self.mlo = 2 if mp % 2 == 0 else 1
        self.mhi = mp // self.mlo
        me = lax.axis_index("dp")
        self.h, self.l = me // self.lo, lax.rem(me, self.lo)
        self.m = lax.axis_index("mp")
        self.y, self.c = self.m // self.mlo, lax.rem(self.m, self.mlo)

    def z(self, k):
        return {"dp": lax.rem(self.h + (k + self.hi) % self.hi, self.hi) * self.lo + self.l}

    def x(self, j):
        return {"dp": self.h * self.lo + lax.rem(self.l + (j + self.lo) % self.lo, self.lo)}

    def part(self, k, i):
        return lax.rem(self.y + k, self.mhi) * self.mlo + lax.rem(self.c + i, self.mlo)

    def others_dp(self):
        out = []
        for j in range(self.lo):
            for k in range(self.hi):
                if j or k:
                    out.append((j * self.hi + k, self.owner(j, k)))
        return out

    def owner(self, j, k):
        return lax.rem(self.h + self.hi - k, self.hi) * self.lo + lax.rem(
            self.l + self.lo - j, self.lo
        )

    def others_mp(self):
        return [(s, lax.rem(self.m + s, self.mp)) for s in range(1, self.mp)]

    def barrier(self):
        bar = pltpu.get_barrier_semaphore()
        peers = [{"dp": d} for _, d in self.others_dp()] + [{"mp": m} for _, m in self.others_mp()]
        for p in peers:
            pl.semaphore_signal(bar, inc=1, device_id=p, device_id_type=MESH_ID)
        pl.semaphore_wait(bar, len(peers))


def remote(src, dst, send, recv, to):
    return pltpu.make_async_remote_copy(src, dst, send, recv, to, MESH_ID)


class Gather:
    def __init__(self, shapes, axes, splits, dp, late=()):
        self.hi, self.lo = split_dp(dp)
        self.shapes, self.axes, self.late = shapes, axes, late
        self.chunks = []
        for i, s in enumerate(shapes):
            step = s[0] // splits[i]
            self.chunks += [(i, n * step, step) for n in range(splits[i])]
        self.count = len(self.chunks)

    def out_shapes(self):
        n = self.hi * self.lo
        return [
            jax.ShapeDtypeStruct((s[0] * n, s[1]) if a == 0 else (s[0], s[1] * n), low_type)
            for s, a in zip(self.shapes, self.axes)
        ]

    def scratch(self):
        c, hi, lo = self.count, self.hi, self.lo
        return [
            DMA((c, hi - 1)),
            DMA((c, hi - 1)),
            DMA((c, hi, max(lo - 1, 1))),
            DMA((c, hi, max(lo - 1, 1))),
            DMA((c,)),
        ]

    def bind(self, place, ins, outs, sems):
        zs, zr, xs, xr, ls = sems
        hi, lo = self.hi, self.lo

        def dst(c, r):
            i, at, step = self.chunks[c]
            rows, cols = self.shapes[i]
            if self.axes[i] == 0:
                return outs[i].at[pl.ds(r * rows + at, step)]
            return outs[i].at[pl.ds(at, step), pl.ds(r * cols, cols)]

        def src(c):
            i, at, step = self.chunks[c]
            return ins[i].at[pl.ds(at, step)]

        self.zc = {
            (c, k): remote(src(c), dst(c, k), zs.at[c, k - 1], zr.at[c, k - 1], place.z(k))
            for c in range(self.count)
            for k in range(1, hi)
        }
        self.xc = {
            (c, k, j): remote(
                src(c) if k == 0 else dst(c, k),
                dst(c, j * hi + k),
                xs.at[c, k, j - 1],
                xr.at[c, k, j - 1],
                place.x(j),
            )
            for c in range(self.count)
            for k in range(hi)
            for j in range(1, lo)
        }
        self.lc = [pltpu.make_async_copy(src(c), dst(c, 0), ls.at[c]) for c in range(self.count)]
        self.items = []
        self.started = 0
        self.window = 2
        for c in range(self.count):
            for k in range(1, hi):
                self.items.append((c, k))
        self.arrived = [False] * self.count

    def start_own(self, c):
        for j in range(1, self.lo):
            self.xc[c, 0, j].start()
        self.lc[c].start()

    def start_z(self, c):
        if c in self.late:
            self.late[c]()
            self.start_own(c)
        for k in range(1, self.hi):
            self.zc[c, k].start()

    def begin(self):
        for c in range(self.count):
            if c < self.window:
                self.start_z(c)
            if c not in self.late:
                self.start_own(c)
        self.started = min(self.window, self.count)

    def step(self, n=1):
        for _ in range(n):
            if not self.items:
                return
            c, k = self.items.pop(0)
            self.zc[c, k].wait_recv()
            for j in range(1, self.lo):
                self.xc[c, k, j].start()
            if k == self.hi - 1 and self.started < self.count:
                self.start_z(self.started)
                self.started += 1

    def arrive(self, c):
        if self.arrived[c]:
            return
        while any(i[0] <= c for i in self.items):
            self.step()
        self.lc[c].wait()
        for k in range(self.hi):
            for j in range(1, self.lo):
                self.xc[c, k, j].wait_recv()
        self.arrived[c] = True

    def finish(self):
        for c in range(self.count):
            self.arrive(c)
        for c in range(self.count):
            for k in range(1, self.hi):
                self.zc[c, k].wait_send()
            for k in range(self.hi):
                for j in range(1, self.lo):
                    self.xc[c, k, j].wait_send()


class RowSum:
    def __init__(self, rows, width, mp):
        self.mlo = 2 if mp % 2 == 0 else 1
        self.mhi = mp // self.mlo
        self.share, self.width = rows // mp, width
        self.tile = min(512, width)
        self.tiles = width // self.tile

    def scratch(self):
        h, t = self.mhi, self.tiles
        g = max(h - 1, 1)
        return [
            pltpu.VMEM((h, self.share, self.width), low_type),
            pltpu.VMEM((h, self.share, self.width), low_type),
            pltpu.VMEM((g, self.share, self.width), low_type),
            pltpu.VMEM((g, self.share, self.width), low_type),
            pltpu.VMEM((self.share, self.width), f32),
            DMA((h, t)),
            DMA((h, t)),
            DMA((g, t)),
            DMA((g, t)),
        ]

    def bind(self, place, refs):
        self.place = place
        (self.cs, self.cr, self.ys, self.yr, self.acc) = refs[:5]
        css, crs, yss, yrs = refs[5:]
        h = self.mhi

        def sl(ref, k, t):
            return ref.at[k, :, pl.ds(t * self.tile, self.tile)]

        other = {"mp": place.part(0, 1)}
        self.cc = {
            (k, t): remote(sl(self.cs, k, t), sl(self.cr, k, t), css.at[k, t], crs.at[k, t], other)
            for k in range(h)
            for t in range(self.tiles)
        }
        self.yc = {
            (k, t): remote(
                sl(self.ys, k - 1, t),
                sl(self.yr, k - 1, t),
                yss.at[k - 1, t],
                yrs.at[k - 1, t],
                {"mp": place.part(k, 0)},
            )
            for k in range(1, h)
            for t in range(self.tiles)
        }

    def start_of(self, k, i):
        return pl.multiple_of(self.place.part(k, i) * self.share, 8)

    def scatter(self, partial, before=lambda t: None, between=lambda: None):
        order = list(range(1, self.mhi)) + [0]
        for t in range(self.tiles):
            before(t)
            cols = pl.ds(t * self.tile, self.tile)
            if self.mlo > 1:
                for k in order:
                    v = partial(self.start_of(k, 1), self.share, t, self.tile)
                    self.cs[k, :, cols] = v.astype(low_type)
                    self.cc[k, t].start()
            for k in order:
                v = partial(self.start_of(k, 0), self.share, t, self.tile)
                if self.mlo > 1:
                    self.cc[k, t].wait_recv()
                    v += self.cr[k, :, cols].astype(f32)
                if k:
                    self.ys[k - 1, :, cols] = v.astype(low_type)
                    self.yc[k, t].start()
                else:
                    self.acc[:, cols] = v
            between()

    def arrive(self):
        for t in range(self.tiles):
            for k in range(1, self.mhi):
                self.yc[k, t].wait_recv()

        def read(at, count):
            v = self.acc[pl.ds(at, count), :]
            for k in range(1, self.mhi):
                v += self.yr[k - 1, pl.ds(at, count), :].astype(f32)
            return v

        return read

    def finish(self):
        for t in range(self.tiles):
            if self.mlo > 1:
                for k in range(self.mhi):
                    self.cc[k, t].wait_send()
            for k in range(1, self.mhi):
                self.yc[k, t].wait_send()


class Spread:
    def __init__(self, rows, mp, parts):
        self.mlo = 2 if mp % 2 == 0 else 1
        self.mhi = mp // self.mlo
        self.share, self.parts = rows // mp, parts
        self.step = self.share // parts

    def scratch(self):
        h, p = self.mhi, self.parts
        g = max(h - 1, 1)
        return [DMA((g, p)), DMA((g, p)), DMA((h, p)), DMA((h, p))]

    def bind(self, place, refs, full, own=None):
        gys, gyr, gcs, gcr = refs
        h, p = self.mhi, self.parts
        other = {"mp": place.part(0, 1)}

        def rows_at(m, r):
            return full.at[pl.ds(pl.multiple_of(m * self.share + r * self.step, 8), self.step), :]

        def mine(r):
            if own is None:
                return rows_at(place.m, r)
            return own.at[pl.ds(r * self.step, self.step), :]

        self.gy = {
            (k, r): remote(
                mine(r),
                rows_at(place.m, r),
                gys.at[k - 1, r],
                gyr.at[k - 1, r],
                {"mp": place.part(k, 0)},
            )
            for k in range(1, h)
            for r in range(p)
        }
        self.gc = {
            (k, r): remote(
                rows_at(place.part((h - k) % h, 0), r) if k else mine(r),
                rows_at(place.part((h - k) % h, 0), r),
                gcs.at[k, r],
                gcr.at[k, r],
                other,
            )
            for k in range(h)
            for r in range(p)
        }

    def send(self, r):
        for k in range(1, self.mhi):
            self.gy[k, r].start()
        if self.mlo > 1:
            self.gc[0, r].start()

    def forward(self, r):
        for k in range(1, self.mhi):
            self.gy[k, r].wait_recv()
            if self.mlo > 1:
                self.gc[k, r].start()

    def finish(self):
        for r in range(self.parts):
            if self.mlo > 1:
                for k in range(self.mhi):
                    self.gc[k, r].wait()
            for k in range(1, self.mhi):
                self.gy[k, r].wait_send()


def sequence_length(seg, rows):
    top = jnp.max(jnp.max(seg, axis=1, keepdims=True), axis=0, keepdims=True)
    return jnp.where(top == 0, rows, jnp.where(top == 1, rows // 2, rows // 4))


def attention_bias(length, start, count, keys):
    row = start + lax.broadcasted_iota(jnp.int32, (count, 1), 0)
    first = row - (row & (length - 1))
    col = lax.broadcasted_iota(jnp.int32, (count, keys), 1)
    return jnp.where((col <= row) & (col >= first), 0.0, -1e30)


def small_rows(total, step, fn):
    @pl.loop(0, total // step)
    def _(t):
        fn(pl.multiple_of(t * step, step))


def forward_call(attn, wo, x_own, gain, gate, up, down, dp, mp, cid, eps):
    rows, width = attn.shape[0], x_own.shape[1]
    ff = gate.shape[1]
    gather = Gather([gate.shape, up.shape, down.shape], (0, 0, 0), (2, 2, 4), dp)
    rsum, spread = RowSum(rows, width, mp), Spread(rows, mp, 2)
    share = rsum.share
    n_g, n_r = len(gather.scratch()), len(rsum.scratch())
    tile = 128

    def kernel(attn_r, wo_r, x_r, gain_r, gate_r, up_r, down_r, *refs):
        wg_o, wu_o, wd_o, h_o, inv_o, act_o, hid_o, ga_o, ub_o = refs[:9]
        wg_v, wu_v, wsem = refs[9:12]
        g_s = refs[12 : 12 + n_g]
        r_s = refs[12 + n_g : 12 + n_g + n_r]
        place = Place(dp, mp)
        place.barrier()
        gather.bind(place, (gate_r, up_r, down_r), (wg_o, wu_o, wd_o), g_s)
        rsum.bind(place, r_s)
        spread.bind(place, refs[12 + n_g + n_r :], act_o)
        gather.begin()

        def partial(start, count, t, n):
            return jnp.dot(
                attn_r[pl.ds(start, count), :],
                wo_r[:, pl.ds(t * n, n)],
                preferred_element_type=f32,
            )

        rsum.scatter(partial)
        gather.step(2)
        read = rsum.arrive()
        for r in range(spread.parts):
            base = r * spread.step
            own = place.m * share

            def norm(at):
                v = x_r[pl.ds(base + at, 32), :].astype(f32) + read(base + at, 32)
                h_o[pl.ds(base + at, 32), :] = v
                inv = lax.rsqrt(jnp.mean(v * v, axis=-1, keepdims=True) + eps)
                inv_o[pl.ds(base + at, 32), :] = jnp.broadcast_to(inv, (32, 128))
                act_o[pl.ds(pl.multiple_of(own + base + at, 32), 32), :] = (
                    v * inv * gain_r[...]
                ).astype(low_type)

            small_rows(spread.step, 32, norm)
            spread.send(r)
            gather.step(1)
        for r in range(spread.parts):
            spread.forward(r)
            gather.step(1)
        spread.finish()
        rsum.finish()
        for c in range(2):
            gather.arrive(c)
        cg = pltpu.make_async_copy(wg_o, wg_v, wsem.at[0])
        cg.start()
        for c in range(2, 4):
            gather.arrive(c)
        cu = pltpu.make_async_copy(wu_o, wu_v, wsem.at[1])
        cu.start()
        cg.wait()
        cu.wait()
        groups = 4
        per = rows // tile // groups
        for q in range(groups):

            @pl.loop(q * per, (q + 1) * per)
            def _(t):
                rs = pl.ds(pl.multiple_of(t * tile, tile), tile)
                a = act_o[rs, :]
                gp = jnp.dot(a, wg_v[...], preferred_element_type=f32)
                upv = jnp.dot(a, wu_v[...], preferred_element_type=f32)
                sg = jax.nn.sigmoid(gp)
                sw = gp * sg
                hid_o[rs, :] = (sw * upv).astype(low_type)
                ga_o[rs, :] = (upv * sg * (1.0 + gp * (1.0 - sg))).astype(low_type)
                ub_o[rs, :] = sw.astype(low_type)

            gather.step(3)
        gather.finish()

    sds = jax.ShapeDtypeStruct
    act_shape = sds((rows, ff), low_type)
    return pl.pallas_call(
        kernel,
        name="forward_mlp",
        out_shape=gather.out_shapes()
        + [
            sds((share, width), f32),
            sds((share, 128), f32),
            sds((rows, width), low_type),
            act_shape,
            act_shape,
            act_shape,
        ],
        in_specs=[VM] * 4 + [HBM] * 3,
        out_specs=[HBM] * 3 + [VM] * 6,
        scratch_shapes=[
            pltpu.VMEM((width, ff), low_type),
            pltpu.VMEM((width, ff), low_type),
            DMA((2,)),
        ]
        + gather.scratch()
        + rsum.scratch()
        + spread.scratch(),
        compiler_params=big(cid),
        cost_estimate=cost(2e10, 1e8),
    )(attn, wo, x_own, gain, gate, up, down)


def fold_order(hi):
    return sorted(range(1, hi), key=lambda k: -min(k, hi - k)) + [0]


class Fold:
    def __init__(self, rows, cols, dp, sub):
        self.hi, self.lo = split_dp(dp)
        self.rows, self.cols, self.sub = rows, cols, sub
        self.step = rows // sub
        self.order = fold_order(self.hi)

    def scratch(self):
        hi, lo, s = self.hi, self.lo, self.sub
        j = max(lo - 1, 1)
        return [
            pltpu.VMEM((lo * hi, self.rows, self.cols), low_type),
            pltpu.VMEM((j * hi, self.rows, self.cols), low_type),
            pltpu.VMEM((hi - 1, self.rows, self.cols), low_type),
            DMA((j, hi, s)),
            DMA((j, hi, s)),
            DMA((hi - 1, s)),
            DMA((hi - 1, s)),
        ]

    def out_shapes(self):
        return [
            jax.ShapeDtypeStruct((self.rows, self.cols), f32),
            jax.ShapeDtypeStruct((8, self.cols), f32),
        ]

    def bind(self, place, refs):
        self.g, self.xb, self.zb, xs, xr, zs, zr = refs
        hi, lo = self.hi, self.lo

        def part(s):
            return pl.ds(s * self.step, self.step)

        self.part = part
        self.xc = {
            (k, j, s): remote(
                self.g.at[j * hi + k, part(s), :],
                self.xb.at[(j - 1) * hi + k, part(s), :],
                xs.at[j - 1, k, s],
                xr.at[j - 1, k, s],
                place.x(-j),
            )
            for k in range(hi)
            for j in range(1, lo)
            for s in range(self.sub)
        }
        self.zc = {
            (k, s): remote(
                self.g.at[k, part(s), :],
                self.zb.at[k - 1, part(s), :],
                zs.at[k - 1, s],
                zr.at[k - 1, s],
                place.z(-k),
            )
            for k in range(1, hi)
            for s in range(self.sub)
        }
        self.items = [(k, s) for k in self.order for s in range(self.sub)]
        self.blocks = [(j, k) for j in range(1, lo) for k in self.order]
        self.blocks += [(0, k) for k in self.order]
        self.small = next(n for n in (64, 32, 16, 8) if self.step % n == 0)

    def ready(self, j, k):
        if j:
            for s in range(self.sub):
                self.xc[k, j, s].start()

    def tiles(self, s, fn):
        @pl.loop(0, self.step // self.small)
        def _(t):
            fn(pl.ds(pl.multiple_of(s * self.step + t * self.small, self.small), self.small))

    def step_once(self):
        if not self.items:
            return
        k, s = self.items.pop(0)
        for j in range(1, self.lo):
            self.xc[k, j, s].wait_recv()
        if k:

            def add(rs):
                v = self.g[k, rs, :].astype(f32)
                for j in range(1, self.lo):
                    v += self.xb[(j - 1) * self.hi + k, rs, :].astype(f32)
                self.g[k, rs, :] = v.astype(low_type)

            self.tiles(s, add)
            self.zc[k, s].start()

    def finish(self, out, squares):
        while self.items:
            self.step_once()
        squares[...] = jnp.zeros_like(squares)
        for s in range(self.sub):
            for k in range(1, self.hi):
                self.zc[k, s].wait_recv()

            def add(rs):
                v = self.g[0, rs, :].astype(f32)
                for j in range(1, self.lo):
                    v += self.xb[(j - 1) * self.hi, rs, :].astype(f32)
                for k in range(1, self.hi):
                    v += self.zb[k - 1, rs, :].astype(f32)
                out[rs, :] = v
                squares[...] += jnp.sum((v * v).reshape(self.small // 8, 8, self.cols), axis=0)

            self.tiles(s, add)
        for c in self.xc.values():
            c.wait_send()
        for c in self.zc.values():
            c.wait_send()


def big(cid, remote_kernel=True):
    extra = {"collective_id": cid, "has_side_effects": True} if remote_kernel else {}
    return pltpu.CompilerParams(vmem_limit_bytes=61 * 2**20, **extra)


def cost(flops, bytes_accessed):
    return pl.CostEstimate(
        flops=int(flops), bytes_accessed=int(bytes_accessed), transcendentals=10**6
    )


def attention_call(
    tokens, out_grad, wq, wkv, wo, gains, gateup, down, segment, rates,
    heads, kv_heads, dp, mp, cid, eps
):
    rows, width = tokens.shape
    hd = rates.shape[1]
    blk, qcols = wq.shape
    kv_rows = wkv.shape[1]
    ff = down.shape[0]
    block = min(256, rows)
    scale = hd**-0.5
    share = rows // mp
    cols = qcols + 2 * hd
    late = {}
    gather = Gather(
        [(16, blk), wq.shape, (blk, 2 * hd), wo.shape], (0, 0, 0, 1), (1, 2, 1, 2), dp, late
    )
    n_g = len(gather.scratch())

    def kernel(tok_r, og_r, q_f, kv_f, wo_f, gn_f, gu_r, dn_r, sg_r, rt_r, *refs):
        (wqkv_o, wo_o, gain_o, og_o, x_o, a_o, inv_o, qo, ko, vo, ob_o, lse_o, gl_o, ul_o, dl_o) = (
            refs[:15]
        )
        c_r, s_r = refs[15:17]
        kvx, gall, xv, wv, bias, q_r, kv_r, wo_r, gn_r, ks, kr, cs_, ws = refs[17:30]
        g_s = refs[30:]
        place = Place(dp, mp)
        copies = []
        for j in range(place.lo):
            for k in range(place.hi):
                r = j * place.hi + k
                at = pl.ds(pl.multiple_of(place.owner(j, k) * blk, 128), blk)
                to = pl.ds(r * blk, blk)
                copies.append(pltpu.make_async_copy(tok_r.at[:, at], xv.at[:, to], cs_.at[0, r]))
                copies.append(
                    pltpu.make_async_copy(og_r.at[:, at], og_o.at[:, to], cs_.at[1, r])
                )
        for c in copies:
            c.start()
        gn_r[...] = jnp.zeros_like(gn_r)
        gn_r[:2, :] = gn_f[...].astype(low_type)
        q_r[...] = q_f[...].astype(low_type)
        for n in range(kv_heads):
            for i in range(2):
                kv_r[:, (2 * n + i) * hd : (2 * n + i + 1) * hd] = kv_f[
                    i, :, n * hd : (n + 1) * hd
                ].astype(low_type)
        wo_r[...] = wo_f[...].astype(low_type)
        place.barrier()
        here = pl.ds(pl.multiple_of(place.m * kv_rows, kv_rows), kv_rows)
        swaps = []
        for n, m in place.others_mp():
            head = m * kv_heads // mp
            c = remote(
                kv_r.at[:, pl.ds(pl.multiple_of(head * 2 * hd, 128), 2 * hd)],
                kvx.at[here],
                ks.at[n],
                kr.at[n],
                {"mp": m},
            )
            c.start()
            swaps.append(c)
        head = place.m * kv_heads // mp
        mine = pltpu.make_async_copy(
            kv_r.at[:, pl.ds(pl.multiple_of(head * 2 * hd, 128), 2 * hd)], kvx.at[here], ks.at[0]
        )
        mine.start()

        def swapped():
            mine.wait()
            for c in swaps:
                c.wait_recv()

        late[3] = swapped
        gather.bind(
            place,
            (gn_r, q_r, kvx, wo_r),
            (gall, wqkv_o.at[:, pl.ds(0, qcols)], wqkv_o.at[:, pl.ds(qcols, 2 * hd)], wo_o),
            g_s,
        )
        gather.begin()

        @pl.loop(0, blk // 32)
        def _(t):
            rs = pl.ds(pl.multiple_of(t * 32, 32), 32)
            gl_o[rs, :] = gu_r[0, rs, :].astype(low_type)
            ul_o[rs, :] = gu_r[1, rs, :].astype(low_type)

        dl_o[...] = dn_r[...].T.astype(low_type)
        gather.step(2 * (gather.hi - 1))
        length = sequence_length(sg_r[...], rows)

        @pl.loop(0, rows // 128)
        def _(t):
            at = pl.multiple_of(t * 128, 128)
            row = at + lax.broadcasted_iota(jnp.int32, (128, 1), 0)
            angle = (row & (length - 1)).astype(f32) * rt_r[...]
            lane = lax.broadcasted_iota(jnp.int32, (128, hd), 1)
            c_r[pl.ds(at, 128), :] = jnp.cos(angle)
            sn = jnp.sin(angle)
            s_r[pl.ds(at, 128), :] = jnp.where(lane < hd // 2, -sn, sn)

        for c in copies:
            c.wait()
        own = place.m * share

        @pl.loop(0, share // 32)
        def _(t):
            at = pl.multiple_of(t * 32, 32)
            v = xv[pl.ds(pl.multiple_of(own + at, 32), 32), :]
            x_o[pl.ds(at, 32), :] = v
            v = v.astype(f32)
            inv = lax.rsqrt(jnp.mean(v * v, axis=-1, keepdims=True) + eps)
            inv_o[pl.ds(at, 32), :] = jnp.broadcast_to(inv, (32, 128))

        gather.arrive(0)
        for c in (1, 2, 3):
            gather.arrive(c)
        wcopy = pltpu.make_async_copy(wqkv_o, wv, ws.at[0])
        wcopy.start()
        for r in range(dp):
            at = r * 16
            gain_o[:, r * blk : (r + 1) * blk] = gall[at : at + 8, :].astype(f32)
        wcopy.wait()
        gain = gain_o[:1, :]
        half = rows // 128 // 2
        for q in range(2):

            @pl.loop(q * half, (q + 1) * half)
            def _(t):
                rs = pl.ds(pl.multiple_of(t * 128, 128), 128)
                v = xv[rs, :].astype(f32)
                inv = lax.rsqrt(jnp.mean(v * v, axis=-1, keepdims=True) + eps)
                a = (v * inv * gain).astype(low_type)
                a_o[rs, :] = a
                raw = jnp.dot(a, wv[...], preferred_element_type=f32)
                cs, sn = c_r[rs, :], s_r[rs, :]
                for n in range(heads):
                    u = raw[:, n * hd : (n + 1) * hd]
                    qo[rs, n * hd : (n + 1) * hd] = (
                        u * cs + pltpu.roll(u, hd // 2, 1) * sn
                    ).astype(low_type)
                u = raw[:, qcols : qcols + hd]
                ko[rs, :] = (u * cs + pltpu.roll(u, hd // 2, 1) * sn).astype(low_type)
                vo[rs, :] = raw[:, qcols + hd :].astype(low_type)

            gather.step(1)

        for q in range(rows // block):
            rs = pl.ds(q * block, block)
            keys = (q + 1) * block
            bias[:, :keys] = attention_bias(length, q * block, block, keys)
            lane = lax.broadcasted_iota(jnp.int32, (block, 128), 1)
            lse = jnp.zeros((block, 128), f32)
            for n in range(heads):
                hs = slice(n * hd, (n + 1) * hd)
                s = lax.dot_general(qo[rs, hs], ko[:keys, :], NT, preferred_element_type=f32)
                s = s * scale + bias[:, :keys]
                top = jnp.max(s, axis=-1, keepdims=True)
                e = jnp.exp(s - top)
                total = jnp.sum(e, axis=-1, keepdims=True)
                p = (e * (1.0 / total)).astype(low_type)
                ob_o[rs, hs] = jnp.dot(p, vo[:keys, :], preferred_element_type=f32).astype(
                    low_type
                )
                lse = jnp.where(lane == n, top + jnp.log(total), lse)
            lse_o[rs, :] = lse
            gather.step(1)
        gather.finish()
        for c in swaps:
            c.wait_send()

    sds = jax.ShapeDtypeStruct
    return pl.pallas_call(
        kernel,
        name="attention_forward",
        out_shape=[
            sds((width, cols), low_type),
            sds((qcols, width), low_type),
            sds((8, width), f32),
            sds((rows, width), low_type),
            sds((share, width), low_type),
            sds((rows, width), low_type),
            sds((share, 128), f32),
            sds((rows, qcols), low_type),
            sds((rows, hd), low_type),
            sds((rows, hd), low_type),
            sds((rows, qcols), low_type),
            sds((rows, 128), f32),
            sds((blk, ff), low_type),
            sds((blk, ff), low_type),
            sds((blk, ff), low_type),
            sds((rows, hd), f32),
            sds((rows, hd), f32),
        ],
        in_specs=[HBM] * 2 + [VM] * 8,
        out_specs=[HBM, HBM] + [VM] * 15,
        scratch_shapes=[
            pltpu.VMEM((blk, 2 * hd), low_type),
            pltpu.VMEM((16 * dp, blk), low_type),
            pltpu.VMEM((rows, width), low_type),
            pltpu.VMEM((width, cols), low_type),
            pltpu.VMEM((block, rows), f32),
            pltpu.VMEM((blk, qcols), low_type),
            pltpu.VMEM((kv_rows, kv_heads * 2 * hd), low_type),
            pltpu.VMEM(wo.shape, low_type),
            pltpu.VMEM((16, blk), low_type),
            DMA((mp,)),
            DMA((mp,)),
            DMA((2, dp)),
            DMA((1,)),
        ]
        + gather.scratch(),
        compiler_params=big(cid),
        cost_estimate=cost(6e9, 2e7),
    )(tokens, out_grad, wq, wkv, wo, gains, gateup, down, segment, rates)


def put_natural(place, ref, rows, value, blk):
    for j in range(place.lo):
        for k in range(place.hi):
            owner = place.owner(j, k)
            r = j * place.hi + k
            ref[rows, pl.ds(pl.multiple_of(owner * blk, 128), blk)] = value[
                :, r * blk : (r + 1) * blk
            ]


def mlp_back_call(hid, og, act, ga, ub, wd, wg, wu, h_own, inv_own, gain, dp, mp, cid):
    rows, ff = hid.shape
    width = og.shape[1]
    blk = width // dp
    folds = [Fold(blk, ff, dp, 2), Fold(blk, ff, dp, 2)]
    rsum, spread = RowSum(rows, width, mp), Spread(rows, mp, 2)
    share, tile = rsum.share, rsum.tile
    n_f, n_r = len(folds[0].scratch()), len(rsum.scratch())

    def kernel(
        hid_r, og_r, act_r, ga_r, ub_r, wd_r, wg_r, wu_r, h_r, inv_r, g_r, *refs
    ):
        (down_o, dsq_o, gate_o, gsq_o, du_o, dh_o, dhb_o, gg_o) = refs[:8]
        pb, ogx, dg, du, wbuf, ls, ws, wd_s = refs[8:16]
        at = 16
        for f in folds:
            f_refs = refs[at : at + n_f]
            at += n_f
            f.refs = f_refs
        r_s = refs[at : at + n_r]
        p_s = refs[at + n_r :]
        place = Place(dp, mp)
        own = pl.multiple_of(place.m * share, 8)
        load_og = pltpu.make_async_copy(og_r, pb, ls.at[0])
        load_hid = pltpu.make_async_copy(hid_r, dg, ls.at[1])
        load_ub = pltpu.make_async_copy(ub_r, du, ls.at[2])
        load_own = pltpu.make_async_copy(og_r.at[pl.ds(own, share), :], ogx, ls.at[3])
        load_ga = pltpu.make_async_copy(ga_r, dg, ls.at[4])
        load_act = pltpu.make_async_copy(act_r, pb, ls.at[5])
        store_du = pltpu.make_async_copy(du, du_o, ls.at[6])
        tiles = rsum.tiles
        load_wd = [
            pltpu.make_async_copy(
                wd_r.at[pl.ds(t * tile, tile), :], wbuf.at[t // 2, t % 2], wd_s.at[t]
            )
            for t in range(tiles)
        ]

        def fetch(t):
            rs = pl.ds(t * tile, tile)
            return [
                pltpu.make_async_copy(w.at[rs, :], wbuf.at[t % 2, i], ws.at[t, i])
                for i, w in enumerate((wg_r, wu_r))
            ]

        for c in [load_og, load_hid, load_ub, load_own] + load_wd:
            c.start()
        place.barrier()
        for f in folds:
            f.bind(place, f.refs)
        rsum.bind(place, r_s)
        spread.bind(place, p_s, dhb_o)
        load_og.wait()
        load_hid.wait()
        first, second = folds
        for j, k in first.blocks:
            r = j * first.hi + k
            first.g[r] = jnp.dot(
                pb[:, r * blk : (r + 1) * blk].T, dg[...], preferred_element_type=f32
            ).astype(low_type)
            first.ready(j, k)
        load_ga.start()
        for c in load_wd + [load_ub, load_ga]:
            c.wait()
        groups = 4
        per = rows // 128 // groups
        for q in range(groups):

            @pl.loop(q * per, (q + 1) * per)
            def _(n):
                rs = pl.ds(pl.multiple_of(n * 128, 128), 128)
                d = jnp.dot(pb[rs, :tile], wbuf[0, 0], preferred_element_type=f32)
                for t in range(1, tiles):
                    d += jnp.dot(
                        pb[rs, t * tile : (t + 1) * tile],
                        wbuf[t // 2, t % 2],
                        preferred_element_type=f32,
                    )
                dg[rs, :] = (d * dg[rs, :].astype(f32)).astype(low_type)
                du[rs, :] = (d * du[rs, :].astype(f32)).astype(low_type)

            if q > 0:
                first.step_once()
        store_du.start()
        load_act.start()
        for c in fetch(0):
            c.start()

        def before(t):
            for c in fetch(t):
                c.wait()
            if t + 1 < tiles:
                for c in fetch(t + 1):
                    c.start()

        def partial(start, count, t, n):
            rs = pl.ds(start, count)
            return lax.dot_general(
                dg[rs, :], wbuf[t % 2, 0], NT, preferred_element_type=f32
            ) + lax.dot_general(du[rs, :], wbuf[t % 2, 1], NT, preferred_element_type=f32)

        rsum.scatter(partial, before, first.step_once)
        load_act.wait()
        for n, (j, k) in enumerate(second.blocks):
            r = j * second.hi + k
            second.g[r] = jnp.dot(
                pb[:, r * blk : (r + 1) * blk].T, dg[...], preferred_element_type=f32
            ).astype(low_type)
            second.ready(j, k)
        load_own.wait()
        read = rsum.arrive()
        gg_o[...] = jnp.zeros_like(gg_o)
        for r in range(spread.parts):

            @pl.loop(0, spread.step // 32)
            def _(t):
                at = pl.multiple_of(r * spread.step + t * 32, 32)
                rs = pl.ds(at, 32)
                v, h = read(at, 32), h_r[rs, :]
                inv = inv_r[rs, :1]
                weighted = v * g_r[...]
                mean = jnp.mean(weighted * h, axis=-1, keepdims=True)
                dh = ogx[rs, :].astype(f32) + inv * weighted - h * (inv * inv * inv * mean)
                dh_o[rs, :] = dh
                dhb_o[pl.ds(pl.multiple_of(own + at, 32), 32), :] = dh.astype(low_type)
                gg_o[...] += jnp.sum((v * h * inv).reshape(4, 8, width), axis=0)

            spread.send(r)
            first.step_once()
        for r in range(spread.parts):
            spread.forward(r)
            second.step_once()
        first.finish(gate_o, dsq_o)
        down_o[...] = gate_o[...].T
        second.finish(gate_o, gsq_o)
        spread.finish()
        rsum.finish()
        store_du.wait()

    sds = jax.ShapeDtypeStruct
    square = sds((8, ff), f32)
    return pl.pallas_call(
        kernel,
        name="mlp_backward",
        out_shape=[
            sds((ff, blk), f32),
            square,
            sds((blk, ff), f32),
            square,
            sds((rows, ff), low_type),
            sds((share, width), f32),
            sds((rows, width), low_type),
            sds((8, width), f32),
        ],
        in_specs=[HBM] * 8 + [VM] * 3,
        out_specs=[VM] * 4 + [HBM] + [VM] * 3,
        scratch_shapes=[
            pltpu.VMEM((rows, width), low_type),
            pltpu.VMEM((share, width), low_type),
            pltpu.VMEM((rows, ff), low_type),
            pltpu.VMEM((rows, ff), low_type),
            pltpu.VMEM((2, 2, tile, ff), low_type),
            DMA((7,)),
            DMA((rsum.tiles, 2)),
            DMA((rsum.tiles,)),
        ]
        + folds[0].scratch()
        + folds[1].scratch()
        + rsum.scratch()
        + spread.scratch(),
        compiler_params=big(cid),
        cost_estimate=cost(4e10, 1e8),
    )(hid, og, act, ga, ub, wd, wg, wu, h_own, inv_own, gain)


def attention_back_call(
    act, du, hid, wd, h_own, dhb, wo, q, k, v, lse, cosine, sine, segment,
    wqkv, x_own, inv_own, dh_own, gain, heads, dp, mp, cid
):
    rows, width = act.shape
    ff = du.shape[1]
    hd = cosine.shape[1]
    qcols = heads * hd
    blk = width // dp
    block = min(256, rows)
    scale = hd**-0.5
    fold = Fold(blk, ff, dp, 2)
    sums = [RowSum(rows, width, mp), RowSum(rows, width, mp)]
    share, tile, tiles = sums[0].share, sums[0].tile, sums[0].tiles
    n_f, n_r = len(fold.scratch()), len(sums[0].scratch())

    def kernel(
        act_r, du_r, hid_r, wd_r, dhb_r, h_r, wo_r, q_r, k_r, v_r, l_r, c_r, s_r, sg_r,
        w_r, x_r, inv_r, dh_r, g_r, *refs
    ):
        up_o, usq_o, y_o, in_o, out, gg_o = refs[:6]
        pb, db, wbuf, bias, dk, dv, ls, ws = refs[6:14]
        f_s = refs[14 : 14 + n_f]
        load_act = pltpu.make_async_copy(act_r, pb, ls.at[0])
        load_du = pltpu.make_async_copy(du_r, db, ls.at[1])
        load_dhb = pltpu.make_async_copy(dhb_r, pb, ls.at[2])
        load_hid = pltpu.make_async_copy(hid_r, db, ls.at[3])
        load_act.start()
        load_du.start()

        def fetch(t):
            return pltpu.make_async_copy(
                wd_r.at[pl.ds(t * tile, tile), :], wbuf.at[t % 2], ws.at[t]
            )

        fetch(0).start()
        place = Place(dp, mp)
        own = pl.multiple_of(place.m * share, 8)
        place.barrier()
        fold.bind(place, f_s)
        for n, r in enumerate(sums):
            r.bind(place, refs[14 + n_f + n * n_r : 14 + n_f + (n + 1) * n_r])
        load_act.wait()
        load_du.wait()
        for j, kk in fold.blocks:
            r = j * fold.hi + kk
            fold.g[r] = jnp.dot(
                pb[:, r * blk : (r + 1) * blk].T, db[...], preferred_element_type=f32
            ).astype(low_type)
            fold.ready(j, kk)
        load_hid.start()
        load_dhb.start()
        load_hid.wait()

        def before(t):
            fetch(t).wait()
            if t + 1 < tiles:
                fetch(t + 1).start()

        def partial_y(start, count, t, n):
            return lax.dot_general(
                db[pl.ds(start, count), :], wbuf[t % 2], NT, preferred_element_type=f32
            )

        sums[0].scatter(partial_y, before)
        fold.step_once()
        load_dhb.wait()
        dk[...] = jnp.zeros_like(dk)
        dv[...] = jnp.zeros_like(dv)
        length = sequence_length(sg_r[...], rows)
        for b in range(rows // block):
            rs = pl.ds(b * block, block)
            keys = (b + 1) * block
            ks = slice(0, keys)
            bias[:, ks] = attention_bias(length, b * block, block, keys)
            do = lax.dot_general(pb[rs, :], wo_r[...], NT, preferred_element_type=f32).astype(
                low_type
            )
            cs, sn = c_r[rs, :], s_r[rs, :]
            for n in range(heads):
                hs = slice(n * hd, (n + 1) * hd)
                qb = q_r[rs, hs]
                s = lax.dot_general(qb, k_r[ks, :], NT, preferred_element_type=f32)
                p = jnp.exp(s * scale + bias[:, ks] - l_r[rs, n : n + 1])
                dpr = lax.dot_general(do[:, hs], v_r[ks, :], NT, preferred_element_type=f32)
                centre = jnp.sum(p * dpr, axis=-1, keepdims=True)
                ds = (p * (dpr - centre)).astype(low_type)
                u = jnp.dot(ds, k_r[ks, :], preferred_element_type=f32) * scale
                out[rs, hs] = (u * cs - pltpu.roll(u, hd // 2, 1) * sn).astype(low_type)
                dk[ks, :] += lax.dot_general(ds, qb, TN, preferred_element_type=f32)
                dv[ks, :] += lax.dot_general(
                    p.astype(low_type), do[:, hs], TN, preferred_element_type=f32
                )
            fold.step_once()

        u = dk[...] * scale
        out[:, qcols : qcols + hd] = (
            u * c_r[...] - pltpu.roll(u, hd // 2, 1) * s_r[...]
        ).astype(low_type)
        out[:, qcols + hd :] = dv[...].astype(low_type)

        def partial_in(start, count, t, n):
            return lax.dot_general(
                out[pl.ds(start, count), :],
                w_r[pl.ds(t * n, n), :],
                NT,
                preferred_element_type=f32,
            )

        sums[1].scatter(partial_in)
        read_y = sums[0].arrive()

        @pl.loop(0, share // 32)
        def _(t):
            rs = pl.ds(pl.multiple_of(t * 32, 32), 32)
            v = (h_r[rs, :] + read_y(t * 32, 32)).astype(low_type)
            put_natural(place, y_o, rs, v, blk)

        fold.step_once()
        read = sums[1].arrive()
        gg_o[...] = jnp.zeros_like(gg_o)

        @pl.loop(0, share // 32)
        def _(t):
            rs = pl.ds(pl.multiple_of(t * 32, 32), 32)
            v, x = read(t * 32, 32), x_r[rs, :].astype(f32)
            inv = inv_r[rs, :1]
            weighted = v * g_r[...]
            mean = jnp.mean(weighted * x, axis=-1, keepdims=True)
            d = dh_r[rs, :] + inv * weighted - x * (inv * inv * inv * mean)
            put_natural(place, in_o, rs, d.astype(low_type), blk)
            gg_o[...] += jnp.sum((v * x * inv).reshape(4, 8, width), axis=0)

        fold.finish(up_o, usq_o)
        for r in sums:
            r.finish()

    sds = jax.ShapeDtypeStruct
    return pl.pallas_call(
        kernel,
        name="attention_backward",
        out_shape=fold.out_shapes()
        + [
            sds((share, width), low_type),
            sds((share, width), low_type),
            sds((rows, qcols + 2 * hd), low_type),
            sds((8, width), f32),
        ],
        in_specs=[HBM] * 5 + [VM] * 14,
        out_specs=[VM] * 6,
        scratch_shapes=[
            pltpu.VMEM((rows, width), low_type),
            pltpu.VMEM((rows, ff), low_type),
            pltpu.VMEM((2, tile, ff), low_type),
            pltpu.VMEM((block, rows), f32),
            pltpu.VMEM((rows, hd), f32),
            pltpu.VMEM((rows, hd), f32),
            DMA((4,)),
            DMA((tiles,)),
        ]
        + fold.scratch()
        + sums[0].scratch()
        + sums[1].scratch(),
        compiler_params=big(cid),
        cost_estimate=cost(3e10, 1e8),
    )(
        act, du, hid, wd, dhb, h_own, wo, q, k, v, lse, cosine, sine, segment,
        wqkv, x_own, inv_own, dh_own, gain
    )


def inputs_back_call(
    dhb, ob, a1, dqkv, y_own, in_own, gain_one, gain_two, squares, kv_heads, dp, mp, cid
):
    rows, width = dhb.shape
    qcols, cols = ob.shape[1], dqkv.shape[1]
    blk = width // dp
    kv_rows, wide = blk // mp, cols - qcols
    folds = [Fold(blk, cols, dp, 2), Fold(qcols, blk, dp, 2)]
    spreads = [Spread(rows, mp, 2), Spread(rows, mp, 2)]
    share = rows // mp
    n_f, n_s = len(folds[0].scratch()), len(spreads[0].scratch())
    n_sq = len(squares)
    local = [m * kv_heads // mp for m in range(mp)]
    shared = mp > kv_heads

    def kernel(dhb_r, ob_r, a_r, d_r, y_r, in_r, g1_r, g2_r, *refs):
        sq_r, refs = refs[:n_sq], refs[n_sq:]
        q_o, wo_o, kv_o, y_o, in_o, gain_o, tot_o = refs[:7]
        qkv, sq0, sq1, obt, mine, got, sent, got2, t1, t2, gm, gd, ls, ts = refs[7:21]
        at = 21
        place = Place(dp, mp)
        me_dp, me_mp = lax.axis_index("dp"), place.m
        place.barrier()
        for f in folds:
            f.bind(place, refs[at : at + n_f])
            at += n_f
        mine[...] = jnp.zeros_like(mine)
        mine[0:1, :] = jnp.sum(g1_r[...], axis=0, keepdims=True)
        mine[1:2, :] = jnp.sum(g2_r[...], axis=0, keepdims=True)
        got[place.m] = mine[...]
        gains_mp = []
        for n, m in place.others_mp():
            c = remote(mine, got.at[place.m], gm.at[0, n], gm.at[1, n], {"mp": m})
            c.start()
            gains_mp.append(c)
        keeps = []
        for n, (p, own, full) in enumerate(zip(spreads, (y_r, in_r), (y_o, in_o))):
            p.bind(place, refs[at : at + n_s], full, own)
            at += n_s
            for r in range(p.parts):
                p.send(r)
            c = pltpu.make_async_copy(
                own, full.at[pl.ds(pl.multiple_of(place.m * share, 8), share), :], ls.at[n]
            )
            c.start()
            keeps.append(c)
        for n in range(qcols // 128):
            obt[n * 128 : (n + 1) * 128, :] = ob_r[:, n * 128 : (n + 1) * 128].T
        for j, k in folds[0].blocks:
            r = j * folds[0].hi + k
            bs = slice(r * blk, (r + 1) * blk)
            folds[0].g[r] = jnp.dot(
                a_r[:, bs].T, d_r[...], preferred_element_type=f32
            ).astype(low_type)
            folds[0].ready(j, k)
            folds[1].g[r] = jnp.dot(obt[...], dhb_r[:, bs], preferred_element_type=f32).astype(
                low_type
            )
            folds[1].ready(j, k)

        def both():
            for f in folds:
                f.step_once()

        for c in gains_mp:
            c.wait()
        v = got[0]
        for n in range(1, mp):
            v += got[n]
        for r in range(dp):
            sent[r] = v[:, r * blk : (r + 1) * blk]
        gains_dp = []
        for r, d in place.others_dp():
            c = remote(sent.at[r], got2.at[r], gd.at[0, r], gd.at[1, r], {"dp": d})
            c.start()
            gains_dp.append(c)
        both()
        both()
        for p in spreads:
            for r in range(p.parts):
                p.forward(r)
                both()
        while folds[0].items or folds[1].items:
            both()
        for c in gains_dp:
            c.wait()
        v = sent[0]
        for r in range(1, dp):
            v += got2[r]
        gain_o[...] = v
        total = jnp.zeros((1, 1), f32)
        for q in sq_r:
            total += whole(q[...])
        v = whole(v * v)
        total += jnp.where(me_mp == 0, v, jnp.zeros_like(v))
        folds[0].finish(qkv, sq0)
        q_o[...] = qkv[:, :qcols]
        swaps = []
        for n, m in place.others_mp():
            c = remote(
                qkv.at[pl.ds(pl.multiple_of(m * kv_rows, 8), kv_rows), pl.ds(qcols, wide)],
                kv_o.at[me_mp],
                ts.at[0, n],
                ts.at[1, n],
                {"mp": m},
            )
            c.start()
            swaps.append(c)
        kv_o[me_mp] = qkv[pl.ds(pl.multiple_of(me_mp * kv_rows, 8), kv_rows), qcols:]
        folds[1].finish(wo_o, sq1)
        total += whole(sq1[...])
        if shared:
            total += whole(sq0[:, :qcols])
            for c in swaps:
                c.wait_recv()
            for h in range(kv_heads):
                own = [m for m in range(mp) if local[m] == h]
                v = kv_o[own[0]]
                for m in own[1:]:
                    v += kv_o[m]
                total += whole(v * v)
        else:
            total += whole(sq0[...])
        for peers, table, me, base in (
            ([(n, {"mp": m}) for n, m in place.others_mp()], t1, me_mp, 2),
            ([(n, {"dp": d}) for n, d in place.others_dp()], t2, me_dp, 4),
        ):
            table[me] = jnp.broadcast_to(total, (8, 128))
            waits = []
            for n, to in peers:
                c = remote(table.at[me], table.at[me], ts.at[base, n], ts.at[base + 1, n], to)
                c.start()
                waits.append(c)
            for c in waits:
                c.wait()
            total = table[0]
            for n in range(1, len(peers) + 1):
                total += table[n]
        tot_o[...] = total
        for c in swaps:
            if shared:
                c.wait_send()
            else:
                c.wait()
        for p, c in zip(spreads, keeps):
            p.finish()
            c.wait()

    sds = jax.ShapeDtypeStruct
    return pl.pallas_call(
        kernel,
        name="inputs_backward",
        out_shape=[
            sds((blk, qcols), f32),
            sds((qcols, blk), f32),
            sds((mp, kv_rows, wide), f32),
            sds((rows, width), low_type),
            sds((rows, width), low_type),
            sds((8, blk), f32),
            sds((8, 128), f32),
        ],
        in_specs=[VM] * (8 + n_sq),
        out_specs=[VM] * 7,
        scratch_shapes=[
            pltpu.VMEM((blk, cols), f32),
            pltpu.VMEM((8, cols), f32),
            pltpu.VMEM((8, blk), f32),
            pltpu.VMEM((qcols, rows), low_type),
            pltpu.VMEM((8, width), f32),
            pltpu.VMEM((mp, 8, width), f32),
            pltpu.VMEM((dp, 8, blk), f32),
            pltpu.VMEM((dp, 8, blk), f32),
            pltpu.VMEM((mp, 8, 128), f32),
            pltpu.VMEM((dp, 8, 128), f32),
            DMA((2, mp)),
            DMA((2, dp)),
            DMA((2,)),
            DMA((6, max(dp, mp))),
        ]
        + folds[0].scratch()
        + folds[1].scratch()
        + spreads[0].scratch()
        + spreads[1].scratch(),
        compiler_params=big(cid),
        cost_estimate=cost(1e10, 5e7),
    )(dhb, ob, a1, dqkv, y_own, in_own, gain_one, gain_two, *squares)


def whole(v):
    return jnp.sum(jnp.sum(v, axis=0, keepdims=True), axis=1, keepdims=True)


def update_call(total, widen, groups):
    steps = 8
    count = len(groups)

    def split(shape):
        return shape[-2] % (steps * 8) == 0 and shape[-2] >= 128

    def spec(shape, cut):
        lead = len(shape) - 2
        rows = shape[-2] // steps if cut else shape[-2]
        return pl.BlockSpec(
            shape[:-2] + (rows, shape[-1]), lambda i: (0,) * lead + (i if cut else 0, 0)
        )

    ins, in_specs, outs, out_specs, kinds = [], [], [], [], []
    for weight, moment, square, grads, rate, decay in groups:
        cut = split(weight.shape)
        ins += [weight, moment, square] + grads
        in_specs += [spec(weight.shape, cut)] * 3 + [spec(g.shape, cut) for g in grads]
        outs += [jax.ShapeDtypeStruct(weight.shape, f32)] * 3
        out_specs += [spec(weight.shape, cut)] * 3
        kinds.append((len(grads), rate, decay))

    wide_spec = pl.BlockSpec((widen.shape[0] // steps, widen.shape[1]), lambda i: (i, 0))
    outs.append(jax.ShapeDtypeStruct(widen.shape, f32))
    out_specs.append(wide_spec)

    def kernel(tot_r, wide_r, *refs):
        out_refs = refs[len(ins) :]
        out_refs[-1][...] = wide_r[...].astype(f32)
        norm = jnp.sqrt(tot_r[:1, :1])
        factor = jnp.minimum(1.0, clip_limit / (norm + 1e-06))
        at = 0
        for n, (parts, rate, decay) in enumerate(kinds):
            w_r, m_r, s_r = refs[at : at + 3]
            g_rs = refs[at + 3 : at + 3 + parts]
            at += 3 + parts
            w_o, m_o, s_o = out_refs[3 * n : 3 * n + 3]

            def one(index, gradient):
                new = adam_update(
                    w_r[index], m_r[index], s_r[index], gradient, factor, rate, decay
                )
                w_o[index], m_o[index], s_o[index] = new

            if parts == 1 and g_rs[0].shape == w_r.shape:
                one(..., g_rs[0][...])
            elif parts == 1 and g_rs[0].ndim == 3:
                copies, _, wide = g_rs[0].shape
                hd = wide // 2
                heads = w_r.shape[2] // hd
                for h in range(heads):
                    v = None
                    for m in range(copies):
                        if m * heads // copies == h:
                            v = g_rs[0][m] if v is None else v + g_rs[0][m]
                    for i in range(2):
                        index = (i, slice(None), slice(h * hd, (h + 1) * hd))
                        one(index, v[:, i * hd : (i + 1) * hd])
            elif parts == 1:
                one(..., g_rs[0][: w_r.shape[0], :])
            else:
                for i in range(parts):
                    one(i, g_rs[i][...])

    return pl.pallas_call(
        kernel,
        name="update",
        grid=(steps,),
        out_shape=outs,
        in_specs=[pl.BlockSpec((8, 128), lambda i: (0, 0)), wide_spec] + in_specs,
        out_specs=out_specs,
        compiler_params=pltpu.CompilerParams(vmem_limit_bytes=48 * 2**20),
        cost_estimate=cost(3e7, 4e7),
    )(total, widen, *ins)


def body(
    tokens,
    segment_ids,
    out_grad,
    query_weight,
    keyval_weight,
    output_weight,
    gateup_weight,
    down_weight,
    norm_gains,
    query_moment,
    keyval_moment,
    output_moment,
    gateup_moment,
    down_moment,
    gains_moment,
    query_square,
    keyval_square,
    output_square,
    gateup_square,
    down_square,
    gains_square,
):
    dp = lax.axis_size("dp")
    mp = lax.axis_size("mp")
    heads = H // mp
    rows = tokens.shape[0]
    blk = D // dp
    qcols = query_weight.shape[1]

    half = np.arange(HD // 2, dtype=np.float64) * 2.0 / HD
    rates = jnp.asarray(np.tile(rope_base**-half, 2)[None].astype(np.float32))
    segment = segment_ids.reshape(-1, 128)
    (
        wqkv, wo, gains, og, x_own, act_one, inv_one, q, k, v, attn, lse, gate_low, up_low, down_low,
        cosine, sine,
    ) = attention_call(
        tokens, out_grad, query_weight, keyval_weight, output_weight, norm_gains,
        gateup_weight, down_weight, segment, rates, heads, KV, dp, mp, 0, norm_eps,
    )
    gain_one, gain_two = gains[0:1], gains[1:2]
    wg, wu, wd, h_own, inv_two, act_two, hid, ga, ub = forward_call(
        attn, wo, x_own, gain_two, gate_low, up_low, down_low, dp, mp, 1, norm_eps
    )
    down_share, down_sq, gate_share, gate_sq, du, dh_own, dhb, gain_two_part = mlp_back_call(
        hid, og, act_two, ga, ub, wd, wg, wu, h_own, inv_two, gain_two, dp, mp, 2
    )
    up_share, up_sq, y_own, in_own, dqkv, gain_one_part = attention_back_call(
        act_two, du, hid, wd, h_own, dhb, wo, q, k, v, lse, cosine, sine, segment,
        wqkv, x_own, inv_one, dh_own, gain_one, heads, dp, mp, 3,
    )
    query_share, output_share, kv_parts, layer_out, in_low, gains_share, total = inputs_back_call(
        dhb, attn, act_one, dqkv, y_own, in_own, gain_one_part, gain_two_part,
        [down_sq, gate_sq, up_sq], KV, dp, mp, 4,
    )
    grad_norm = jnp.sqrt(total[0, 0])
    output_rate = matrix_rate * (TOK_DEV * D / (16.0 * H * HD)) ** 0.5
    *news, input_grad = update_call(
        total,
        in_low,
        [
            (query_weight, query_moment, query_square, [query_share], matrix_rate, weight_decay),
            (keyval_weight, keyval_moment, keyval_square, [kv_parts], matrix_rate, weight_decay),
            (
                output_weight, output_moment, output_square, [output_share],
                output_rate, weight_decay,
            ),
            (
                gateup_weight, gateup_moment, gateup_square, [gate_share, up_share],
                matrix_rate, weight_decay,
            ),
            (down_weight, down_moment, down_square, [down_share], matrix_rate, weight_decay),
            (norm_gains, gains_moment, gains_square, [gains_share], gain_rate, 0.0),
        ],
    )
    return (layer_out, input_grad, grad_norm) + tuple(news[0::3] + news[1::3] + news[2::3])


def solution(mesh):
    params = (
        P("dp", "mp"),
        P(None, ("dp", "mp"), None),
        P("mp", "dp"),
        P(None, "dp", "mp"),
        P("mp", "dp"),
        P(None, "dp"),
    )
    rows = P("dp", None)
    return jax.shard_map(
        body,
        mesh=mesh,
        in_specs=(rows, P("dp"), rows) + params * 3,
        out_specs=(rows, rows, P()) + params * 3,
        check_vma=False,
    )
```

```python
import jax
import jax.numpy as jnp
import numpy as np
from jax import lax
from jax.experimental import pallas as pl
from jax.experimental.pallas import tpu as pltpu
from jax.sharding import PartitionSpec as P

MESH_ID = pl.DeviceIdType.MESH
low_type = jnp.bfloat16
f32 = jnp.float32
WINDOW = 32
HBM = pl.BlockSpec(memory_space=pl.ANY)
VM = pl.BlockSpec(memory_space=pltpu.VMEM)
DMA = pltpu.SemaphoreType.DMA
NT = (((1,), (1,)), ((), ()))
TN = (((0,), (0,)), ((), ()))


D = 2048
H = 16
KV = 4
HD = 128
TOK_DEV = 1024
ADAM_STEP = 10


norm_eps = 1e-05
rope_base = 10000.0
clip_limit = 1.0
beta_first = 0.9
beta_second = 0.95
adam_eps = 1e-08
weight_decay = 0.1
matrix_rate = 0.02
gain_rate = 0.6


def adam_update(weight, moment, square, gradient, factor, step_rate, decay_rate):
    clipped = gradient * factor
    moment_new = beta_first * moment + (1.0 - beta_first) * clipped
    square_new = beta_second * square + (1.0 - beta_second) * clipped * clipped
    first_fix = 1.0 - beta_first**ADAM_STEP
    second_fix = 1.0 - beta_second**ADAM_STEP
    step_dir = moment_new / first_fix / (jnp.sqrt(square_new / second_fix) + adam_eps)
    return (weight - step_rate * (step_dir + decay_rate * weight), moment_new, square_new)


def split_dp(count):
    lo = 1
    while lo * lo * 4 <= count:
        lo *= 2
    return count // lo, lo


class Place:
    def __init__(self, dp, mp):
        self.dp, self.mp = dp, mp
        self.hi, self.lo = split_dp(dp)
        self.mlo = 2 if mp % 2 == 0 else 1
        self.mhi = mp // self.mlo
        me = lax.axis_index("dp")
        self.h, self.l = me // self.lo, lax.rem(me, self.lo)
        self.m = lax.axis_index("mp")
        self.y, self.c = self.m // self.mlo, lax.rem(self.m, self.mlo)

    def z(self, k):
        return {"dp": lax.rem(self.h + (k + self.hi) % self.hi, self.hi) * self.lo + self.l}

    def x(self, j):
        return {"dp": self.h * self.lo + lax.rem(self.l + (j + self.lo) % self.lo, self.lo)}

    def part(self, k, i):
        return lax.rem(self.y + k, self.mhi) * self.mlo + lax.rem(self.c + i, self.mlo)

    def others_dp(self):
        out = []
        for j in range(self.lo):
            for k in range(self.hi):
                if j or k:
                    out.append((j * self.hi + k, self.owner(j, k)))
        return out

    def owner(self, j, k):
        return lax.rem(self.h + self.hi - k, self.hi) * self.lo + lax.rem(
            self.l + self.lo - j, self.lo
        )

    def others_mp(self):
        return [(s, lax.rem(self.m + s, self.mp)) for s in range(1, self.mp)]

    def barrier(self):
        bar = pltpu.get_barrier_semaphore()
        peers = [{"dp": d} for _, d in self.others_dp()] + [{"mp": m} for _, m in self.others_mp()]
        for p in peers:
            pl.semaphore_signal(bar, inc=1, device_id=p, device_id_type=MESH_ID)
        pl.semaphore_wait(bar, len(peers))


def remote(src, dst, send, recv, to):
    return pltpu.make_async_remote_copy(src, dst, send, recv, to, MESH_ID)


class Gather:
    def __init__(self, shapes, axes, splits, dp, late=()):
        self.hi, self.lo = split_dp(dp)
        self.shapes, self.axes, self.late = shapes, axes, late
        self.chunks = []
        for i, s in enumerate(shapes):
            step = s[0] // splits[i]
            self.chunks += [(i, n * step, step) for n in range(splits[i])]
        self.count = len(self.chunks)

    def out_shapes(self):
        n = self.hi * self.lo
        return [
            jax.ShapeDtypeStruct((s[0] * n, s[1]) if a == 0 else (s[0], s[1] * n), low_type)
            for s, a in zip(self.shapes, self.axes)
        ]

    def scratch(self):
        c, hi, lo = self.count, self.hi, self.lo
        return [
            DMA((c, hi - 1)),
            DMA((c, hi - 1)),
            DMA((c, hi, max(lo - 1, 1))),
            DMA((c, hi, max(lo - 1, 1))),
            DMA((c,)),
        ]

    def bind(self, place, ins, outs, sems):
        zs, zr, xs, xr, ls = sems
        hi, lo = self.hi, self.lo

        def dst(c, r):
            i, at, step = self.chunks[c]
            rows, cols = self.shapes[i]
            if self.axes[i] == 0:
                return outs[i].at[pl.ds(r * rows + at, step)]
            return outs[i].at[pl.ds(at, step), pl.ds(r * cols, cols)]

        def src(c):
            i, at, step = self.chunks[c]
            return ins[i].at[pl.ds(at, step)]

        self.zc = {
            (c, k): remote(src(c), dst(c, k), zs.at[c, k - 1], zr.at[c, k - 1], place.z(k))
            for c in range(self.count)
            for k in range(1, hi)
        }
        self.xc = {
            (c, k, j): remote(
                src(c) if k == 0 else dst(c, k),
                dst(c, j * hi + k),
                xs.at[c, k, j - 1],
                xr.at[c, k, j - 1],
                place.x(j),
            )
            for c in range(self.count)
            for k in range(hi)
            for j in range(1, lo)
        }
        self.lc = [pltpu.make_async_copy(src(c), dst(c, 0), ls.at[c]) for c in range(self.count)]
        self.items = []
        self.started = 0
        self.window = 2
        for c in range(self.count):
            for k in range(1, hi):
                self.items.append((c, k))
        self.arrived = [False] * self.count

    def start_own(self, c):
        for j in range(1, self.lo):
            self.xc[c, 0, j].start()
        self.lc[c].start()

    def start_z(self, c):
        if c in self.late:
            self.late[c]()
            self.start_own(c)
        for k in range(1, self.hi):
            self.zc[c, k].start()

    def begin(self):
        for c in range(self.count):
            if c < self.window:
                self.start_z(c)
            if c not in self.late:
                self.start_own(c)
        self.started = min(self.window, self.count)

    def step(self, n=1):
        for _ in range(n):
            if not self.items:
                return
            c, k = self.items.pop(0)
            self.zc[c, k].wait_recv()
            for j in range(1, self.lo):
                self.xc[c, k, j].start()
            if k == self.hi - 1 and self.started < self.count:
                self.start_z(self.started)
                self.started += 1

    def arrive(self, c):
        if self.arrived[c]:
            return
        while any(i[0] <= c for i in self.items):
            self.step()
        self.lc[c].wait()
        for k in range(self.hi):
            for j in range(1, self.lo):
                self.xc[c, k, j].wait_recv()
        self.arrived[c] = True

    def finish(self):
        for c in range(self.count):
            self.arrive(c)
        for c in range(self.count):
            for k in range(1, self.hi):
                self.zc[c, k].wait_send()
            for k in range(self.hi):
                for j in range(1, self.lo):
                    self.xc[c, k, j].wait_send()


class LineGather(Gather):
    def __init__(self, shapes, splits, dp, first):
        super().__init__(shapes, (0,) * len(shapes), splits, dp)
        self.first = first

    def scratch(self):
        c, hi, lo = self.count, self.hi, self.lo
        return [
            DMA((c, lo, hi)),
            DMA((c, lo, hi)),
            DMA((c, lo, hi)),
            DMA((c, hi)),
            DMA((c, hi)),
            DMA((c,)),
        ]

    def bind(self, place, ins, outs, sems):
        us, ds, zr, xs, xr, ls = sems
        hi, lo = self.hi, self.lo
        self.h = place.h

        def slot(c, j, k):
            i, at, step = self.chunks[c]
            r = j * hi + k
            return outs[i].at[pl.ds(r * self.shapes[i][0] + at, step)]

        def src(c, j, k):
            i, at, step = self.chunks[c]
            return slot(c, j, k) if j or k else ins[i].at[pl.ds(at, step)]

        self.rows_of = [range(lo) if c in self.first else range(1) for c in range(self.count)]
        each = [(c, j, k) for c in range(self.count) for j in self.rows_of[c] for k in range(hi)]
        self.up = {
            (c, j, k): remote(
                src(c, j, k), slot(c, j, k + 1), us.at[c, j, k], zr.at[c, j, k + 1], place.z(1)
            )
            for c, j, k in each
            if k < hi - 1
        }
        self.down = {
            (c, j, k): remote(
                src(c, j, k),
                slot(c, j, (k - 1) % hi),
                ds.at[c, j, k],
                zr.at[c, j, (k - 1) % hi],
                place.z(-1),
            )
            for c, j, k in each
            if k != 1
        }
        self.into = {
            (c, j, k): remote(
                slot(c, j, k), slot(c, j, k), us.at[c, j, k - 1], zr.at[c, j, k], place.z(1)
            )
            for c, j, k in each
            if k
        }
        self.xc = {
            (c, k): remote(src(c, 0, k), slot(c, 1, k), xs.at[c, k], xr.at[c, k], place.x(1))
            for c in range(self.count)
            for k in range(1 if c in self.first else hi)
        }
        self.lc = [
            pltpu.make_async_copy(src(c, 0, 0), slot(c, 0, 0), ls.at[c]) for c in range(self.count)
        ]
        self.items = [
            (c, j, k) for c in range(self.count) for j in self.rows_of[c] for k in (1, 3, 2)
        ]
        self.window = 3
        self.arrived = [False] * self.count

    def passes(self, k):
        h, hi = self.h, self.hi
        if k == 0:
            return h < hi - 1, h > 0
        return (h >= k) & (h < hi - 1), (h < k) & (h > 0)

    def pass_on(self, key, act):
        c, j, k = key
        up, down = self.passes(k)
        if key in self.up:

            @pl.when(up)
            def _():
                act(self.up[key])

        if key in self.down:

            @pl.when(down)
            def _():
                act(self.down[key])

    def start_z(self, c):
        for j in self.rows_of[c]:
            if j:
                self.xc[c, 0].wait_recv()
            self.pass_on((c, j, 0), lambda copy: copy.start())

    def begin(self):
        for c in range(self.count):
            if c < self.window:
                self.start_z(c)
            self.xc[c, 0].start()
            self.lc[c].start()
        self.started = min(self.window, self.count)

    def step(self, n=1):
        for _ in range(n):
            if not self.items:
                return
            c, j, k = self.items.pop(0)
            self.into[c, j, k].wait_recv()
            self.pass_on((c, j, k), lambda copy: copy.start())
            if (c, k) in self.xc:
                self.xc[c, k].start()
            if (j, k) == (self.rows_of[c][-1], 2) and self.started < self.count:
                self.start_z(self.started)
                self.started += 1

    def arrive(self, c):
        if self.arrived[c]:
            return
        while any(i[0] <= c for i in self.items):
            self.step()
        self.lc[c].wait()
        for k in range(self.hi):
            if (c, k) in self.xc and c not in self.first:
                self.xc[c, k].wait_recv()
        self.arrived[c] = True

    def finish(self):
        for c in range(self.count):
            self.arrive(c)
        for c in range(self.count):
            for j in self.rows_of[c]:
                for k in range(self.hi):
                    self.pass_on((c, j, k), lambda copy: copy.wait_send())
        for copy in self.xc.values():
            copy.wait_send()


class RowSum:
    def __init__(self, rows, width, mp):
        self.mlo = 2 if mp % 2 == 0 else 1
        self.mhi = mp // self.mlo
        self.share, self.width = rows // mp, width
        self.tile = min(512, width)
        self.tiles = width // self.tile

    def scratch(self):
        h, t = self.mhi, self.tiles
        g = max(h - 1, 1)
        return [
            pltpu.VMEM((h, self.share, self.width), low_type),
            pltpu.VMEM((h, self.share, self.width), low_type),
            pltpu.VMEM((g, self.share, self.width), low_type),
            pltpu.VMEM((g, self.share, self.width), low_type),
            pltpu.VMEM((self.share, self.width), f32),
            DMA((h, t)),
            DMA((h, t)),
            DMA((g, t)),
            DMA((g, t)),
        ]

    def bind(self, place, refs):
        self.place = place
        (self.cs, self.cr, self.ys, self.yr, self.acc) = refs[:5]
        css, crs, yss, yrs = refs[5:]
        h = self.mhi

        def sl(ref, k, t):
            return ref.at[k, :, pl.ds(t * self.tile, self.tile)]

        other = {"mp": place.part(0, 1)}
        self.cc = {
            (k, t): remote(sl(self.cs, k, t), sl(self.cr, k, t), css.at[k, t], crs.at[k, t], other)
            for k in range(h)
            for t in range(self.tiles)
        }
        self.yc = {
            (k, t): remote(
                sl(self.ys, k - 1, t),
                sl(self.yr, k - 1, t),
                yss.at[k - 1, t],
                yrs.at[k - 1, t],
                {"mp": place.part(k, 0)},
            )
            for k in range(1, h)
            for t in range(self.tiles)
        }

    def start_of(self, k, i):
        return pl.multiple_of(self.place.part(k, i) * self.share, 8)

    def scatter(self, partial, before=lambda t: None, between=lambda: None):
        order = list(range(1, self.mhi)) + [0]
        for t in range(self.tiles):
            before(t)
            cols = pl.ds(t * self.tile, self.tile)
            if self.mlo > 1:
                for k in order:
                    v = partial(self.start_of(k, 1), self.share, t, self.tile)
                    self.cs[k, :, cols] = v.astype(low_type)
                    self.cc[k, t].start()
            for k in order:
                v = partial(self.start_of(k, 0), self.share, t, self.tile)
                if self.mlo > 1:
                    self.cc[k, t].wait_recv()
                    v += self.cr[k, :, cols].astype(f32)
                if k:
                    self.ys[k - 1, :, cols] = v.astype(low_type)
                    self.yc[k, t].start()
                else:
                    self.acc[:, cols] = v
            between()

    def arrive(self):
        for t in range(self.tiles):
            for k in range(1, self.mhi):
                self.yc[k, t].wait_recv()

        def read(at, count):
            v = self.acc[pl.ds(at, count), :]
            for k in range(1, self.mhi):
                v += self.yr[k - 1, pl.ds(at, count), :].astype(f32)
            return v

        return read

    def finish(self):
        for t in range(self.tiles):
            if self.mlo > 1:
                for k in range(self.mhi):
                    self.cc[k, t].wait_send()
            for k in range(1, self.mhi):
                self.yc[k, t].wait_send()

    def free(self, credit):
        for k in range(1, self.mhi):
            to = {"mp": self.place.part(k, 0)}
            pl.semaphore_signal(credit, inc=1, device_id=to, device_id_type=MESH_ID)
        for i in range(1, self.mlo):
            to = {"mp": self.place.part(0, i)}
            pl.semaphore_signal(credit, inc=1, device_id=to, device_id_type=MESH_ID)

    def freed(self, credit):
        pl.semaphore_wait(credit, self.mhi - 1 + self.mlo - 1)


class Spread:
    def __init__(self, rows, mp, parts):
        self.mlo = 2 if mp % 2 == 0 else 1
        self.mhi = mp // self.mlo
        self.share, self.parts = rows // mp, parts
        self.step = self.share // parts

    def scratch(self):
        h, p = self.mhi, self.parts
        g = max(h - 1, 1)
        return [DMA((g, p)), DMA((g, p)), DMA((h, p)), DMA((h, p))]

    def bind(self, place, refs, full, own=None):
        gys, gyr, gcs, gcr = refs
        h, p = self.mhi, self.parts
        other = {"mp": place.part(0, 1)}

        def rows_at(m, r):
            return full.at[pl.ds(pl.multiple_of(m * self.share + r * self.step, 8), self.step), :]

        def mine(r):
            if own is None:
                return rows_at(place.m, r)
            return own.at[pl.ds(r * self.step, self.step), :]

        self.gy = {
            (k, r): remote(
                mine(r),
                rows_at(place.m, r),
                gys.at[k - 1, r],
                gyr.at[k - 1, r],
                {"mp": place.part(k, 0)},
            )
            for k in range(1, h)
            for r in range(p)
        }
        self.gc = {
            (k, r): remote(
                rows_at(place.part((h - k) % h, 0), r) if k else mine(r),
                rows_at(place.part((h - k) % h, 0), r),
                gcs.at[k, r],
                gcr.at[k, r],
                other,
            )
            for k in range(h)
            for r in range(p)
        }

    def send(self, r):
        for k in range(1, self.mhi):
            self.gy[k, r].start()
        if self.mlo > 1:
            self.gc[0, r].start()

    def forward(self, r):
        for k in range(1, self.mhi):
            self.gy[k, r].wait_recv()
            if self.mlo > 1:
                self.gc[k, r].start()

    def finish(self):
        for r in range(self.parts):
            if self.mlo > 1:
                for k in range(self.mhi):
                    self.gc[k, r].wait()
            for k in range(1, self.mhi):
                self.gy[k, r].wait_send()


def sequence_length(seg, rows):
    top = jnp.max(jnp.max(seg, axis=1, keepdims=True), axis=0, keepdims=True)
    return jnp.where(top == 0, rows, jnp.where(top == 1, rows // 2, rows // 4))


def attention_bias(length, start, count, keys):
    row = start + lax.broadcasted_iota(jnp.int32, (count, 1), 0)
    first = row - (row & (length - 1))
    col = lax.broadcasted_iota(jnp.int32, (count, keys), 1)
    return jnp.where((col <= row) & (col >= first), 0.0, -1e30)


def small_rows(total, step, fn):
    @pl.loop(0, total // step)
    def _(t):
        fn(pl.multiple_of(t * step, step))


def forward_call(attn, wo, x_own, gain, gate, up, down, dp, mp, cid, eps):
    rows, width = attn.shape[0], x_own.shape[1]
    ff = gate.shape[1]
    shapes = [gate.shape, up.shape, down.shape]
    if split_dp(dp) == (4, 2):
        gather = LineGather(shapes, (2, 2, 2), dp, (5,))
    else:
        gather = Gather(shapes, (0, 0, 0), (2, 2, 2), dp)
    rsum, spread = RowSum(rows, width, mp), Spread(rows, mp, 2)
    share = rsum.share
    n_g, n_r = len(gather.scratch()), len(rsum.scratch())
    tile = 128

    def kernel(attn_r, wo_r, x_r, gain_r, gate_r, up_r, down_r, *refs):
        wg_o, wu_o, wd_o, h_o, inv_o, act_o = refs[:6]
        saved = refs[6:9]
        hid_v, ga_v, ub_v, wg_v, wu_v, wsem, ssem = refs[9:16]
        g_s = refs[16 : 16 + n_g]
        r_s = refs[16 + n_g : 16 + n_g + n_r]
        place = Place(dp, mp)
        place.barrier()
        gather.bind(place, (gate_r, up_r, down_r), (wg_o, wu_o, wd_o), g_s)
        rsum.bind(place, r_s)
        spread.bind(place, refs[16 + n_g + n_r :], act_o)
        gather.begin()

        def partial(start, count, t, n):
            return jnp.dot(
                attn_r[pl.ds(start, count), :],
                wo_r[:, pl.ds(t * n, n)],
                preferred_element_type=f32,
            )

        rsum.scatter(partial)
        gather.step(2)
        read = rsum.arrive()
        for r in range(spread.parts):
            base = r * spread.step
            own = place.m * share

            def norm(at):
                v = x_r[pl.ds(base + at, 32), :].astype(f32) + read(base + at, 32)
                h_o[pl.ds(base + at, 32), :] = v
                inv = lax.rsqrt(jnp.mean(v * v, axis=-1, keepdims=True) + eps)
                inv_o[pl.ds(base + at, 32), :] = jnp.broadcast_to(inv, (32, 128))
                act_o[pl.ds(pl.multiple_of(own + base + at, 32), 32), :] = (
                    v * inv * gain_r[...]
                ).astype(low_type)

            small_rows(spread.step, 32, norm)
            spread.send(r)
            gather.step(1)
        for r in range(spread.parts):
            spread.forward(r)
            gather.step(1)
        spread.finish()
        rsum.finish()
        for c in range(2):
            gather.arrive(c)
        cg = pltpu.make_async_copy(wg_o, wg_v, wsem.at[0])
        cg.start()
        for c in range(2, 4):
            gather.arrive(c)
        cu = pltpu.make_async_copy(wu_o, wu_v, wsem.at[1])
        cu.start()
        cg.wait()
        cu.wait()
        groups = 4
        per = rows // tile // groups
        stores = []
        for q in range(groups):

            @pl.loop(q * per, (q + 1) * per)
            def _(t):
                rs = pl.ds(pl.multiple_of(t * tile, tile), tile)
                a = act_o[rs, :]
                gp = jnp.dot(a, wg_v[...], preferred_element_type=f32)
                upv = jnp.dot(a, wu_v[...], preferred_element_type=f32)
                sg = jax.nn.sigmoid(gp)
                sw = gp * sg
                hid_v[rs, :] = (sw * upv).astype(low_type)
                ga_v[rs, :] = (upv * sg * (1.0 + gp * (1.0 - sg))).astype(low_type)
                ub_v[rs, :] = sw.astype(low_type)

            rs = pl.ds(q * per * tile, per * tile)
            for n, (v, o) in enumerate(zip((hid_v, ga_v, ub_v), saved)):
                c = pltpu.make_async_copy(v.at[rs, :], o.at[rs, :], ssem.at[q, n])
                c.start()
                stores.append(c)
            gather.step(3)
        gather.finish()
        for c in stores:
            c.wait()

    sds = jax.ShapeDtypeStruct
    act_shape = sds((rows, ff), low_type)
    return pl.pallas_call(
        kernel,
        name="forward_mlp",
        out_shape=gather.out_shapes()
        + [
            sds((share, width), f32),
            sds((share, 128), f32),
            sds((rows, width), low_type),
            act_shape,
            act_shape,
            act_shape,
        ],
        in_specs=[VM] * 4 + [HBM] * 3,
        out_specs=[HBM] * 3 + [VM] * 3 + [HBM] * 3,
        scratch_shapes=[pltpu.VMEM((rows, ff), low_type)] * 3
        + [
            pltpu.VMEM((width, ff), low_type),
            pltpu.VMEM((width, ff), low_type),
            DMA((2,)),
            DMA((4, 3)),
        ]
        + gather.scratch()
        + rsum.scratch()
        + spread.scratch(),
        compiler_params=big(cid),
        cost_estimate=cost(2e10, 1e8),
    )(attn, wo, x_own, gain, gate, up, down)


def fold_order(hi):
    return sorted(range(1, hi), key=lambda k: -min(k, hi - k)) + [0]


class Fold:
    def __init__(self, rows, cols, dp, sub):
        self.hi, self.lo = split_dp(dp)
        self.rows, self.cols, self.sub = rows, cols, sub
        self.step = rows // sub
        self.order = fold_order(self.hi)

    def scratch(self):
        hi, lo, s = self.hi, self.lo, self.sub
        j = max(lo - 1, 1)
        return [
            pltpu.VMEM((lo * hi, self.rows, self.cols), low_type),
            pltpu.VMEM((j * hi, self.rows, self.cols), low_type),
            pltpu.VMEM((hi - 1, self.rows, self.cols), low_type),
            DMA((j, hi, s)),
            DMA((j, hi, s)),
            DMA((hi - 1, s)),
            DMA((hi - 1, s)),
        ]

    def out_shapes(self):
        return [
            jax.ShapeDtypeStruct((self.rows, self.cols), f32),
            jax.ShapeDtypeStruct((8, self.cols), f32),
        ]

    def bind(self, place, refs):
        self.g, self.xb, self.zb, xs, xr, zs, zr = refs
        hi, lo = self.hi, self.lo

        def part(s):
            return pl.ds(s * self.step, self.step)

        self.part = part
        self.xc = {
            (k, j, s): remote(
                self.g.at[j * hi + k, part(s), :],
                self.xb.at[(j - 1) * hi + k, part(s), :],
                xs.at[j - 1, k, s],
                xr.at[j - 1, k, s],
                place.x(-j),
            )
            for k in range(hi)
            for j in range(1, lo)
            for s in range(self.sub)
        }
        self.zc = {
            (k, s): remote(
                self.g.at[k, part(s), :],
                self.zb.at[k - 1, part(s), :],
                zs.at[k - 1, s],
                zr.at[k - 1, s],
                place.z(-k),
            )
            for k in range(1, hi)
            for s in range(self.sub)
        }
        self.items = [(k, s) for k in self.order for s in range(self.sub)]
        self.blocks = [(j, k) for j in range(1, lo) for k in self.order]
        self.blocks += [(0, k) for k in self.order]
        self.small = next(n for n in (64, 32, 16, 8) if self.step % n == 0)

    def tiles(self, s, fn):
        @pl.loop(0, self.step // self.small)
        def _(t):
            fn(pl.ds(pl.multiple_of(s * self.step + t * self.small, self.small), self.small))

    def send_x(self, k, s):
        for j in range(1, self.lo):
            self.xc[k, j, s].start()

    def add_and_send(self, k, s):
        for j in range(1, self.lo):
            self.xc[k, j, s].wait_recv()
        if k:

            def add(rs):
                v = self.g[k, rs, :].astype(f32)
                for j in range(1, self.lo):
                    v += self.xb[(j - 1) * self.hi + k, rs, :].astype(f32)
                self.g[k, rs, :] = v.astype(low_type)

            self.tiles(s, add)
            self.zc[k, s].start()

    def finish(self, out, squares):
        squares[...] = jnp.zeros_like(squares)
        for s in range(self.sub):
            for k in range(1, self.hi):
                self.zc[k, s].wait_recv()

            def add(rs):
                v = self.g[0, rs, :].astype(f32)
                for j in range(1, self.lo):
                    v += self.xb[(j - 1) * self.hi, rs, :].astype(f32)
                for k in range(1, self.hi):
                    v += self.zb[k - 1, rs, :].astype(f32)
                out[rs, :] = v
                squares[...] += jnp.sum((v * v).reshape(self.small // 8, 8, self.cols), axis=0)

            self.tiles(s, add)
        for c in self.xc.values():
            c.wait_send()
        for c in self.zc.values():
            c.wait_send()


class FoldQueue:
    def __init__(self, folds, window=WINDOW):
        self.order = [(f, k, s) for f in folds for k, s in f.items]
        self.have = set()
        self.window, self.started, self.done = window, 0, 0

    def ready(self, fold, j, k):
        self.have.add((id(fold), j, k))
        self.pump()

    def pump(self):
        while self.started < min(len(self.order), self.done + self.window):
            f, k, s = self.order[self.started]
            if any((id(f), j, k) not in self.have for j in range(1, f.lo)):
                return
            f.send_x(k, s)
            self.started += 1

    def advance(self, n=1):
        for _ in range(n):
            if self.done == self.started:
                return
            f, k, s = self.order[self.done]
            if (id(f), 0, k) not in self.have:
                return
            f.add_and_send(k, s)
            self.done += 1
            self.pump()

    def finish(self):
        self.advance(len(self.order))
        assert self.done == len(self.order)


def big(cid, remote_kernel=True):
    extra = {"collective_id": cid, "has_side_effects": True} if remote_kernel else {}
    return pltpu.CompilerParams(vmem_limit_bytes=62 * 2**20, **extra)


def cost(flops, bytes_accessed):
    return pl.CostEstimate(
        flops=int(flops), bytes_accessed=int(bytes_accessed), transcendentals=10**6
    )


def attention_call(
    tokens, out_grad, wq, wkv, wo, gains, gateup, down, segment, rates,
    heads, kv_heads, dp, mp, cid, eps
):
    rows, width = tokens.shape
    hd = rates.shape[1]
    blk, qcols = wq.shape
    kv_rows = wkv.shape[1]
    ff = down.shape[0]
    block = min(256, rows)
    scale = hd**-0.5
    share = rows // mp
    cols = qcols + 2 * hd
    late = {}
    gather = Gather(
        [(16, blk), wq.shape, (blk, 2 * hd), wo.shape], (0, 0, 0, 1), (1, 2, 1, 2), dp, late
    )
    n_g = len(gather.scratch())

    def kernel(tok_r, og_r, q_f, kv_f, wo_f, gn_f, gu_r, dn_r, sg_r, rt_r, *refs):
        (wqkv_o, wo_o, gain_o, og_o, x_o, a_o, inv_o, qo, ko, vo, ob_o, lse_o, gl_o, ul_o, dl_o) = (
            refs[:15]
        )
        c_r, s_r = refs[15:17]
        kvx, gall, xv, wv, bias, q_r, kv_r, wo_r, gn_r, ks, kr, cs_, ws = refs[17:30]
        g_s = refs[30:]
        place = Place(dp, mp)
        copies = []
        for j in range(place.lo):
            for k in range(place.hi):
                r = j * place.hi + k
                at = pl.ds(pl.multiple_of(place.owner(j, k) * blk, 128), blk)
                to = pl.ds(r * blk, blk)
                copies.append(pltpu.make_async_copy(tok_r.at[:, at], xv.at[:, to], cs_.at[0, r]))
                copies.append(
                    pltpu.make_async_copy(og_r.at[:, at], og_o.at[:, to], cs_.at[1, r])
                )
        for c in copies:
            c.start()
        gn_r[...] = jnp.zeros_like(gn_r)
        gn_r[:2, :] = gn_f[...].astype(low_type)
        q_r[...] = q_f[...].astype(low_type)
        for n in range(kv_heads):
            for i in range(2):
                kv_r[:, (2 * n + i) * hd : (2 * n + i + 1) * hd] = kv_f[
                    i, :, n * hd : (n + 1) * hd
                ].astype(low_type)
        wo_r[...] = wo_f[...].astype(low_type)
        place.barrier()
        here = pl.ds(pl.multiple_of(place.m * kv_rows, kv_rows), kv_rows)
        swaps = []
        for n, m in place.others_mp():
            head = m * kv_heads // mp
            c = remote(
                kv_r.at[:, pl.ds(pl.multiple_of(head * 2 * hd, 128), 2 * hd)],
                kvx.at[here],
                ks.at[n],
                kr.at[n],
                {"mp": m},
            )
            c.start()
            swaps.append(c)
        head = place.m * kv_heads // mp
        mine = pltpu.make_async_copy(
            kv_r.at[:, pl.ds(pl.multiple_of(head * 2 * hd, 128), 2 * hd)], kvx.at[here], ks.at[0]
        )
        mine.start()

        def swapped():
            mine.wait()
            for c in swaps:
                c.wait_recv()

        late[3] = swapped
        gather.bind(
            place,
            (gn_r, q_r, kvx, wo_r),
            (gall, wqkv_o.at[:, pl.ds(0, qcols)], wqkv_o.at[:, pl.ds(qcols, 2 * hd)], wo_o),
            g_s,
        )
        gather.begin()

        @pl.loop(0, blk // 32)
        def _(t):
            rs = pl.ds(pl.multiple_of(t * 32, 32), 32)
            gl_o[rs, :] = gu_r[0, rs, :].astype(low_type)
            ul_o[rs, :] = gu_r[1, rs, :].astype(low_type)

        dl_o[...] = dn_r[...].T.astype(low_type)
        gather.step(2 * (gather.hi - 1))
        length = sequence_length(sg_r[...], rows)

        @pl.loop(0, rows // 128)
        def _(t):
            at = pl.multiple_of(t * 128, 128)
            row = at + lax.broadcasted_iota(jnp.int32, (128, 1), 0)
            angle = (row & (length - 1)).astype(f32) * rt_r[...]
            lane = lax.broadcasted_iota(jnp.int32, (128, hd), 1)
            c_r[pl.ds(at, 128), :] = jnp.cos(angle)
            sn = jnp.sin(angle)
            s_r[pl.ds(at, 128), :] = jnp.where(lane < hd // 2, -sn, sn)

        for c in copies:
            c.wait()
        own = place.m * share

        @pl.loop(0, share // 32)
        def _(t):
            at = pl.multiple_of(t * 32, 32)
            v = xv[pl.ds(pl.multiple_of(own + at, 32), 32), :]
            x_o[pl.ds(at, 32), :] = v
            v = v.astype(f32)
            inv = lax.rsqrt(jnp.mean(v * v, axis=-1, keepdims=True) + eps)
            inv_o[pl.ds(at, 32), :] = jnp.broadcast_to(inv, (32, 128))

        gather.arrive(0)
        for c in (1, 2, 3):
            gather.arrive(c)
        wcopy = pltpu.make_async_copy(wqkv_o, wv, ws.at[0])
        wcopy.start()
        for r in range(dp):
            at = r * 16
            gain_o[:, r * blk : (r + 1) * blk] = gall[at : at + 8, :].astype(f32)
        wcopy.wait()
        gain = gain_o[:1, :]
        half = rows // 128 // 2
        for q in range(2):

            @pl.loop(q * half, (q + 1) * half)
            def _(t):
                rs = pl.ds(pl.multiple_of(t * 128, 128), 128)
                v = xv[rs, :].astype(f32)
                inv = lax.rsqrt(jnp.mean(v * v, axis=-1, keepdims=True) + eps)
                a = (v * inv * gain).astype(low_type)
                a_o[rs, :] = a
                raw = jnp.dot(a, wv[...], preferred_element_type=f32)
                cs, sn = c_r[rs, :], s_r[rs, :]
                for n in range(heads):
                    u = raw[:, n * hd : (n + 1) * hd]
                    qo[rs, n * hd : (n + 1) * hd] = (
                        u * cs + pltpu.roll(u, hd // 2, 1) * sn
                    ).astype(low_type)
                u = raw[:, qcols : qcols + hd]
                ko[rs, :] = (u * cs + pltpu.roll(u, hd // 2, 1) * sn).astype(low_type)
                vo[rs, :] = raw[:, qcols + hd :].astype(low_type)

            gather.step(1)

        for q in range(rows // block):
            rs = pl.ds(q * block, block)
            keys = (q + 1) * block
            bias[:, :keys] = attention_bias(length, q * block, block, keys)
            lane = lax.broadcasted_iota(jnp.int32, (block, 128), 1)
            lse = jnp.zeros((block, 128), f32)
            for n in range(heads):
                hs = slice(n * hd, (n + 1) * hd)
                s = lax.dot_general(qo[rs, hs], ko[:keys, :], NT, preferred_element_type=f32)
                s = s * scale + bias[:, :keys]
                top = jnp.max(s, axis=-1, keepdims=True)
                e = jnp.exp(s - top)
                total = jnp.sum(e, axis=-1, keepdims=True)
                p = (e * (1.0 / total)).astype(low_type)
                ob_o[rs, hs] = jnp.dot(p, vo[:keys, :], preferred_element_type=f32).astype(
                    low_type
                )
                lse = jnp.where(lane == n, top + jnp.log(total), lse)
            lse_o[rs, :] = lse
            gather.step(1)
        gather.finish()
        for c in swaps:
            c.wait_send()

    sds = jax.ShapeDtypeStruct
    return pl.pallas_call(
        kernel,
        name="attention_forward",
        out_shape=[
            sds((width, cols), low_type),
            sds((qcols, width), low_type),
            sds((8, width), f32),
            sds((rows, width), low_type),
            sds((share, width), low_type),
            sds((rows, width), low_type),
            sds((share, 128), f32),
            sds((rows, qcols), low_type),
            sds((rows, hd), low_type),
            sds((rows, hd), low_type),
            sds((rows, qcols), low_type),
            sds((rows, 128), f32),
            sds((blk, ff), low_type),
            sds((blk, ff), low_type),
            sds((blk, ff), low_type),
            sds((rows, hd), f32),
            sds((rows, hd), f32),
        ],
        in_specs=[HBM] * 2 + [VM] * 8,
        out_specs=[HBM, HBM] + [VM] * 15,
        scratch_shapes=[
            pltpu.VMEM((blk, 2 * hd), low_type),
            pltpu.VMEM((16 * dp, blk), low_type),
            pltpu.VMEM((rows, width), low_type),
            pltpu.VMEM((width, cols), low_type),
            pltpu.VMEM((block, rows), f32),
            pltpu.VMEM((blk, qcols), low_type),
            pltpu.VMEM((kv_rows, kv_heads * 2 * hd), low_type),
            pltpu.VMEM(wo.shape, low_type),
            pltpu.VMEM((16, blk), low_type),
            DMA((mp,)),
            DMA((mp,)),
            DMA((2, dp)),
            DMA((1,)),
        ]
        + gather.scratch(),
        compiler_params=big(cid),
        cost_estimate=cost(6e9, 2e7),
    )(tokens, out_grad, wq, wkv, wo, gains, gateup, down, segment, rates)


def put_natural(place, ref, rows, value, blk):
    for j in range(place.lo):
        for k in range(place.hi):
            owner = place.owner(j, k)
            r = j * place.hi + k
            ref[rows, pl.ds(pl.multiple_of(owner * blk, 128), blk)] = value[
                :, r * blk : (r + 1) * blk
            ]


def mlp_back_call(hid, og, act, ga, ub, wd, wg, wu, h_own, inv_own, gain, dp, mp, cid):
    rows, ff = hid.shape
    width = og.shape[1]
    blk = width // dp
    folds = [Fold(blk, ff, dp, 2), Fold(blk, ff, dp, 2)]
    rsum, spread = RowSum(rows, width, mp), Spread(rows, mp, 2)
    share, tile = rsum.share, rsum.tile
    n_f, n_r = len(folds[0].scratch()), len(rsum.scratch())

    def kernel(
        hid_r, og_r, act_r, ga_r, ub_r, wd_r, wg_r, wu_r, h_r, inv_r, g_r, *refs
    ):
        (down_o, dsq_o, gate_o, gsq_o, du_o, dh_o, dhb_o, gg_o) = refs[:8]
        pb, ogx, dg, du, wbuf, ls, ws, wd_s = refs[8:16]
        at = 16
        for f in folds:
            f_refs = refs[at : at + n_f]
            at += n_f
            f.refs = f_refs
        r_s = refs[at : at + n_r]
        p_s = refs[at + n_r :]
        place = Place(dp, mp)
        own = pl.multiple_of(place.m * share, 8)
        load_og = pltpu.make_async_copy(og_r, pb, ls.at[0])
        load_hid = pltpu.make_async_copy(hid_r, dg, ls.at[1])
        load_ub = pltpu.make_async_copy(ub_r, du, ls.at[2])
        load_own = pltpu.make_async_copy(og_r.at[pl.ds(own, share), :], ogx, ls.at[3])
        load_ga = pltpu.make_async_copy(ga_r, dg, ls.at[4])
        load_act = pltpu.make_async_copy(act_r, pb, ls.at[5])
        store_du = pltpu.make_async_copy(du, du_o, ls.at[6])
        tiles = rsum.tiles
        load_wd = [
            pltpu.make_async_copy(
                wd_r.at[pl.ds(t * tile, tile), :], wbuf.at[t // 2, t % 2], wd_s.at[t]
            )
            for t in range(tiles)
        ]

        def fetch(t):
            rs = pl.ds(t * tile, tile)
            return [
                pltpu.make_async_copy(w.at[rs, :], wbuf.at[t % 2, i], ws.at[t, i])
                for i, w in enumerate((wg_r, wu_r))
            ]

        for c in [load_og, load_hid, load_ub, load_own] + load_wd:
            c.start()
        place.barrier()
        for f in folds:
            f.bind(place, f.refs)
        rsum.bind(place, r_s)
        spread.bind(place, p_s, dhb_o)
        load_og.wait()
        load_hid.wait()
        first, second = folds
        queue = FoldQueue(folds)
        for j, k in first.blocks:
            r = j * first.hi + k
            first.g[r] = jnp.dot(
                pb[:, r * blk : (r + 1) * blk].T, dg[...], preferred_element_type=f32
            ).astype(low_type)
            queue.ready(first, j, k)
        load_ga.start()
        for c in load_wd + [load_ub, load_ga]:
            c.wait()
        groups = 4
        per = rows // 128 // groups
        for q in range(groups):

            @pl.loop(q * per, (q + 1) * per)
            def _(n):
                rs = pl.ds(pl.multiple_of(n * 128, 128), 128)
                d = jnp.dot(pb[rs, :tile], wbuf[0, 0], preferred_element_type=f32)
                for t in range(1, tiles):
                    d += jnp.dot(
                        pb[rs, t * tile : (t + 1) * tile],
                        wbuf[t // 2, t % 2],
                        preferred_element_type=f32,
                    )
                dg[rs, :] = (d * dg[rs, :].astype(f32)).astype(low_type)
                du[rs, :] = (d * du[rs, :].astype(f32)).astype(low_type)

            if q > 0:
                queue.advance()
        store_du.start()
        load_act.start()
        for c in fetch(0):
            c.start()

        def before(t):
            for c in fetch(t):
                c.wait()
            if t + 1 < tiles:
                for c in fetch(t + 1):
                    c.start()

        def partial(start, count, t, n):
            rs = pl.ds(start, count)
            return lax.dot_general(
                dg[rs, :], wbuf[t % 2, 0], NT, preferred_element_type=f32
            ) + lax.dot_general(du[rs, :], wbuf[t % 2, 1], NT, preferred_element_type=f32)

        rsum.scatter(partial, before, queue.advance)
        load_act.wait()
        for n, (j, k) in enumerate(second.blocks):
            r = j * second.hi + k
            second.g[r] = jnp.dot(
                pb[:, r * blk : (r + 1) * blk].T, dg[...], preferred_element_type=f32
            ).astype(low_type)
            queue.ready(second, j, k)
        load_own.wait()
        read = rsum.arrive()
        gg_o[...] = jnp.zeros_like(gg_o)
        for r in range(spread.parts):

            @pl.loop(0, spread.step // 32)
            def _(t):
                at = pl.multiple_of(r * spread.step + t * 32, 32)
                rs = pl.ds(at, 32)
                v, h = read(at, 32), h_r[rs, :]
                inv = inv_r[rs, :1]
                weighted = v * g_r[...]
                mean = jnp.mean(weighted * h, axis=-1, keepdims=True)
                dh = ogx[rs, :].astype(f32) + inv * weighted - h * (inv * inv * inv * mean)
                dh_o[rs, :] = dh
                dhb_o[pl.ds(pl.multiple_of(own + at, 32), 32), :] = dh.astype(low_type)
                gg_o[...] += jnp.sum((v * h * inv).reshape(4, 8, width), axis=0)

            spread.send(r)
            queue.advance()
        for r in range(spread.parts):
            spread.forward(r)
            queue.advance()
        queue.finish()
        first.finish(gate_o, dsq_o)
        down_o[...] = gate_o[...].T
        second.finish(gate_o, gsq_o)
        spread.finish()
        rsum.finish()
        store_du.wait()

    sds = jax.ShapeDtypeStruct
    square = sds((8, ff), f32)
    return pl.pallas_call(
        kernel,
        name="mlp_backward",
        out_shape=[
            sds((ff, blk), f32),
            square,
            sds((blk, ff), f32),
            square,
            sds((rows, ff), low_type),
            sds((share, width), f32),
            sds((rows, width), low_type),
            sds((8, width), f32),
        ],
        in_specs=[HBM] * 8 + [VM] * 3,
        out_specs=[VM] * 4 + [HBM] + [VM] * 3,
        scratch_shapes=[
            pltpu.VMEM((rows, width), low_type),
            pltpu.VMEM((share, width), low_type),
            pltpu.VMEM((rows, ff), low_type),
            pltpu.VMEM((rows, ff), low_type),
            pltpu.VMEM((2, 2, tile, ff), low_type),
            DMA((7,)),
            DMA((rsum.tiles, 2)),
            DMA((rsum.tiles,)),
        ]
        + folds[0].scratch()
        + folds[1].scratch()
        + rsum.scratch()
        + spread.scratch(),
        compiler_params=big(cid),
        cost_estimate=cost(4e10, 1e8),
    )(hid, og, act, ga, ub, wd, wg, wu, h_own, inv_own, gain)


def attention_back_call(
    act, du, hid, wd, dhb, wqkv, a1, h_own, wo, q, k, v, lse, cosine, sine, segment,
    ob, x_own, inv_own, dh_own, gain, gain_two, squares, heads, kv_heads, dp, mp, cid
):
    rows, width = act.shape
    ff = du.shape[1]
    hd = cosine.shape[1]
    qcols, cols = heads * hd, wqkv.shape[1]
    blk = width // dp
    kv_rows, wide = blk // mp, cols - qcols
    block = min(256, rows)
    scale = hd**-0.5
    folds = [Fold(blk, ff, dp, 2), Fold(qcols, blk, dp, 2), Fold(blk, cols, dp, 2)]
    rsum = RowSum(rows, width, mp)
    spreads = [Spread(rows, mp, 2), Spread(rows, mp, 2)]
    share, tile, tiles = rsum.share, rsum.tile, rsum.tiles
    n_f, n_r, n_s = len(folds[0].scratch()), len(rsum.scratch()), len(spreads[0].scratch())
    n_sq = len(squares)
    local = [m * kv_heads // mp for m in range(mp)]
    shared = mp > kv_heads

    def kernel(
        act_r, du_r, hid_r, wd_r, dhb_r, wqkv_r, a_r, h_r, wo_r, q_r, k_r, v_r, l_r, c_r, s_r,
        sg_r, ob_r, x_r, inv_r, dh_r, g_r, g2_r, *refs
    ):
        sq_r, refs = refs[:n_sq], refs[n_sq:]
        up_o, q_o, wo_o, kv_o, y_o, in_o, gain_o, tot_o = refs[:8]
        (pb, db, wbuf, bias, dk, dv, out, y_own, in_own, sq0, sq1, sq2, obt) = refs[8:21]
        (gg, mine, got, sent, got2, t1, t2, ls, ws, gm, gd, ts, credit) = refs[21:34]
        at = 34
        place = Place(dp, mp)
        me_dp, me_mp = lax.axis_index("dp"), place.m
        own = pl.multiple_of(place.m * share, 8)
        load_act = pltpu.make_async_copy(act_r, pb, ls.at[0])
        load_du = pltpu.make_async_copy(du_r, db, ls.at[1])
        load_dhb = pltpu.make_async_copy(dhb_r, pb, ls.at[2])
        load_hid = pltpu.make_async_copy(hid_r, db, ls.at[3])
        load_a = pltpu.make_async_copy(a_r, pb, ls.at[4])
        keeps = [
            pltpu.make_async_copy(o, full.at[pl.ds(own, share), :], ls.at[5 + n])
            for n, (o, full) in enumerate(((y_own, y_o), (in_own, in_o)))
        ]

        def fetch(t):
            return pltpu.make_async_copy(
                wd_r.at[pl.ds(t * tile, tile), :], wbuf.at[t % 2], ws.at[0, t]
            )

        def fetch_qkv(t):
            return pltpu.make_async_copy(
                wqkv_r.at[pl.ds(t * tile, tile), :],
                wbuf.at[t % 2, :, pl.ds(0, cols)],
                ws.at[1, t],
            )

        load_act.start()
        load_du.start()
        fetch(0).start()
        place.barrier()
        for f in folds:
            f.bind(place, refs[at : at + n_f])
            at += n_f
        rsum.bind(place, refs[at : at + n_r])
        at += n_r
        for p, o, full in zip(spreads, (y_own, in_own), (y_o, in_o)):
            p.bind(place, refs[at : at + n_s], full, o)
            at += n_s
        up, wof, qkvf = folds
        spread_y, spread_in = spreads
        queue = FoldQueue(folds)
        advance = queue.advance

        load_act.wait()
        load_du.wait()
        for j, kk in up.blocks:
            r = j * up.hi + kk
            up.g[r] = jnp.dot(
                pb[:, r * blk : (r + 1) * blk].T, db[...], preferred_element_type=f32
            ).astype(low_type)
            queue.ready(up, j, kk)
        load_hid.start()
        load_dhb.start()
        load_hid.wait()

        def before(t):
            fetch(t).wait()
            if t + 1 < tiles:
                fetch(t + 1).start()

        def partial_y(start, count, t, n):
            return lax.dot_general(
                db[pl.ds(start, count), :], wbuf[t % 2], NT, preferred_element_type=f32
            )

        rsum.scatter(partial_y, before)
        fetch_qkv(0).start()
        advance()
        for n in range(qcols // 128):
            obt[n * 128 : (n + 1) * 128, :] = ob_r[:, n * 128 : (n + 1) * 128].T
        load_dhb.wait()
        for j, kk in wof.blocks:
            r = j * wof.hi + kk
            wof.g[r] = jnp.dot(
                obt[...], pb[:, r * blk : (r + 1) * blk], preferred_element_type=f32
            ).astype(low_type)
            queue.ready(wof, j, kk)
        dk[...] = jnp.zeros_like(dk)
        dv[...] = jnp.zeros_like(dv)
        length = sequence_length(sg_r[...], rows)
        count = rows // block
        for b in range(count):
            rs = pl.ds(b * block, block)
            keys = (b + 1) * block
            ks = slice(0, keys)
            bias[:, ks] = attention_bias(length, b * block, block, keys)
            do = lax.dot_general(pb[rs, :], wo_r[...], NT, preferred_element_type=f32).astype(
                low_type
            )
            cs, sn = c_r[rs, :], s_r[rs, :]
            for n in range(heads):
                hs = slice(n * hd, (n + 1) * hd)
                qb = q_r[rs, hs]
                s = lax.dot_general(qb, k_r[ks, :], NT, preferred_element_type=f32)
                p = jnp.exp(s * scale + bias[:, ks] - l_r[rs, n : n + 1])
                dpr = lax.dot_general(do[:, hs], v_r[ks, :], NT, preferred_element_type=f32)
                centre = jnp.sum(p * dpr, axis=-1, keepdims=True)
                ds = (p * (dpr - centre)).astype(low_type)
                u = jnp.dot(ds, k_r[ks, :], preferred_element_type=f32) * scale
                out[rs, hs] = (u * cs - pltpu.roll(u, hd // 2, 1) * sn).astype(low_type)
                dk[ks, :] += lax.dot_general(ds, qb, TN, preferred_element_type=f32)
                dv[ks, :] += lax.dot_general(
                    p.astype(low_type), do[:, hs], TN, preferred_element_type=f32
                )
            if b == count // 2:
                read_y = rsum.arrive()

                @pl.loop(0, share // 32)
                def _(t):
                    rt = pl.ds(pl.multiple_of(t * 32, 32), 32)
                    y = (h_r[rt, :] + read_y(t * 32, 32)).astype(low_type)
                    put_natural(place, y_own, rt, y, blk)

                for r in range(spread_y.parts):
                    spread_y.send(r)
                keeps[0].start()
                rsum.finish()
                rsum.free(credit)
            advance()
        load_a.start()
        u = dk[...] * scale
        out[:, qcols : qcols + hd] = (
            u * c_r[...] - pltpu.roll(u, hd // 2, 1) * s_r[...]
        ).astype(low_type)
        out[:, qcols + hd :] = dv[...].astype(low_type)

        def before_in(t):
            fetch_qkv(t).wait()
            if t + 1 < tiles:
                fetch_qkv(t + 1).start()

        def partial_in(start, count, t, n):
            return lax.dot_general(
                out[pl.ds(start, count), :],
                wbuf[t % 2, :, :cols],
                NT,
                preferred_element_type=f32,
            )

        rsum.freed(credit)
        rsum.scatter(partial_in, before_in)
        advance()
        load_a.wait()
        for n, (j, kk) in enumerate(qkvf.blocks):
            r = j * qkvf.hi + kk
            qkvf.g[r] = jnp.dot(
                pb[:, r * blk : (r + 1) * blk].T, out[...], preferred_element_type=f32
            ).astype(low_type)
            queue.ready(qkvf, j, kk)
            if n % 4 == 3:
                advance()
        for r in range(spread_y.parts):
            spread_y.forward(r)
            advance(2)
        advance(2)
        read = rsum.arrive()
        gg[...] = jnp.zeros_like(gg)

        @pl.loop(0, share // 32)
        def _(t):
            rs = pl.ds(pl.multiple_of(t * 32, 32), 32)
            g, x = read(t * 32, 32), x_r[rs, :].astype(f32)
            inv = inv_r[rs, :1]
            weighted = g * g_r[...]
            mean = jnp.mean(weighted * x, axis=-1, keepdims=True)
            d = dh_r[rs, :] + inv * weighted - x * (inv * inv * inv * mean)
            put_natural(place, in_own, rs, d.astype(low_type), blk)
            gg[...] += jnp.sum((g * x * inv).reshape(4, 8, width), axis=0)

        mine[...] = jnp.zeros_like(mine)
        mine[0:1, :] = jnp.sum(gg[...], axis=0, keepdims=True)
        mine[1:2, :] = jnp.sum(g2_r[...], axis=0, keepdims=True)
        got[place.m] = mine[...]
        gains_mp = []
        for n, m in place.others_mp():
            c = remote(mine, got.at[place.m], gm.at[0, n], gm.at[1, n], {"mp": m})
            c.start()
            gains_mp.append(c)
        for r in range(spread_in.parts):
            spread_in.send(r)
        keeps[1].start()
        advance(4)
        for c in gains_mp:
            c.wait()
        g = got[0]
        for n in range(1, mp):
            g += got[n]
        for r in range(dp):
            sent[r] = g[:, r * blk : (r + 1) * blk]
        gains_dp = []
        for r, d in place.others_dp():
            c = remote(sent.at[r], got2.at[r], gd.at[0, r], gd.at[1, r], {"dp": d})
            c.start()
            gains_dp.append(c)
        advance(2)
        for r in range(spread_in.parts):
            spread_in.forward(r)
            advance(1)
        queue.finish()
        for c in gains_dp:
            c.wait()
        g = sent[0]
        for r in range(1, dp):
            g += got2[r]
        gain_o[...] = g
        g = whole(g * g)
        total = jnp.where(me_mp == 0, g, jnp.zeros_like(g))
        for a in sq_r:
            total += whole(a[...])
        up.finish(up_o, sq0)
        wof.finish(wo_o, sq1)
        total += whole(sq0[...]) + whole(sq1[...])
        qkv = rsum.acc.at[pl.ds(0, blk), pl.ds(0, cols)]
        qkvf.finish(qkv, sq2)
        swaps = []
        for n, m in place.others_mp():
            c = remote(
                qkv.at[pl.ds(pl.multiple_of(m * kv_rows, 8), kv_rows), pl.ds(qcols, wide)],
                kv_o.at[me_mp],
                ts.at[0, n],
                ts.at[1, n],
                {"mp": m},
            )
            c.start()
            swaps.append(c)
        kv_o[me_mp] = qkv[pl.ds(pl.multiple_of(me_mp * kv_rows, 8), kv_rows), qcols:]
        if shared:
            total += whole(sq2[:, :qcols])
            for c in swaps:
                c.wait_recv()
            for h in range(kv_heads):
                of = [m for m in range(mp) if local[m] == h]
                g = kv_o[of[0]]
                for m in of[1:]:
                    g += kv_o[m]
                total += whole(g * g)
        else:
            total += whole(sq2[...])
        for peers, table, me, base in (
            ([(n, {"mp": m}) for n, m in place.others_mp()], t1, me_mp, 2),
            ([(n, {"dp": d}) for n, d in place.others_dp()], t2, me_dp, 4),
        ):
            table[me] = jnp.broadcast_to(total, (8, 128))
            waits = []
            for n, to in peers:
                c = remote(table.at[me], table.at[me], ts.at[base, n], ts.at[base + 1, n], to)
                c.start()
                waits.append(c)
            if base == 2:
                q_o[...] = qkv[:, :qcols]
            for c in waits:
                c.wait()
            total = table[0]
            for n in range(1, len(peers) + 1):
                total += table[n]
        tot_o[...] = total
        for c in swaps:
            if shared:
                c.wait_send()
            else:
                c.wait()
        rsum.finish()
        for p, c in zip(spreads, keeps):
            p.finish()
            c.wait()

    sds = jax.ShapeDtypeStruct
    scratch = []
    for part in folds + [rsum] + spreads:
        scratch += part.scratch()
    return pl.pallas_call(
        kernel,
        name="attention_backward",
        out_shape=[
            sds((blk, ff), f32),
            sds((blk, qcols), f32),
            sds((qcols, blk), f32),
            sds((mp, kv_rows, wide), f32),
            sds((rows, width), low_type),
            sds((rows, width), low_type),
            sds((8, blk), f32),
            sds((8, 128), f32),
        ],
        in_specs=[HBM] * 7 + [VM] * (15 + n_sq),
        out_specs=[VM] * 4 + [HBM] * 2 + [VM] * 2,
        scratch_shapes=[
            pltpu.VMEM((rows, width), low_type),
            pltpu.VMEM((rows, ff), low_type),
            pltpu.VMEM((2, tile, max(ff, cols)), low_type),
            pltpu.VMEM((block, rows), f32),
            pltpu.VMEM((rows, hd), f32),
            pltpu.VMEM((rows, hd), f32),
            pltpu.VMEM((rows, cols), low_type),
            pltpu.VMEM((share, width), low_type),
            pltpu.VMEM((share, width), low_type),
            pltpu.VMEM((8, ff), f32),
            pltpu.VMEM((8, blk), f32),
            pltpu.VMEM((8, cols), f32),
            pltpu.VMEM((qcols, rows), low_type),
            pltpu.VMEM((8, width), f32),
            pltpu.VMEM((8, width), f32),
            pltpu.VMEM((mp, 8, width), f32),
            pltpu.VMEM((dp, 8, blk), f32),
            pltpu.VMEM((dp, 8, blk), f32),
            pltpu.VMEM((mp, 8, 128), f32),
            pltpu.VMEM((dp, 8, 128), f32),
            DMA((7,)),
            DMA((2, tiles)),
            DMA((2, mp)),
            DMA((2, dp)),
            DMA((6, max(dp, mp))),
            pltpu.SemaphoreType.REGULAR,
        ]
        + scratch,
        compiler_params=big(cid),
        cost_estimate=cost(4e10, 1e8),
    )(
        act, du, hid, wd, dhb, wqkv, a1, h_own, wo, q, k, v, lse, cosine, sine, segment,
        ob, x_own, inv_own, dh_own, gain, gain_two, *squares
    )


def whole(v):
    return jnp.sum(jnp.sum(v, axis=0, keepdims=True), axis=1, keepdims=True)


def update_call(total, widen, keep, groups):
    steps = 8
    count = len(groups)

    def split(shape):
        return shape[-2] % (steps * 8) == 0 and shape[-2] >= 128

    def spec(shape, cut):
        lead = len(shape) - 2
        rows = shape[-2] // steps if cut else shape[-2]
        return pl.BlockSpec(
            shape[:-2] + (rows, shape[-1]), lambda i: (0,) * lead + (i if cut else 0, 0)
        )

    ins, in_specs, outs, out_specs, kinds = [], [], [], [], []
    for weight, moment, square, grads, rate, decay in groups:
        cut = split(weight.shape)
        ins += [weight, moment, square] + grads
        in_specs += [spec(weight.shape, cut)] * 3 + [spec(g.shape, cut) for g in grads]
        outs += [jax.ShapeDtypeStruct(weight.shape, f32)] * 3
        out_specs += [spec(weight.shape, cut)] * 3
        kinds.append((len(grads), rate, decay))

    wide_spec = pl.BlockSpec((widen.shape[0] // steps, widen.shape[1]), lambda i: (i, 0))
    outs += [jax.ShapeDtypeStruct(keep.shape, keep.dtype), jax.ShapeDtypeStruct(widen.shape, f32)]
    out_specs += [wide_spec] * 2

    def kernel(tot_r, wide_r, keep_r, *refs):
        out_refs = refs[len(ins) :]
        out_refs[-1][...] = wide_r[...].astype(f32)
        out_refs[-2][...] = keep_r[...]
        norm = jnp.sqrt(tot_r[:1, :1])
        factor = jnp.minimum(1.0, clip_limit / (norm + 1e-06))
        at = 0
        for n, (parts, rate, decay) in enumerate(kinds):
            w_r, m_r, s_r = refs[at : at + 3]
            g_rs = refs[at + 3 : at + 3 + parts]
            at += 3 + parts
            w_o, m_o, s_o = out_refs[3 * n : 3 * n + 3]

            def one(index, gradient):
                new = adam_update(
                    w_r[index], m_r[index], s_r[index], gradient, factor, rate, decay
                )
                w_o[index], m_o[index], s_o[index] = new

            if parts == 1 and g_rs[0].shape == w_r.shape:
                one(..., g_rs[0][...])
            elif parts == 1 and g_rs[0].ndim == 3:
                copies, _, wide = g_rs[0].shape
                hd = wide // 2
                heads = w_r.shape[2] // hd
                for h in range(heads):
                    v = None
                    for m in range(copies):
                        if m * heads // copies == h:
                            v = g_rs[0][m] if v is None else v + g_rs[0][m]
                    for i in range(2):
                        index = (i, slice(None), slice(h * hd, (h + 1) * hd))
                        one(index, v[:, i * hd : (i + 1) * hd])
            elif parts == 1:
                one(..., g_rs[0][: w_r.shape[0], :])
            else:
                for i in range(parts):
                    one(i, g_rs[i][...])

    return pl.pallas_call(
        kernel,
        name="update",
        grid=(steps,),
        out_shape=outs,
        in_specs=[pl.BlockSpec((8, 128), lambda i: (0, 0)), wide_spec, wide_spec] + in_specs,
        out_specs=out_specs,
        compiler_params=pltpu.CompilerParams(vmem_limit_bytes=61 * 2**20),
        cost_estimate=cost(3e7, 4e7),
    )(total, widen, keep, *ins)


def body(
    tokens,
    segment_ids,
    out_grad,
    query_weight,
    keyval_weight,
    output_weight,
    gateup_weight,
    down_weight,
    norm_gains,
    query_moment,
    keyval_moment,
    output_moment,
    gateup_moment,
    down_moment,
    gains_moment,
    query_square,
    keyval_square,
    output_square,
    gateup_square,
    down_square,
    gains_square,
):
    dp = lax.axis_size("dp")
    mp = lax.axis_size("mp")
    heads = H // mp
    rows = tokens.shape[0]
    blk = D // dp
    qcols = query_weight.shape[1]

    half = np.arange(HD // 2, dtype=np.float64) * 2.0 / HD
    rates = jnp.asarray(np.tile(rope_base**-half, 2)[None].astype(np.float32))
    segment = segment_ids.reshape(-1, 128)
    (
        wqkv, wo, gains, og, x_own, act_one, inv_one, q, k, v, attn, lse, gate_low, up_low, down_low,
        cosine, sine,
    ) = attention_call(
        tokens, out_grad, query_weight, keyval_weight, output_weight, norm_gains,
        gateup_weight, down_weight, segment, rates, heads, KV, dp, mp, 0, norm_eps,
    )
    gain_one, gain_two = gains[0:1], gains[1:2]
    wg, wu, wd, h_own, inv_two, act_two, hid, ga, ub = forward_call(
        attn, wo, x_own, gain_two, gate_low, up_low, down_low, dp, mp, 1, norm_eps
    )
    down_share, down_sq, gate_share, gate_sq, du, dh_own, dhb, gain_two_part = mlp_back_call(
        hid, og, act_two, ga, ub, wd, wg, wu, h_own, inv_two, gain_two, dp, mp, 2
    )
    (
        up_share, query_share, output_share, kv_parts, layer_out, in_low, gains_share, total
    ) = attention_back_call(
        act_two, du, hid, wd, dhb, wqkv, act_one, h_own, wo, q, k, v, lse, cosine, sine, segment,
        attn, x_own, inv_one, dh_own, gain_one, gain_two_part, [down_sq, gate_sq],
        heads, KV, dp, mp, 3,
    )
    grad_norm = jnp.sqrt(total[0, 0])
    output_rate = matrix_rate * (TOK_DEV * D / (16.0 * H * HD)) ** 0.5
    *news, layer_out, input_grad = update_call(
        total,
        in_low,
        layer_out,
        [
            (query_weight, query_moment, query_square, [query_share], matrix_rate, weight_decay),
            (keyval_weight, keyval_moment, keyval_square, [kv_parts], matrix_rate, weight_decay),
            (
                output_weight, output_moment, output_square, [output_share],
                output_rate, weight_decay,
            ),
            (
                gateup_weight, gateup_moment, gateup_square, [gate_share, up_share],
                matrix_rate, weight_decay,
            ),
            (down_weight, down_moment, down_square, [down_share], matrix_rate, weight_decay),
            (norm_gains, gains_moment, gains_square, [gains_share], gain_rate, 0.0),
        ],
    )
    return (layer_out, input_grad, grad_norm) + tuple(news[0::3] + news[1::3] + news[2::3])


def solution(mesh):
    params = (
        P("dp", "mp"),
        P(None, ("dp", "mp"), None),
        P("mp", "dp"),
        P(None, "dp", "mp"),
        P("mp", "dp"),
        P(None, "dp"),
    )
    rows = P("dp", None)
    return jax.shard_map(
        body,
        mesh=mesh,
        in_specs=(rows, P("dp"), rows) + params * 3,
        out_specs=(rows, rows, P()) + params * 3,
        check_vma=False,
    )
```

```python
import jax
import jax.numpy as jnp
import numpy as np
from jax import lax
from jax.experimental import pallas as pl
from jax.experimental.pallas import tpu as pltpu
from jax.sharding import PartitionSpec as P

MESH_ID = pl.DeviceIdType.MESH
low_type = jnp.bfloat16
f32 = jnp.float32
WINDOW = 32
HBM = pl.BlockSpec(memory_space=pl.ANY)
VM = pl.BlockSpec(memory_space=pltpu.VMEM)
DMA = pltpu.SemaphoreType.DMA
NT = (((1,), (1,)), ((), ()))
TN = (((0,), (0,)), ((), ()))


D = 2048
H = 16
KV = 4
HD = 128
TOK_DEV = 1024
ADAM_STEP = 10


norm_eps = 1e-05
rope_base = 10000.0
clip_limit = 1.0
beta_first = 0.9
beta_second = 0.95
adam_eps = 1e-08
weight_decay = 0.1
matrix_rate = 0.02
gain_rate = 0.6


def adam_update(weight, moment, square, gradient, factor, step_rate, decay_rate):
    clipped = gradient * factor
    moment_new = beta_first * moment + (1.0 - beta_first) * clipped
    square_new = beta_second * square + (1.0 - beta_second) * clipped * clipped
    first_fix = 1.0 - beta_first**ADAM_STEP
    second_fix = 1.0 - beta_second**ADAM_STEP
    step_dir = moment_new / first_fix / (jnp.sqrt(square_new / second_fix) + adam_eps)
    return (weight - step_rate * (step_dir + decay_rate * weight), moment_new, square_new)


def split_dp(count):
    lo = 1
    while lo * lo * 4 <= count:
        lo *= 2
    return count // lo, lo


class Place:
    def __init__(self, dp, mp):
        self.dp, self.mp = dp, mp
        self.hi, self.lo = split_dp(dp)
        self.mlo = 2 if mp % 2 == 0 else 1
        self.mhi = mp // self.mlo
        me = lax.axis_index("dp")
        self.h, self.l = me // self.lo, lax.rem(me, self.lo)
        self.m = lax.axis_index("mp")
        self.y, self.c = self.m // self.mlo, lax.rem(self.m, self.mlo)

    def z(self, k):
        return {"dp": lax.rem(self.h + (k + self.hi) % self.hi, self.hi) * self.lo + self.l}

    def x(self, j):
        return {"dp": self.h * self.lo + lax.rem(self.l + (j + self.lo) % self.lo, self.lo)}

    def part(self, k, i):
        return lax.rem(self.y + k, self.mhi) * self.mlo + lax.rem(self.c + i, self.mlo)

    def others_dp(self):
        out = []
        for j in range(self.lo):
            for k in range(self.hi):
                if j or k:
                    out.append((j * self.hi + k, self.owner(j, k)))
        return out

    def owner(self, j, k):
        return lax.rem(self.h + self.hi - k, self.hi) * self.lo + lax.rem(
            self.l + self.lo - j, self.lo
        )

    def others_mp(self):
        return [(s, lax.rem(self.m + s, self.mp)) for s in range(1, self.mp)]

    def barrier(self):
        bar = pltpu.get_barrier_semaphore()
        peers = [{"dp": d} for _, d in self.others_dp()] + [{"mp": m} for _, m in self.others_mp()]
        for p in peers:
            pl.semaphore_signal(bar, inc=1, device_id=p, device_id_type=MESH_ID)
        pl.semaphore_wait(bar, len(peers))


def remote(src, dst, send, recv, to):
    return pltpu.make_async_remote_copy(src, dst, send, recv, to, MESH_ID)


class Gather:
    def __init__(self, shapes, axes, splits, dp, late=()):
        self.hi, self.lo = split_dp(dp)
        self.shapes, self.axes, self.late = shapes, axes, late
        self.chunks = []
        for i, s in enumerate(shapes):
            step = s[0] // splits[i]
            self.chunks += [(i, n * step, step) for n in range(splits[i])]
        self.count = len(self.chunks)

    def out_shapes(self):
        n = self.hi * self.lo
        return [
            jax.ShapeDtypeStruct((s[0] * n, s[1]) if a == 0 else (s[0], s[1] * n), low_type)
            for s, a in zip(self.shapes, self.axes)
        ]

    def scratch(self):
        c, hi, lo = self.count, self.hi, self.lo
        return [
            DMA((c, hi - 1)),
            DMA((c, hi - 1)),
            DMA((c, hi, max(lo - 1, 1))),
            DMA((c, hi, max(lo - 1, 1))),
            DMA((c,)),
        ]

    def bind(self, place, ins, outs, sems):
        zs, zr, xs, xr, ls = sems
        hi, lo = self.hi, self.lo

        def dst(c, r):
            i, at, step = self.chunks[c]
            rows, cols = self.shapes[i]
            if self.axes[i] == 0:
                return outs[i].at[pl.ds(r * rows + at, step)]
            return outs[i].at[pl.ds(at, step), pl.ds(r * cols, cols)]

        def src(c):
            i, at, step = self.chunks[c]
            return ins[i].at[pl.ds(at, step)]

        self.zc = {
            (c, k): remote(src(c), dst(c, k), zs.at[c, k - 1], zr.at[c, k - 1], place.z(k))
            for c in range(self.count)
            for k in range(1, hi)
        }
        self.xc = {
            (c, k, j): remote(
                src(c) if k == 0 else dst(c, k),
                dst(c, j * hi + k),
                xs.at[c, k, j - 1],
                xr.at[c, k, j - 1],
                place.x(j),
            )
            for c in range(self.count)
            for k in range(hi)
            for j in range(1, lo)
        }
        self.lc = [pltpu.make_async_copy(src(c), dst(c, 0), ls.at[c]) for c in range(self.count)]
        self.items = []
        self.started = 0
        self.window = 2
        for c in range(self.count):
            for k in range(1, hi):
                self.items.append((c, k))
        self.arrived = [False] * self.count

    def start_own(self, c):
        for j in range(1, self.lo):
            self.xc[c, 0, j].start()
        self.lc[c].start()

    def start_z(self, c):
        if c in self.late:
            self.late[c]()
            self.start_own(c)
        for k in range(1, self.hi):
            self.zc[c, k].start()

    def begin(self):
        for c in range(self.count):
            if c < self.window:
                self.start_z(c)
            if c not in self.late:
                self.start_own(c)
        self.started = min(self.window, self.count)

    def step(self, n=1):
        for _ in range(n):
            if not self.items:
                return
            c, k = self.items.pop(0)
            self.zc[c, k].wait_recv()
            for j in range(1, self.lo):
                self.xc[c, k, j].start()
            if k == self.hi - 1 and self.started < self.count:
                self.start_z(self.started)
                self.started += 1

    def arrive(self, c):
        if self.arrived[c]:
            return
        while any(i[0] <= c for i in self.items):
            self.step()
        self.lc[c].wait()
        for k in range(self.hi):
            for j in range(1, self.lo):
                self.xc[c, k, j].wait_recv()
        self.arrived[c] = True

    def finish(self):
        for c in range(self.count):
            self.arrive(c)
        for c in range(self.count):
            for k in range(1, self.hi):
                self.zc[c, k].wait_send()
            for k in range(self.hi):
                for j in range(1, self.lo):
                    self.xc[c, k, j].wait_send()


class LineGather(Gather):
    def __init__(self, shapes, splits, dp, first):
        super().__init__(shapes, (0,) * len(shapes), splits, dp)
        self.first = first

    def scratch(self):
        c, hi, lo = self.count, self.hi, self.lo
        return [
            DMA((c, lo, hi)),
            DMA((c, lo, hi)),
            DMA((c, lo, hi)),
            DMA((c, hi)),
            DMA((c, hi)),
            DMA((c,)),
        ]

    def bind(self, place, ins, outs, sems):
        us, ds, zr, xs, xr, ls = sems
        hi, lo = self.hi, self.lo
        self.h = place.h

        def slot(c, j, k):
            i, at, step = self.chunks[c]
            r = j * hi + k
            return outs[i].at[pl.ds(r * self.shapes[i][0] + at, step)]

        def src(c, j, k):
            i, at, step = self.chunks[c]
            return slot(c, j, k) if j or k else ins[i].at[pl.ds(at, step)]

        self.rows_of = [range(lo) if c in self.first else range(1) for c in range(self.count)]
        each = [(c, j, k) for c in range(self.count) for j in self.rows_of[c] for k in range(hi)]
        self.up = {
            (c, j, k): remote(
                src(c, j, k), slot(c, j, k + 1), us.at[c, j, k], zr.at[c, j, k + 1], place.z(1)
            )
            for c, j, k in each
            if k < hi - 1
        }
        self.down = {
            (c, j, k): remote(
                src(c, j, k),
                slot(c, j, (k - 1) % hi),
                ds.at[c, j, k],
                zr.at[c, j, (k - 1) % hi],
                place.z(-1),
            )
            for c, j, k in each
            if k != 1
        }
        self.into = {
            (c, j, k): remote(
                slot(c, j, k), slot(c, j, k), us.at[c, j, k - 1], zr.at[c, j, k], place.z(1)
            )
            for c, j, k in each
            if k
        }
        self.xc = {
            (c, k): remote(src(c, 0, k), slot(c, 1, k), xs.at[c, k], xr.at[c, k], place.x(1))
            for c in range(self.count)
            for k in range(1 if c in self.first else hi)
        }
        self.lc = [
            pltpu.make_async_copy(src(c, 0, 0), slot(c, 0, 0), ls.at[c]) for c in range(self.count)
        ]
        self.items = [
            (c, j, k) for c in range(self.count) for j in self.rows_of[c] for k in (1, 3, 2)
        ]
        self.window = 3
        self.arrived = [False] * self.count

    def passes(self, k):
        h, hi = self.h, self.hi
        if k == 0:
            return h < hi - 1, h > 0
        return (h >= k) & (h < hi - 1), (h < k) & (h > 0)

    def pass_on(self, key, act):
        c, j, k = key
        up, down = self.passes(k)
        if key in self.up:

            @pl.when(up)
            def _():
                act(self.up[key])

        if key in self.down:

            @pl.when(down)
            def _():
                act(self.down[key])

    def start_z(self, c):
        for j in self.rows_of[c]:
            if j:
                self.xc[c, 0].wait_recv()
            self.pass_on((c, j, 0), lambda copy: copy.start())

    def begin(self):
        for c in range(self.count):
            if c < self.window:
                self.start_z(c)
            self.xc[c, 0].start()
            self.lc[c].start()
        self.started = min(self.window, self.count)

    def step(self, n=1):
        for _ in range(n):
            if not self.items:
                return
            c, j, k = self.items.pop(0)
            self.into[c, j, k].wait_recv()
            self.pass_on((c, j, k), lambda copy: copy.start())
            if (c, k) in self.xc:
                self.xc[c, k].start()
            if (j, k) == (self.rows_of[c][-1], 2) and self.started < self.count:
                self.start_z(self.started)
                self.started += 1

    def arrive(self, c):
        if self.arrived[c]:
            return
        while any(i[0] <= c for i in self.items):
            self.step()
        self.lc[c].wait()
        for k in range(self.hi):
            if (c, k) in self.xc and c not in self.first:
                self.xc[c, k].wait_recv()
        self.arrived[c] = True

    def finish(self):
        for c in range(self.count):
            self.arrive(c)
        for c in range(self.count):
            for j in self.rows_of[c]:
                for k in range(self.hi):
                    self.pass_on((c, j, k), lambda copy: copy.wait_send())
        for copy in self.xc.values():
            copy.wait_send()


class RowSum:
    def __init__(self, rows, width, mp):
        self.mlo = 2 if mp % 2 == 0 else 1
        self.mhi = mp // self.mlo
        self.share, self.width = rows // mp, width
        self.tile = min(512, width)
        self.tiles = width // self.tile

    def scratch(self):
        h, t = self.mhi, self.tiles
        g = max(h - 1, 1)
        return [
            pltpu.VMEM((h, self.share, self.width), low_type),
            pltpu.VMEM((h, self.share, self.width), low_type),
            pltpu.VMEM((g, self.share, self.width), low_type),
            pltpu.VMEM((g, self.share, self.width), low_type),
            pltpu.VMEM((self.share, self.width), f32),
            DMA((h, t)),
            DMA((h, t)),
            DMA((g, t)),
            DMA((g, t)),
        ]

    def bind(self, place, refs):
        self.place = place
        (self.cs, self.cr, self.ys, self.yr, self.acc) = refs[:5]
        css, crs, yss, yrs = refs[5:]
        h = self.mhi

        def sl(ref, k, t):
            return ref.at[k, :, pl.ds(t * self.tile, self.tile)]

        other = {"mp": place.part(0, 1)}
        self.cc = {
            (k, t): remote(sl(self.cs, k, t), sl(self.cr, k, t), css.at[k, t], crs.at[k, t], other)
            for k in range(h)
            for t in range(self.tiles)
        }
        self.yc = {
            (k, t): remote(
                sl(self.ys, k - 1, t),
                sl(self.yr, k - 1, t),
                yss.at[k - 1, t],
                yrs.at[k - 1, t],
                {"mp": place.part(k, 0)},
            )
            for k in range(1, h)
            for t in range(self.tiles)
        }

    def start_of(self, k, i):
        return pl.multiple_of(self.place.part(k, i) * self.share, 8)

    def scatter(self, partial, before=lambda t: None, between=lambda: None):
        order = list(range(1, self.mhi)) + [0]
        for t in range(self.tiles):
            before(t)
            cols = pl.ds(t * self.tile, self.tile)
            if self.mlo > 1:
                for k in order:
                    v = partial(self.start_of(k, 1), self.share, t, self.tile)
                    self.cs[k, :, cols] = v.astype(low_type)
                    self.cc[k, t].start()
            for k in order:
                v = partial(self.start_of(k, 0), self.share, t, self.tile)
                if self.mlo > 1:
                    self.cc[k, t].wait_recv()
                    v += self.cr[k, :, cols].astype(f32)
                if k:
                    self.ys[k - 1, :, cols] = v.astype(low_type)
                    self.yc[k, t].start()
                else:
                    self.acc[:, cols] = v
            between()

    def arrive(self):
        for t in range(self.tiles):
            for k in range(1, self.mhi):
                self.yc[k, t].wait_recv()

        def read(at, count):
            v = self.acc[pl.ds(at, count), :]
            for k in range(1, self.mhi):
                v += self.yr[k - 1, pl.ds(at, count), :].astype(f32)
            return v

        return read

    def finish(self):
        for t in range(self.tiles):
            if self.mlo > 1:
                for k in range(self.mhi):
                    self.cc[k, t].wait_send()
            for k in range(1, self.mhi):
                self.yc[k, t].wait_send()

    def free(self, credit):
        for k in range(1, self.mhi):
            to = {"mp": self.place.part(k, 0)}
            pl.semaphore_signal(credit, inc=1, device_id=to, device_id_type=MESH_ID)
        for i in range(1, self.mlo):
            to = {"mp": self.place.part(0, i)}
            pl.semaphore_signal(credit, inc=1, device_id=to, device_id_type=MESH_ID)

    def freed(self, credit):
        pl.semaphore_wait(credit, self.mhi - 1 + self.mlo - 1)


class Spread:
    def __init__(self, rows, mp, parts):
        self.mlo = 2 if mp % 2 == 0 else 1
        self.mhi = mp // self.mlo
        self.share, self.parts = rows // mp, parts
        self.step = self.share // parts

    def scratch(self):
        h, p = self.mhi, self.parts
        g = max(h - 1, 1)
        return [DMA((g, p)), DMA((g, p)), DMA((h, p)), DMA((h, p))]

    def bind(self, place, refs, full, own=None):
        gys, gyr, gcs, gcr = refs
        h, p = self.mhi, self.parts
        other = {"mp": place.part(0, 1)}

        def rows_at(m, r):
            return full.at[pl.ds(pl.multiple_of(m * self.share + r * self.step, 8), self.step), :]

        def mine(r):
            if own is None:
                return rows_at(place.m, r)
            return own.at[pl.ds(r * self.step, self.step), :]

        self.gy = {
            (k, r): remote(
                mine(r),
                rows_at(place.m, r),
                gys.at[k - 1, r],
                gyr.at[k - 1, r],
                {"mp": place.part(k, 0)},
            )
            for k in range(1, h)
            for r in range(p)
        }
        self.gc = {
            (k, r): remote(
                rows_at(place.part((h - k) % h, 0), r) if k else mine(r),
                rows_at(place.part((h - k) % h, 0), r),
                gcs.at[k, r],
                gcr.at[k, r],
                other,
            )
            for k in range(h)
            for r in range(p)
        }

    def send(self, r):
        for k in range(1, self.mhi):
            self.gy[k, r].start()
        if self.mlo > 1:
            self.gc[0, r].start()

    def forward(self, r):
        for k in range(1, self.mhi):
            self.gy[k, r].wait_recv()
            if self.mlo > 1:
                self.gc[k, r].start()

    def finish(self):
        for r in range(self.parts):
            if self.mlo > 1:
                for k in range(self.mhi):
                    self.gc[k, r].wait()
            for k in range(1, self.mhi):
                self.gy[k, r].wait_send()


def sequence_length(seg, rows):
    top = jnp.max(jnp.max(seg, axis=1, keepdims=True), axis=0, keepdims=True)
    return jnp.where(top == 0, rows, jnp.where(top == 1, rows // 2, rows // 4))


def attention_bias(length, start, count, keys):
    row = start + lax.broadcasted_iota(jnp.int32, (count, 1), 0)
    first = row - (row & (length - 1))
    col = lax.broadcasted_iota(jnp.int32, (count, keys), 1)
    return jnp.where((col <= row) & (col >= first), 0.0, -1e30)


def small_rows(total, step, fn):
    @pl.loop(0, total // step)
    def _(t):
        fn(pl.multiple_of(t * step, step))


def forward_call(attn, wo, x_own, gain, gate, up, down, dp, mp, cid, eps):
    rows, width = attn.shape[0], x_own.shape[1]
    ff = gate.shape[1]
    shapes = [gate.shape, up.shape, down.shape]
    if split_dp(dp) == (4, 2):
        gather = LineGather(shapes, (2, 2, 2), dp, (5,))
    else:
        gather = Gather(shapes, (0, 0, 0), (2, 2, 2), dp)
    rsum, spread = RowSum(rows, width, mp), Spread(rows, mp, 2)
    share = rsum.share
    n_g, n_r = len(gather.scratch()), len(rsum.scratch())
    tile = 128

    def kernel(attn_r, wo_r, x_r, gains_r, gate_r, up_r, down_r, *refs):
        gain_r = gains_r.at[pl.ds(1, 1), :]
        wg_o, wu_o, wd_o, h_o, inv_o, act_o = refs[:6]
        saved = refs[6:9]
        hid_v, ga_v, ub_v, wg_v, wu_v, wsem, ssem = refs[9:16]
        g_s = refs[16 : 16 + n_g]
        r_s = refs[16 + n_g : 16 + n_g + n_r]
        place = Place(dp, mp)
        place.barrier()
        gather.bind(place, (gate_r, up_r, down_r), (wg_o, wu_o, wd_o), g_s)
        rsum.bind(place, r_s)
        spread.bind(place, refs[16 + n_g + n_r :], act_o)
        gather.begin()

        def partial(start, count, t, n):
            return jnp.dot(
                attn_r[pl.ds(start, count), :],
                wo_r[:, pl.ds(t * n, n)],
                preferred_element_type=f32,
            )

        rsum.scatter(partial)
        gather.step(2)
        read = rsum.arrive()
        for r in range(spread.parts):
            base = r * spread.step
            own = place.m * share

            def norm(at):
                v = x_r[pl.ds(base + at, 32), :].astype(f32) + read(base + at, 32)
                h_o[pl.ds(base + at, 32), :] = v
                inv = lax.rsqrt(jnp.mean(v * v, axis=-1, keepdims=True) + eps)
                inv_o[pl.ds(base + at, 32), :] = jnp.broadcast_to(inv, (32, 128))
                act_o[pl.ds(pl.multiple_of(own + base + at, 32), 32), :] = (
                    v * inv * gain_r[...]
                ).astype(low_type)

            small_rows(spread.step, 32, norm)
            spread.send(r)
            gather.step(1)
        for r in range(spread.parts):
            spread.forward(r)
            gather.step(1)
        spread.finish()
        rsum.finish()
        for c in range(2):
            gather.arrive(c)
        cg = pltpu.make_async_copy(wg_o, wg_v, wsem.at[0])
        cg.start()
        for c in range(2, 4):
            gather.arrive(c)
        cu = pltpu.make_async_copy(wu_o, wu_v, wsem.at[1])
        cu.start()
        cg.wait()
        cu.wait()
        groups = 4
        per = rows // tile // groups
        stores = []
        for q in range(groups):

            @pl.loop(q * per, (q + 1) * per)
            def _(t):
                rs = pl.ds(pl.multiple_of(t * tile, tile), tile)
                a = act_o[rs, :]
                gp = jnp.dot(a, wg_v[...], preferred_element_type=f32)
                upv = jnp.dot(a, wu_v[...], preferred_element_type=f32)
                sg = jax.nn.sigmoid(gp)
                sw = gp * sg
                hid_v[rs, :] = (sw * upv).astype(low_type)
                ga_v[rs, :] = (upv * sg * (1.0 + gp * (1.0 - sg))).astype(low_type)
                ub_v[rs, :] = sw.astype(low_type)

            rs = pl.ds(q * per * tile, per * tile)
            for n, (v, o) in enumerate(zip((hid_v, ga_v, ub_v), saved)):
                c = pltpu.make_async_copy(v.at[rs, :], o.at[rs, :], ssem.at[q, n])
                c.start()
                stores.append(c)
            gather.step(3)
        gather.finish()
        for c in stores:
            c.wait()

    sds = jax.ShapeDtypeStruct
    act_shape = sds((rows, ff), low_type)
    return pl.pallas_call(
        kernel,
        name="forward_mlp",
        out_shape=gather.out_shapes()
        + [
            sds((share, width), f32),
            sds((share, 128), f32),
            sds((rows, width), low_type),
            act_shape,
            act_shape,
            act_shape,
        ],
        in_specs=[VM] * 4 + [HBM] * 3,
        out_specs=[HBM] * 3 + [VM] * 3 + [HBM] * 3,
        scratch_shapes=[pltpu.VMEM((rows, ff), low_type)] * 3
        + [
            pltpu.VMEM((width, ff), low_type),
            pltpu.VMEM((width, ff), low_type),
            DMA((2,)),
            DMA((4, 3)),
        ]
        + gather.scratch()
        + rsum.scratch()
        + spread.scratch(),
        compiler_params=big(cid),
        cost_estimate=cost(2e10, 1e8),
    )(attn, wo, x_own, gain, gate, up, down)


def fold_order(hi):
    return sorted(range(1, hi), key=lambda k: -min(k, hi - k)) + [0]


class Fold:
    def __init__(self, rows, cols, dp, sub):
        self.hi, self.lo = split_dp(dp)
        self.rows, self.cols, self.sub = rows, cols, sub
        self.step = rows // sub
        self.order = fold_order(self.hi)

    def scratch(self):
        hi, lo, s = self.hi, self.lo, self.sub
        j = max(lo - 1, 1)
        return [
            pltpu.VMEM((lo * hi, self.rows, self.cols), low_type),
            pltpu.VMEM((j * hi, self.rows, self.cols), low_type),
            pltpu.VMEM((hi - 1, self.rows, self.cols), low_type),
            DMA((j, hi, s)),
            DMA((j, hi, s)),
            DMA((hi - 1, s)),
            DMA((hi - 1, s)),
        ]

    def out_shapes(self):
        return [
            jax.ShapeDtypeStruct((self.rows, self.cols), f32),
            jax.ShapeDtypeStruct((8, self.cols), f32),
        ]

    def bind(self, place, refs):
        self.g, self.xb, self.zb, xs, xr, zs, zr = refs
        hi, lo = self.hi, self.lo

        def part(s):
            return pl.ds(s * self.step, self.step)

        self.part = part
        self.xc = {
            (k, j, s): remote(
                self.g.at[j * hi + k, part(s), :],
                self.xb.at[(j - 1) * hi + k, part(s), :],
                xs.at[j - 1, k, s],
                xr.at[j - 1, k, s],
                place.x(-j),
            )
            for k in range(hi)
            for j in range(1, lo)
            for s in range(self.sub)
        }
        self.zc = {
            (k, s): remote(
                self.g.at[k, part(s), :],
                self.zb.at[k - 1, part(s), :],
                zs.at[k - 1, s],
                zr.at[k - 1, s],
                place.z(-k),
            )
            for k in range(1, hi)
            for s in range(self.sub)
        }
        self.items = [(k, s) for k in self.order for s in range(self.sub)]
        self.blocks = [(j, k) for j in range(1, lo) for k in self.order]
        self.blocks += [(0, k) for k in self.order]
        self.small = next(n for n in (64, 32, 16, 8) if self.step % n == 0)

    def tiles(self, s, fn):
        @pl.loop(0, self.step // self.small)
        def _(t):
            fn(pl.ds(pl.multiple_of(s * self.step + t * self.small, self.small), self.small))

    def send_x(self, k, s):
        for j in range(1, self.lo):
            self.xc[k, j, s].start()

    def add_and_send(self, k, s):
        for j in range(1, self.lo):
            self.xc[k, j, s].wait_recv()
        if k:

            def add(rs):
                v = self.g[k, rs, :].astype(f32)
                for j in range(1, self.lo):
                    v += self.xb[(j - 1) * self.hi + k, rs, :].astype(f32)
                self.g[k, rs, :] = v.astype(low_type)

            self.tiles(s, add)
            self.zc[k, s].start()

    def finish(self, out, squares):
        squares[...] = jnp.zeros_like(squares)
        for s in range(self.sub):
            for k in range(1, self.hi):
                self.zc[k, s].wait_recv()

            def add(rs):
                v = self.g[0, rs, :].astype(f32)
                for j in range(1, self.lo):
                    v += self.xb[(j - 1) * self.hi, rs, :].astype(f32)
                for k in range(1, self.hi):
                    v += self.zb[k - 1, rs, :].astype(f32)
                out[rs, :] = v
                squares[...] += jnp.sum((v * v).reshape(self.small // 8, 8, self.cols), axis=0)

            self.tiles(s, add)
        for c in self.xc.values():
            c.wait_send()
        for c in self.zc.values():
            c.wait_send()


class FoldQueue:
    def __init__(self, folds, window=WINDOW):
        self.order = [(f, k, s) for f in folds for k, s in f.items]
        self.have = set()
        self.window, self.started, self.done = window, 0, 0

    def ready(self, fold, j, k):
        self.have.add((id(fold), j, k))
        self.pump()

    def pump(self):
        while self.started < min(len(self.order), self.done + self.window):
            f, k, s = self.order[self.started]
            if any((id(f), j, k) not in self.have for j in range(1, f.lo)):
                return
            f.send_x(k, s)
            self.started += 1

    def advance(self, n=1):
        for _ in range(n):
            if self.done == self.started:
                return
            f, k, s = self.order[self.done]
            if (id(f), 0, k) not in self.have:
                return
            f.add_and_send(k, s)
            self.done += 1
            self.pump()

    def finish(self):
        self.advance(len(self.order))
        assert self.done == len(self.order)


def big(cid, remote_kernel=True):
    extra = {"collective_id": cid, "has_side_effects": True} if remote_kernel else {}
    return pltpu.CompilerParams(vmem_limit_bytes=62 * 2**20, **extra)


def cost(flops, bytes_accessed):
    return pl.CostEstimate(
        flops=int(flops), bytes_accessed=int(bytes_accessed), transcendentals=10**6
    )


def attention_call(
    tokens, out_grad, wq, wkv, wo, gains, gateup, down, segment, rates,
    heads, kv_heads, dp, mp, cid, eps
):
    rows, width = tokens.shape
    hd = rates.shape[1]
    blk, qcols = wq.shape
    kv_rows = wkv.shape[1]
    ff = down.shape[0]
    block = min(256, rows)
    scale = hd**-0.5
    share = rows // mp
    cols = qcols + 2 * hd
    late = {}
    gather = Gather(
        [(16, blk), wq.shape, (blk, 2 * hd), wo.shape], (0, 0, 0, 1), (1, 2, 1, 2), dp, late
    )
    n_g = len(gather.scratch())

    def kernel(tok_r, og_r, q_f, kv_f, wo_f, gn_f, gu_h, dn_h, sg_r, rt_r, *refs):
        (wqkv_o, wo_o, gain_o, og_h, x_o, a_h, inv_o, qo, ko, vo, ob_o, lse_o, gl_h, ul_h, dl_h) = (
            refs[:15]
        )
        c_r, s_r = refs[15:17]
        kvx, gall, xv, wv, bias, q_r, kv_r, wo_r, gn_r, ks, kr, cs_, ws = refs[17:30]
        og_o, a_o, gl_o, ul_o, dl_o, gu_r, dn_r, io = refs[30:38]
        g_s = refs[38:]
        loads = [
            pltpu.make_async_copy(gu_h, gu_r, io.at[0]),
            pltpu.make_async_copy(dn_h, dn_r, io.at[1]),
        ]
        for c in loads:
            c.start()
        stores = []

        def store(src, dst):
            c = pltpu.make_async_copy(src, dst, io.at[2 + len(stores)])
            c.start()
            stores.append(c)

        place = Place(dp, mp)
        copies = []
        for j in range(place.lo):
            for k in range(place.hi):
                r = j * place.hi + k
                at = pl.ds(pl.multiple_of(place.owner(j, k) * blk, 128), blk)
                to = pl.ds(r * blk, blk)
                copies.append(pltpu.make_async_copy(tok_r.at[:, at], xv.at[:, to], cs_.at[0, r]))
                copies.append(
                    pltpu.make_async_copy(og_r.at[:, at], og_o.at[:, to], cs_.at[1, r])
                )
        for c in copies:
            c.start()
        gn_r[...] = jnp.zeros_like(gn_r)
        gn_r[:2, :] = gn_f[...].astype(low_type)
        q_r[...] = q_f[...].astype(low_type)
        for n in range(kv_heads):
            for i in range(2):
                kv_r[:, (2 * n + i) * hd : (2 * n + i + 1) * hd] = kv_f[
                    i, :, n * hd : (n + 1) * hd
                ].astype(low_type)
        wo_r[...] = wo_f[...].astype(low_type)
        place.barrier()
        here = pl.ds(pl.multiple_of(place.m * kv_rows, kv_rows), kv_rows)
        swaps = []
        for n, m in place.others_mp():
            head = m * kv_heads // mp
            c = remote(
                kv_r.at[:, pl.ds(pl.multiple_of(head * 2 * hd, 128), 2 * hd)],
                kvx.at[here],
                ks.at[n],
                kr.at[n],
                {"mp": m},
            )
            c.start()
            swaps.append(c)
        head = place.m * kv_heads // mp
        mine = pltpu.make_async_copy(
            kv_r.at[:, pl.ds(pl.multiple_of(head * 2 * hd, 128), 2 * hd)], kvx.at[here], ks.at[0]
        )
        mine.start()

        def swapped():
            mine.wait()
            for c in swaps:
                c.wait_recv()

        late[3] = swapped
        late[4] = late[5] = lambda: None
        gather.bind(
            place,
            (gn_r, q_r, kvx, wo_r),
            (gall, wqkv_o.at[:, pl.ds(0, qcols)], wqkv_o.at[:, pl.ds(qcols, 2 * hd)], wo_o),
            g_s,
        )
        gather.begin()
        for c in loads:
            c.wait()

        @pl.loop(0, blk // 32)
        def _(t):
            rs = pl.ds(pl.multiple_of(t * 32, 32), 32)
            gl_o[rs, :] = gu_r[0, rs, :].astype(low_type)
            ul_o[rs, :] = gu_r[1, rs, :].astype(low_type)

        dl_o[...] = dn_r[...].T.astype(low_type)
        store(gl_o, gl_h)
        store(ul_o, ul_h)
        store(dl_o, dl_h)
        gather.step(2 * (gather.hi - 1))
        length = sequence_length(sg_r[...], rows)

        @pl.loop(0, rows // 128)
        def _(t):
            at = pl.multiple_of(t * 128, 128)
            row = at + lax.broadcasted_iota(jnp.int32, (128, 1), 0)
            angle = (row & (length - 1)).astype(f32) * rt_r[...]
            lane = lax.broadcasted_iota(jnp.int32, (128, hd), 1)
            c_r[pl.ds(at, 128), :] = jnp.cos(angle)
            sn = jnp.sin(angle)
            s_r[pl.ds(at, 128), :] = jnp.where(lane < hd // 2, -sn, sn)

        for c in copies:
            c.wait()
        store(og_o, og_h)
        own = place.m * share

        @pl.loop(0, share // 32)
        def _(t):
            at = pl.multiple_of(t * 32, 32)
            v = xv[pl.ds(pl.multiple_of(own + at, 32), 32), :]
            x_o[pl.ds(at, 32), :] = v
            v = v.astype(f32)
            inv = lax.rsqrt(jnp.mean(v * v, axis=-1, keepdims=True) + eps)
            inv_o[pl.ds(at, 32), :] = jnp.broadcast_to(inv, (32, 128))

        gather.arrive(0)
        for c in (1, 2, 3):
            gather.arrive(c)
        wcopy = pltpu.make_async_copy(wqkv_o, wv, ws.at[0])
        wcopy.start()
        for r in range(dp):
            at = r * 16
            gain_o[:, r * blk : (r + 1) * blk] = gall[at : at + 8, :].astype(f32)
        wcopy.wait()
        gain = gain_o[:1, :]
        half = rows // 128 // 2
        for q in range(2):

            @pl.loop(q * half, (q + 1) * half)
            def _(t):
                rs = pl.ds(pl.multiple_of(t * 128, 128), 128)
                v = xv[rs, :].astype(f32)
                inv = lax.rsqrt(jnp.mean(v * v, axis=-1, keepdims=True) + eps)
                a = (v * inv * gain).astype(low_type)
                a_o[rs, :] = a
                raw = jnp.dot(a, wv[...], preferred_element_type=f32)
                cs, sn = c_r[rs, :], s_r[rs, :]
                for n in range(heads):
                    u = raw[:, n * hd : (n + 1) * hd]
                    qo[rs, n * hd : (n + 1) * hd] = (
                        u * cs + pltpu.roll(u, hd // 2, 1) * sn
                    ).astype(low_type)
                u = raw[:, qcols : qcols + hd]
                ko[rs, :] = (u * cs + pltpu.roll(u, hd // 2, 1) * sn).astype(low_type)
                vo[rs, :] = raw[:, qcols + hd :].astype(low_type)

            done = pl.ds(q * half * 128, half * 128)
            store(a_o.at[done, :], a_h.at[done, :])
            gather.step(1)

        for q in range(rows // block):
            rs = pl.ds(q * block, block)
            keys = (q + 1) * block
            bias[:, :keys] = attention_bias(length, q * block, block, keys)
            lane = lax.broadcasted_iota(jnp.int32, (block, 128), 1)
            lse = jnp.zeros((block, 128), f32)
            for n in range(heads):
                hs = slice(n * hd, (n + 1) * hd)
                s = lax.dot_general(qo[rs, hs], ko[:keys, :], NT, preferred_element_type=f32)
                s = s * scale + bias[:, :keys]
                top = jnp.max(s, axis=-1, keepdims=True)
                e = jnp.exp(s - top)
                total = jnp.sum(e, axis=-1, keepdims=True)
                p = (e * (1.0 / total)).astype(low_type)
                ob_o[rs, hs] = jnp.dot(p, vo[:keys, :], preferred_element_type=f32).astype(
                    low_type
                )
                lse = jnp.where(lane == n, top + jnp.log(total), lse)
            lse_o[rs, :] = lse
            gather.step(1)
        gather.finish()
        for c in swaps:
            c.wait_send()
        for c in stores:
            c.wait()

    sds = jax.ShapeDtypeStruct
    return pl.pallas_call(
        kernel,
        name="attention_forward",
        out_shape=[
            sds((width, cols), low_type),
            sds((qcols, width), low_type),
            sds((8, width), f32),
            sds((rows, width), low_type),
            sds((share, width), low_type),
            sds((rows, width), low_type),
            sds((share, 128), f32),
            sds((rows, qcols), low_type),
            sds((rows, hd), low_type),
            sds((rows, hd), low_type),
            sds((rows, qcols), low_type),
            sds((rows, 128), f32),
            sds((blk, ff), low_type),
            sds((blk, ff), low_type),
            sds((blk, ff), low_type),
            sds((rows, hd), f32),
            sds((rows, hd), f32),
        ],
        in_specs=[HBM] * 2 + [VM] * 4 + [HBM] * 2 + [VM] * 2,
        out_specs=[HBM, HBM, VM, HBM, VM, HBM] + [VM] * 6 + [HBM] * 3 + [VM] * 2,
        scratch_shapes=[
            pltpu.VMEM((blk, 2 * hd), low_type),
            pltpu.VMEM((16 * dp, blk), low_type),
            pltpu.VMEM((rows, width), low_type),
            pltpu.VMEM((width, cols), low_type),
            pltpu.VMEM((block, rows), f32),
            pltpu.VMEM((blk, qcols), low_type),
            pltpu.VMEM((kv_rows, kv_heads * 2 * hd), low_type),
            pltpu.VMEM(wo.shape, low_type),
            pltpu.VMEM((16, blk), low_type),
            DMA((mp,)),
            DMA((mp,)),
            DMA((2, dp)),
            DMA((1,)),
            pltpu.VMEM((rows, width), low_type),
            pltpu.VMEM((rows, width), low_type),
            pltpu.VMEM((blk, ff), low_type),
            pltpu.VMEM((blk, ff), low_type),
            pltpu.VMEM((blk, ff), low_type),
            pltpu.VMEM(gateup.shape, f32),
            pltpu.VMEM(down.shape, f32),
            DMA((8,)),
        ]
        + gather.scratch(),
        compiler_params=big(cid),
        cost_estimate=cost(6e9, 2e7),
    )(tokens, out_grad, wq, wkv, wo, gains, gateup, down, segment, rates)


def put_natural(place, ref, rows, value, blk):
    for j in range(place.lo):
        for k in range(place.hi):
            owner = place.owner(j, k)
            r = j * place.hi + k
            ref[rows, pl.ds(pl.multiple_of(owner * blk, 128), blk)] = value[
                :, r * blk : (r + 1) * blk
            ]


def mlp_back_call(hid, og, act, ga, ub, wd, wg, wu, h_own, inv_own, gain, dp, mp, cid):
    rows, ff = hid.shape
    width = og.shape[1]
    blk = width // dp
    folds = [Fold(blk, ff, dp, 2), Fold(blk, ff, dp, 2)]
    rsum, spread = RowSum(rows, width, mp), Spread(rows, mp, 2)
    share, tile = rsum.share, rsum.tile
    n_f, n_r = len(folds[0].scratch()), len(rsum.scratch())

    def kernel(
        hid_r, og_r, act_r, ga_r, ub_r, wd_r, wg_r, wu_r, h_r, inv_r, gn_r, *refs
    ):
        g_r = gn_r.at[pl.ds(1, 1), :]
        (down_o, dsq_o, gate_o, gsq_o, du_o, dh_h, dhb_h, gg_o) = refs[:8]
        pb, ogx, dg, du, wbuf, dh_o, dhb_o, ls, ws, wd_s = refs[8:18]
        at = 18
        for f in folds:
            f_refs = refs[at : at + n_f]
            at += n_f
            f.refs = f_refs
        r_s = refs[at : at + n_r]
        p_s = refs[at + n_r :]
        place = Place(dp, mp)
        own = pl.multiple_of(place.m * share, 8)
        load_og = pltpu.make_async_copy(og_r, pb, ls.at[0])
        load_hid = pltpu.make_async_copy(hid_r, dg, ls.at[1])
        load_ub = pltpu.make_async_copy(ub_r, du, ls.at[2])
        load_own = pltpu.make_async_copy(og_r.at[pl.ds(own, share), :], ogx, ls.at[3])
        load_ga = pltpu.make_async_copy(ga_r, dg, ls.at[4])
        load_act = pltpu.make_async_copy(act_r, pb, ls.at[5])
        store_du = pltpu.make_async_copy(du, du_o, ls.at[6])
        tiles = rsum.tiles
        load_wd = [
            pltpu.make_async_copy(
                wd_r.at[pl.ds(t * tile, tile), :], wbuf.at[t // 2, t % 2], wd_s.at[t]
            )
            for t in range(tiles)
        ]

        def fetch(t):
            rs = pl.ds(t * tile, tile)
            return [
                pltpu.make_async_copy(w.at[rs, :], wbuf.at[t % 2, i], ws.at[t, i])
                for i, w in enumerate((wg_r, wu_r))
            ]

        for c in [load_og, load_hid, load_ub, load_own] + load_wd:
            c.start()
        place.barrier()
        for f in folds:
            f.bind(place, f.refs)
        rsum.bind(place, r_s)
        spread.bind(place, p_s, dhb_o)
        load_og.wait()
        load_hid.wait()
        first, second = folds
        queue = FoldQueue(folds)
        for j, k in first.blocks:
            r = j * first.hi + k
            first.g[r] = jnp.dot(
                pb[:, r * blk : (r + 1) * blk].T, dg[...], preferred_element_type=f32
            ).astype(low_type)
            queue.ready(first, j, k)
        load_ga.start()
        for c in load_wd + [load_ub, load_ga]:
            c.wait()
        groups = 4
        per = rows // 128 // groups
        for q in range(groups):

            @pl.loop(q * per, (q + 1) * per)
            def _(n):
                rs = pl.ds(pl.multiple_of(n * 128, 128), 128)
                d = jnp.dot(pb[rs, :tile], wbuf[0, 0], preferred_element_type=f32)
                for t in range(1, tiles):
                    d += jnp.dot(
                        pb[rs, t * tile : (t + 1) * tile],
                        wbuf[t // 2, t % 2],
                        preferred_element_type=f32,
                    )
                dg[rs, :] = (d * dg[rs, :].astype(f32)).astype(low_type)
                du[rs, :] = (d * du[rs, :].astype(f32)).astype(low_type)

            if q > 0:
                queue.advance()
        store_du.start()
        load_act.start()
        for c in fetch(0):
            c.start()

        def before(t):
            for c in fetch(t):
                c.wait()
            if t + 1 < tiles:
                for c in fetch(t + 1):
                    c.start()

        def partial(start, count, t, n):
            rs = pl.ds(start, count)
            return lax.dot_general(
                dg[rs, :], wbuf[t % 2, 0], NT, preferred_element_type=f32
            ) + lax.dot_general(du[rs, :], wbuf[t % 2, 1], NT, preferred_element_type=f32)

        rsum.scatter(partial, before, queue.advance)
        load_act.wait()
        for n, (j, k) in enumerate(second.blocks):
            r = j * second.hi + k
            second.g[r] = jnp.dot(
                pb[:, r * blk : (r + 1) * blk].T, dg[...], preferred_element_type=f32
            ).astype(low_type)
            queue.ready(second, j, k)
        load_own.wait()
        read = rsum.arrive()
        gg_o[...] = jnp.zeros_like(gg_o)
        for r in range(spread.parts):

            @pl.loop(0, spread.step // 32)
            def _(t):
                at = pl.multiple_of(r * spread.step + t * 32, 32)
                rs = pl.ds(at, 32)
                v, h = read(at, 32), h_r[rs, :]
                inv = inv_r[rs, :1]
                weighted = v * g_r[...]
                mean = jnp.mean(weighted * h, axis=-1, keepdims=True)
                dh = ogx[rs, :].astype(f32) + inv * weighted - h * (inv * inv * inv * mean)
                dh_o[rs, :] = dh
                dhb_o[pl.ds(pl.multiple_of(own + at, 32), 32), :] = dh.astype(low_type)
                gg_o[...] += jnp.sum((v * h * inv).reshape(4, 8, width), axis=0)

            spread.send(r)
            queue.advance()
        store_dh = pltpu.make_async_copy(dh_o, dh_h, ls.at[7])
        store_dh.start()
        for r in range(spread.parts):
            spread.forward(r)
            queue.advance()
        spread.finish()
        store_dhb = pltpu.make_async_copy(dhb_o, dhb_h, ls.at[8])
        store_dhb.start()
        queue.finish()
        first.finish(gate_o, dsq_o)
        down_o[...] = gate_o[...].T
        second.finish(gate_o, gsq_o)
        rsum.finish()
        for c in (store_du, store_dh, store_dhb):
            c.wait()

    sds = jax.ShapeDtypeStruct
    square = sds((8, ff), f32)
    return pl.pallas_call(
        kernel,
        name="mlp_backward",
        out_shape=[
            sds((ff, blk), f32),
            square,
            sds((blk, ff), f32),
            square,
            sds((rows, ff), low_type),
            sds((share, width), f32),
            sds((rows, width), low_type),
            sds((8, width), f32),
        ],
        in_specs=[HBM] * 8 + [VM] * 3,
        out_specs=[VM] * 4 + [HBM] * 3 + [VM],
        scratch_shapes=[
            pltpu.VMEM((rows, width), low_type),
            pltpu.VMEM((share, width), low_type),
            pltpu.VMEM((rows, ff), low_type),
            pltpu.VMEM((rows, ff), low_type),
            pltpu.VMEM((2, 2, tile, ff), low_type),
            pltpu.VMEM((share, width), f32),
            pltpu.VMEM((rows, width), low_type),
            DMA((9,)),
            DMA((rsum.tiles, 2)),
            DMA((rsum.tiles,)),
        ]
        + folds[0].scratch()
        + folds[1].scratch()
        + rsum.scratch()
        + spread.scratch(),
        compiler_params=big(cid),
        cost_estimate=cost(4e10, 1e8),
    )(hid, og, act, ga, ub, wd, wg, wu, h_own, inv_own, gain)


def attention_back_call(
    act, du, hid, wd, dhb, wqkv, a1, h_own, wo, q, k, v, lse, cosine, sine, segment,
    ob, x_own, inv_own, dh_own, gain, gain_two, squares, heads, kv_heads, dp, mp, cid
):
    rows, width = act.shape
    ff = du.shape[1]
    hd = cosine.shape[1]
    qcols, cols = heads * hd, wqkv.shape[1]
    blk = width // dp
    kv_rows, wide = blk // mp, cols - qcols
    block = min(256, rows)
    scale = hd**-0.5
    folds = [Fold(blk, ff, dp, 2), Fold(qcols, blk, dp, 2), Fold(blk, cols, dp, 2)]
    rsum = RowSum(rows, width, mp)
    spreads = [Spread(rows, mp, 2), Spread(rows, mp, 2)]
    share, tile, tiles = rsum.share, rsum.tile, rsum.tiles
    n_f, n_r, n_s = len(folds[0].scratch()), len(rsum.scratch()), len(spreads[0].scratch())
    n_sq = len(squares)
    local = [m * kv_heads // mp for m in range(mp)]
    shared = mp > kv_heads

    def kernel(
        act_r, du_r, hid_r, wd_r, dhb_r, wqkv_r, a_r, h_h, wo_h, q_r, k_r, v_r, l_h, c_h, s_h,
        sg_r, ob_h, x_h, inv_r, dh_h, gn_r, g2_r, *refs
    ):
        sq_r, refs = refs[:n_sq], refs[n_sq:]
        staged, refs = refs[-9:], refs[:-9]
        h_r, wo_r, l_r, c_r, s_r, ob_r, x_r, dh_r, st = staged
        g_r = gn_r.at[pl.ds(0, 1), :]
        stage = [
            pltpu.make_async_copy(a, b, st.at[n])
            for n, (a, b) in enumerate(
                zip((h_h, wo_h, l_h, c_h, s_h, ob_h, x_h, dh_h), staged[:8])
            )
        ]
        up_o, q_o, wo_o, kv_o, y_o, in_o, gain_o, tot_o = refs[:8]
        (pb, db, wbuf, bias, dk, dv, out, y_own, in_own, sq0, sq1, sq2, obt) = refs[8:21]
        (gg, mine, got, sent, got2, t1, t2, ls, ws, gm, gd, ts, credit) = refs[21:34]
        at = 34
        place = Place(dp, mp)
        me_dp, me_mp = lax.axis_index("dp"), place.m
        own = pl.multiple_of(place.m * share, 8)
        load_act = pltpu.make_async_copy(act_r, pb, ls.at[0])
        load_du = pltpu.make_async_copy(du_r, db, ls.at[1])
        load_dhb = pltpu.make_async_copy(dhb_r, pb, ls.at[2])
        load_hid = pltpu.make_async_copy(hid_r, db, ls.at[3])
        load_a = pltpu.make_async_copy(a_r, pb, ls.at[4])
        keeps = [
            pltpu.make_async_copy(o, full.at[pl.ds(own, share), :], ls.at[5 + n])
            for n, (o, full) in enumerate(((y_own, y_o), (in_own, in_o)))
        ]

        def fetch(t):
            return pltpu.make_async_copy(
                wd_r.at[pl.ds(t * tile, tile), :], wbuf.at[t % 2], ws.at[0, t]
            )

        def fetch_qkv(t):
            return pltpu.make_async_copy(
                wqkv_r.at[pl.ds(t * tile, tile), :],
                wbuf.at[t % 2, :, pl.ds(0, cols)],
                ws.at[1, t],
            )

        load_act.start()
        load_du.start()
        fetch(0).start()
        for c in stage:
            c.start()
        place.barrier()
        for f in folds:
            f.bind(place, refs[at : at + n_f])
            at += n_f
        rsum.bind(place, refs[at : at + n_r])
        at += n_r
        for p, o, full in zip(spreads, (y_own, in_own), (y_o, in_o)):
            p.bind(place, refs[at : at + n_s], full, o)
            at += n_s
        up, wof, qkvf = folds
        spread_y, spread_in = spreads
        queue = FoldQueue(folds)
        advance = queue.advance

        load_act.wait()
        load_du.wait()
        for j, kk in up.blocks:
            r = j * up.hi + kk
            up.g[r] = jnp.dot(
                pb[:, r * blk : (r + 1) * blk].T, db[...], preferred_element_type=f32
            ).astype(low_type)
            queue.ready(up, j, kk)
        load_hid.start()
        load_dhb.start()
        for c in stage:
            c.wait()
        load_hid.wait()

        def before(t):
            fetch(t).wait()
            if t + 1 < tiles:
                fetch(t + 1).start()

        def partial_y(start, count, t, n):
            return lax.dot_general(
                db[pl.ds(start, count), :], wbuf[t % 2], NT, preferred_element_type=f32
            )

        rsum.scatter(partial_y, before)
        fetch_qkv(0).start()
        advance()
        for n in range(qcols // 128):
            obt[n * 128 : (n + 1) * 128, :] = ob_r[:, n * 128 : (n + 1) * 128].T
        load_dhb.wait()
        for j, kk in wof.blocks:
            r = j * wof.hi + kk
            wof.g[r] = jnp.dot(
                obt[...], pb[:, r * blk : (r + 1) * blk], preferred_element_type=f32
            ).astype(low_type)
            queue.ready(wof, j, kk)
        dk[...] = jnp.zeros_like(dk)
        dv[...] = jnp.zeros_like(dv)
        length = sequence_length(sg_r[...], rows)
        count = rows // block
        for b in range(count):
            rs = pl.ds(b * block, block)
            keys = (b + 1) * block
            ks = slice(0, keys)
            bias[:, ks] = attention_bias(length, b * block, block, keys)
            do = lax.dot_general(pb[rs, :], wo_r[...], NT, preferred_element_type=f32).astype(
                low_type
            )
            cs, sn = c_r[rs, :], s_r[rs, :]
            for n in range(heads):
                hs = slice(n * hd, (n + 1) * hd)
                qb = q_r[rs, hs]
                s = lax.dot_general(qb, k_r[ks, :], NT, preferred_element_type=f32)
                p = jnp.exp(s * scale + bias[:, ks] - l_r[rs, n : n + 1])
                dpr = lax.dot_general(do[:, hs], v_r[ks, :], NT, preferred_element_type=f32)
                centre = jnp.sum(p * dpr, axis=-1, keepdims=True)
                ds = (p * (dpr - centre)).astype(low_type)
                u = jnp.dot(ds, k_r[ks, :], preferred_element_type=f32) * scale
                out[rs, hs] = (u * cs - pltpu.roll(u, hd // 2, 1) * sn).astype(low_type)
                dk[ks, :] += lax.dot_general(ds, qb, TN, preferred_element_type=f32)
                dv[ks, :] += lax.dot_general(
                    p.astype(low_type), do[:, hs], TN, preferred_element_type=f32
                )
            if b == count // 2:
                read_y = rsum.arrive()

                @pl.loop(0, share // 32)
                def _(t):
                    rt = pl.ds(pl.multiple_of(t * 32, 32), 32)
                    y = (h_r[rt, :] + read_y(t * 32, 32)).astype(low_type)
                    put_natural(place, y_own, rt, y, blk)

                for r in range(spread_y.parts):
                    spread_y.send(r)
                keeps[0].start()
                rsum.finish()
                rsum.free(credit)
            advance()
        load_a.start()
        u = dk[...] * scale
        out[:, qcols : qcols + hd] = (
            u * c_r[...] - pltpu.roll(u, hd // 2, 1) * s_r[...]
        ).astype(low_type)
        out[:, qcols + hd :] = dv[...].astype(low_type)

        def before_in(t):
            fetch_qkv(t).wait()
            if t + 1 < tiles:
                fetch_qkv(t + 1).start()

        def partial_in(start, count, t, n):
            return lax.dot_general(
                out[pl.ds(start, count), :],
                wbuf[t % 2, :, :cols],
                NT,
                preferred_element_type=f32,
            )

        rsum.freed(credit)
        rsum.scatter(partial_in, before_in)
        advance()
        load_a.wait()
        for n, (j, kk) in enumerate(qkvf.blocks):
            r = j * qkvf.hi + kk
            qkvf.g[r] = jnp.dot(
                pb[:, r * blk : (r + 1) * blk].T, out[...], preferred_element_type=f32
            ).astype(low_type)
            queue.ready(qkvf, j, kk)
            if n % 4 == 3:
                advance()
        for r in range(spread_y.parts):
            spread_y.forward(r)
            advance(2)
        advance(2)
        read = rsum.arrive()
        gg[...] = jnp.zeros_like(gg)

        @pl.loop(0, share // 32)
        def _(t):
            rs = pl.ds(pl.multiple_of(t * 32, 32), 32)
            g, x = read(t * 32, 32), x_r[rs, :].astype(f32)
            inv = inv_r[rs, :1]
            weighted = g * g_r[...]
            mean = jnp.mean(weighted * x, axis=-1, keepdims=True)
            d = dh_r[rs, :] + inv * weighted - x * (inv * inv * inv * mean)
            put_natural(place, in_own, rs, d.astype(low_type), blk)
            gg[...] += jnp.sum((g * x * inv).reshape(4, 8, width), axis=0)

        mine[...] = jnp.zeros_like(mine)
        mine[0:1, :] = jnp.sum(gg[...], axis=0, keepdims=True)
        mine[1:2, :] = jnp.sum(g2_r[...], axis=0, keepdims=True)
        got[place.m] = mine[...]
        gains_mp = []
        for n, m in place.others_mp():
            c = remote(mine, got.at[place.m], gm.at[0, n], gm.at[1, n], {"mp": m})
            c.start()
            gains_mp.append(c)
        for r in range(spread_in.parts):
            spread_in.send(r)
        keeps[1].start()
        advance(4)
        for c in gains_mp:
            c.wait()
        g = got[0]
        for n in range(1, mp):
            g += got[n]
        for r in range(dp):
            sent[r] = g[:, r * blk : (r + 1) * blk]
        gains_dp = []
        for r, d in place.others_dp():
            c = remote(sent.at[r], got2.at[r], gd.at[0, r], gd.at[1, r], {"dp": d})
            c.start()
            gains_dp.append(c)
        advance(2)
        for r in range(spread_in.parts):
            spread_in.forward(r)
            advance(1)
        queue.finish()
        for c in gains_dp:
            c.wait()
        g = sent[0]
        for r in range(1, dp):
            g += got2[r]
        gain_o[...] = g
        g = whole(g * g)
        total = jnp.where(me_mp == 0, g, jnp.zeros_like(g))
        for a in sq_r:
            total += whole(a[...])
        up.finish(up_o, sq0)
        wof.finish(wo_o, sq1)
        total += whole(sq0[...]) + whole(sq1[...])
        qkv = rsum.acc.at[pl.ds(0, blk), pl.ds(0, cols)]
        qkvf.finish(qkv, sq2)
        swaps = []
        for n, m in place.others_mp():
            c = remote(
                qkv.at[pl.ds(pl.multiple_of(m * kv_rows, 8), kv_rows), pl.ds(qcols, wide)],
                kv_o.at[me_mp],
                ts.at[0, n],
                ts.at[1, n],
                {"mp": m},
            )
            c.start()
            swaps.append(c)
        kv_o[me_mp] = qkv[pl.ds(pl.multiple_of(me_mp * kv_rows, 8), kv_rows), qcols:]
        if shared:
            total += whole(sq2[:, :qcols])
            for c in swaps:
                c.wait_recv()
            for h in range(kv_heads):
                of = [m for m in range(mp) if local[m] == h]
                g = kv_o[of[0]]
                for m in of[1:]:
                    g += kv_o[m]
                total += whole(g * g)
        else:
            total += whole(sq2[...])
        for peers, table, me, base in (
            ([(n, {"mp": m}) for n, m in place.others_mp()], t1, me_mp, 2),
            ([(n, {"dp": d}) for n, d in place.others_dp()], t2, me_dp, 4),
        ):
            table[me] = jnp.broadcast_to(total, (8, 128))
            waits = []
            for n, to in peers:
                c = remote(table.at[me], table.at[me], ts.at[base, n], ts.at[base + 1, n], to)
                c.start()
                waits.append(c)
            if base == 2:
                q_o[...] = qkv[:, :qcols]
            for c in waits:
                c.wait()
            total = table[0]
            for n in range(1, len(peers) + 1):
                total += table[n]
        tot_o[...] = total
        for c in swaps:
            if shared:
                c.wait_send()
            else:
                c.wait()
        rsum.finish()
        for p, c in zip(spreads, keeps):
            p.finish()
            c.wait()

    sds = jax.ShapeDtypeStruct
    scratch = []
    for part in folds + [rsum] + spreads:
        scratch += part.scratch()
    staged = (h_own, wo, lse, cosine, sine, ob, x_own, dh_own)
    scratch += [pltpu.VMEM(a.shape, a.dtype) for a in staged] + [DMA((len(staged),))]
    return pl.pallas_call(
        kernel,
        name="attention_backward",
        out_shape=[
            sds((blk, ff), f32),
            sds((blk, qcols), f32),
            sds((qcols, blk), f32),
            sds((mp, kv_rows, wide), f32),
            sds((rows, width), low_type),
            sds((rows, width), low_type),
            sds((8, blk), f32),
            sds((8, 128), f32),
        ],
        in_specs=[HBM] * 9
        + [VM] * 3
        + [HBM] * 3
        + [VM]
        + [HBM] * 2
        + [VM, HBM]
        + [VM] * (2 + n_sq),
        out_specs=[VM] * 4 + [HBM] * 2 + [VM] * 2,
        scratch_shapes=[
            pltpu.VMEM((rows, width), low_type),
            pltpu.VMEM((rows, ff), low_type),
            pltpu.VMEM((2, tile, max(ff, cols)), low_type),
            pltpu.VMEM((block, rows), f32),
            pltpu.VMEM((rows, hd), f32),
            pltpu.VMEM((rows, hd), f32),
            pltpu.VMEM((rows, cols), low_type),
            pltpu.VMEM((share, width), low_type),
            pltpu.VMEM((share, width), low_type),
            pltpu.VMEM((8, ff), f32),
            pltpu.VMEM((8, blk), f32),
            pltpu.VMEM((8, cols), f32),
            pltpu.VMEM((qcols, rows), low_type),
            pltpu.VMEM((8, width), f32),
            pltpu.VMEM((8, width), f32),
            pltpu.VMEM((mp, 8, width), f32),
            pltpu.VMEM((dp, 8, blk), f32),
            pltpu.VMEM((dp, 8, blk), f32),
            pltpu.VMEM((mp, 8, 128), f32),
            pltpu.VMEM((dp, 8, 128), f32),
            DMA((7,)),
            DMA((2, tiles)),
            DMA((2, mp)),
            DMA((2, dp)),
            DMA((6, max(dp, mp))),
            pltpu.SemaphoreType.REGULAR,
        ]
        + scratch,
        compiler_params=big(cid),
        cost_estimate=cost(4e10, 1e8),
    )(
        act, du, hid, wd, dhb, wqkv, a1, h_own, wo, q, k, v, lse, cosine, sine, segment,
        ob, x_own, inv_own, dh_own, gain, gain_two, *squares
    )


def whole(v):
    return jnp.sum(jnp.sum(v, axis=0, keepdims=True), axis=1, keepdims=True)


def update_call(total, widen, keep, groups):
    steps = 4
    count = len(groups)

    def split(shape):
        return shape[-2] % (steps * 8) == 0 and shape[-2] >= 128

    def spec(shape, cut):
        lead = len(shape) - 2
        rows = shape[-2] // steps if cut else shape[-2]
        return pl.BlockSpec(
            shape[:-2] + (rows, shape[-1]), lambda i: (0,) * lead + (i if cut else 0, 0)
        )

    ins, in_specs, outs, out_specs, kinds = [], [], [], [], []
    for weight, moment, square, grads, rate, decay in groups:
        cut = split(weight.shape)
        ins += [weight, moment, square] + grads
        in_specs += [spec(weight.shape, cut)] * 3 + [spec(g.shape, cut) for g in grads]
        outs += [jax.ShapeDtypeStruct(weight.shape, f32)] * 3
        out_specs += [spec(weight.shape, cut)] * 3
        kinds.append((len(grads), rate, decay))

    wide_spec = pl.BlockSpec((widen.shape[0] // steps, widen.shape[1]), lambda i: (i, 0))
    outs += [
        jax.ShapeDtypeStruct((1, 1), f32),
        jax.ShapeDtypeStruct(keep.shape, keep.dtype),
        jax.ShapeDtypeStruct(widen.shape, f32),
    ]
    out_specs += [pl.BlockSpec((1, 1), lambda i: (0, 0)), wide_spec, wide_spec]

    def kernel(tot_r, wide_r, keep_r, *refs):
        out_refs = refs[len(ins) :]
        out_refs[-1][...] = wide_r[...].astype(f32)
        out_refs[-2][...] = keep_r[...]
        norm = jnp.sqrt(tot_r[:1, :1])
        out_refs[-3][...] = norm
        factor = jnp.minimum(1.0, clip_limit / (norm + 1e-06))
        at = 0
        for n, (parts, rate, decay) in enumerate(kinds):
            w_r, m_r, s_r = refs[at : at + 3]
            g_rs = refs[at + 3 : at + 3 + parts]
            at += 3 + parts
            w_o, m_o, s_o = out_refs[3 * n : 3 * n + 3]

            def one(index, gradient):
                new = adam_update(
                    w_r[index], m_r[index], s_r[index], gradient, factor, rate, decay
                )
                w_o[index], m_o[index], s_o[index] = new

            if parts == 1 and g_rs[0].shape == w_r.shape:
                one(..., g_rs[0][...])
            elif parts == 1 and g_rs[0].ndim == 3:
                copies, _, wide = g_rs[0].shape
                hd = wide // 2
                heads = w_r.shape[2] // hd
                for h in range(heads):
                    v = None
                    for m in range(copies):
                        if m * heads // copies == h:
                            v = g_rs[0][m] if v is None else v + g_rs[0][m]
                    for i in range(2):
                        index = (i, slice(None), slice(h * hd, (h + 1) * hd))
                        one(index, v[:, i * hd : (i + 1) * hd])
            elif parts == 1:
                one(..., g_rs[0][: w_r.shape[0], :])
            else:
                for i in range(parts):
                    one(i, g_rs[i][...])

    return pl.pallas_call(
        kernel,
        name="update",
        grid=(steps,),
        out_shape=outs,
        in_specs=[pl.BlockSpec((8, 128), lambda i: (0, 0)), wide_spec, wide_spec] + in_specs,
        out_specs=out_specs,
        compiler_params=pltpu.CompilerParams(vmem_limit_bytes=61 * 2**20),
        cost_estimate=cost(3e7, 4e7),
    )(total, widen, keep, *ins)


def body(
    tokens,
    segment_ids,
    out_grad,
    query_weight,
    keyval_weight,
    output_weight,
    gateup_weight,
    down_weight,
    norm_gains,
    query_moment,
    keyval_moment,
    output_moment,
    gateup_moment,
    down_moment,
    gains_moment,
    query_square,
    keyval_square,
    output_square,
    gateup_square,
    down_square,
    gains_square,
):
    dp = lax.axis_size("dp")
    mp = lax.axis_size("mp")
    heads = H // mp
    rows = tokens.shape[0]
    blk = D // dp
    qcols = query_weight.shape[1]

    half = np.arange(HD // 2, dtype=np.float64) * 2.0 / HD
    rates = jnp.asarray(np.tile(rope_base**-half, 2)[None].astype(np.float32))
    segment = segment_ids.reshape(-1, 128)
    (
        wqkv, wo, gains, og, x_own, act_one, inv_one, q, k, v, attn, lse, gate_low, up_low, down_low,
        cosine, sine,
    ) = attention_call(
        tokens, out_grad, query_weight, keyval_weight, output_weight, norm_gains,
        gateup_weight, down_weight, segment, rates, heads, KV, dp, mp, 0, norm_eps,
    )
    wg, wu, wd, h_own, inv_two, act_two, hid, ga, ub = forward_call(
        attn, wo, x_own, gains, gate_low, up_low, down_low, dp, mp, 1, norm_eps
    )
    down_share, down_sq, gate_share, gate_sq, du, dh_own, dhb, gain_two_part = mlp_back_call(
        hid, og, act_two, ga, ub, wd, wg, wu, h_own, inv_two, gains, dp, mp, 2
    )
    (
        up_share, query_share, output_share, kv_parts, layer_out, in_low, gains_share, total
    ) = attention_back_call(
        act_two, du, hid, wd, dhb, wqkv, act_one, h_own, wo, q, k, v, lse, cosine, sine, segment,
        attn, x_own, inv_one, dh_own, gains, gain_two_part, [down_sq, gate_sq],
        heads, KV, dp, mp, 3,
    )
    output_rate = matrix_rate * (TOK_DEV * D / (16.0 * H * HD)) ** 0.5
    *news, grad_norm, layer_out, input_grad = update_call(
        total,
        in_low,
        layer_out,
        [
            (query_weight, query_moment, query_square, [query_share], matrix_rate, weight_decay),
            (keyval_weight, keyval_moment, keyval_square, [kv_parts], matrix_rate, weight_decay),
            (
                output_weight, output_moment, output_square, [output_share],
                output_rate, weight_decay,
            ),
            (
                gateup_weight, gateup_moment, gateup_square, [gate_share, up_share],
                matrix_rate, weight_decay,
            ),
            (down_weight, down_moment, down_square, [down_share], matrix_rate, weight_decay),
            (norm_gains, gains_moment, gains_square, [gains_share], gain_rate, 0.0),
        ],
    )
    return (layer_out, input_grad, grad_norm.reshape(())) + tuple(news[0::3] + news[1::3] + news[2::3])


def solution(mesh):
    params = (
        P("dp", "mp"),
        P(None, ("dp", "mp"), None),
        P("mp", "dp"),
        P(None, "dp", "mp"),
        P("mp", "dp"),
        P(None, "dp"),
    )
    rows = P("dp", None)
    return jax.shard_map(
        body,
        mesh=mesh,
        in_specs=(rows, P("dp"), rows) + params * 3,
        out_specs=(rows, rows, P()) + params * 3,
        check_vma=False,
    )
```

```python
import jax
import jax.numpy as jnp
import numpy as np
from jax import lax
from jax.experimental import pallas as pl
from jax.experimental.pallas import tpu as pltpu
from jax.sharding import PartitionSpec as P

MESH_ID = pl.DeviceIdType.MESH
low_type = jnp.bfloat16
f32 = jnp.float32
WINDOW = 32
HBM = pl.BlockSpec(memory_space=pl.ANY)
VM = pl.BlockSpec(memory_space=pltpu.VMEM)
DMA = pltpu.SemaphoreType.DMA
NT = (((1,), (1,)), ((), ()))
TN = (((0,), (0,)), ((), ()))


D = 2048
H = 16
KV = 4
HD = 128
TOK_DEV = 1024
ADAM_STEP = 10


norm_eps = 1e-05
rope_base = 10000.0
clip_limit = 1.0
beta_first = 0.9
beta_second = 0.95
adam_eps = 1e-08
weight_decay = 0.1
matrix_rate = 0.02
gain_rate = 0.6


def adam_update(weight, moment, square, gradient, factor, step_rate, decay_rate):
    clipped = gradient * factor
    moment_new = beta_first * moment + (1.0 - beta_first) * clipped
    square_new = beta_second * square + (1.0 - beta_second) * clipped * clipped
    first_fix = 1.0 - beta_first**ADAM_STEP
    second_fix = 1.0 - beta_second**ADAM_STEP
    step_dir = moment_new / first_fix / (jnp.sqrt(square_new / second_fix) + adam_eps)
    return (weight - step_rate * (step_dir + decay_rate * weight), moment_new, square_new)


def split_dp(count):
    lo = 1
    while lo * lo * 4 <= count:
        lo *= 2
    return count // lo, lo


class Place:
    def __init__(self, dp, mp):
        self.dp, self.mp = dp, mp
        self.hi, self.lo = split_dp(dp)
        self.mlo = 2 if mp % 2 == 0 else 1
        self.mhi = mp // self.mlo
        me = lax.axis_index("dp")
        self.h, self.l = me // self.lo, lax.rem(me, self.lo)
        self.m = lax.axis_index("mp")
        self.y, self.c = self.m // self.mlo, lax.rem(self.m, self.mlo)

    def z(self, k):
        return {"dp": lax.rem(self.h + (k + self.hi) % self.hi, self.hi) * self.lo + self.l}

    def x(self, j):
        return {"dp": self.h * self.lo + lax.rem(self.l + (j + self.lo) % self.lo, self.lo)}

    def part(self, k, i):
        return lax.rem(self.y + k, self.mhi) * self.mlo + lax.rem(self.c + i, self.mlo)

    def others_dp(self):
        out = []
        for j in range(self.lo):
            for k in range(self.hi):
                if j or k:
                    out.append((j * self.hi + k, self.owner(j, k)))
        return out

    def owner(self, j, k):
        return lax.rem(self.h + self.hi - k, self.hi) * self.lo + lax.rem(
            self.l + self.lo - j, self.lo
        )

    def others_mp(self):
        return [(s, lax.rem(self.m + s, self.mp)) for s in range(1, self.mp)]

    def barrier(self):
        bar = pltpu.get_barrier_semaphore()
        peers = [{"dp": d} for _, d in self.others_dp()] + [{"mp": m} for _, m in self.others_mp()]
        for p in peers:
            pl.semaphore_signal(bar, inc=1, device_id=p, device_id_type=MESH_ID)
        pl.semaphore_wait(bar, len(peers))


def remote(src, dst, send, recv, to):
    return pltpu.make_async_remote_copy(src, dst, send, recv, to, MESH_ID)


class Gather:
    def __init__(self, shapes, axes, splits, dp, late=()):
        self.hi, self.lo = split_dp(dp)
        self.shapes, self.axes, self.late = shapes, axes, late
        self.chunks = []
        for i, s in enumerate(shapes):
            step = s[0] // splits[i]
            self.chunks += [(i, n * step, step) for n in range(splits[i])]
        self.count = len(self.chunks)

    def out_shapes(self):
        n = self.hi * self.lo
        return [
            jax.ShapeDtypeStruct((s[0] * n, s[1]) if a == 0 else (s[0], s[1] * n), low_type)
            for s, a in zip(self.shapes, self.axes)
        ]

    def scratch(self):
        c, hi, lo = self.count, self.hi, self.lo
        return [
            DMA((c, hi - 1)),
            DMA((c, hi - 1)),
            DMA((c, hi, max(lo - 1, 1))),
            DMA((c, hi, max(lo - 1, 1))),
            DMA((c,)),
        ]

    def bind(self, place, ins, outs, sems):
        zs, zr, xs, xr, ls = sems
        hi, lo = self.hi, self.lo

        def dst(c, r):
            i, at, step = self.chunks[c]
            rows, cols = self.shapes[i]
            if self.axes[i] == 0:
                return outs[i].at[pl.ds(r * rows + at, step)]
            return outs[i].at[pl.ds(at, step), pl.ds(r * cols, cols)]

        def src(c):
            i, at, step = self.chunks[c]
            return ins[i].at[pl.ds(at, step)]

        self.zc = {
            (c, k): remote(src(c), dst(c, k), zs.at[c, k - 1], zr.at[c, k - 1], place.z(k))
            for c in range(self.count)
            for k in range(1, hi)
        }
        self.xc = {
            (c, k, j): remote(
                src(c) if k == 0 else dst(c, k),
                dst(c, j * hi + k),
                xs.at[c, k, j - 1],
                xr.at[c, k, j - 1],
                place.x(j),
            )
            for c in range(self.count)
            for k in range(hi)
            for j in range(1, lo)
        }
        self.lc = [pltpu.make_async_copy(src(c), dst(c, 0), ls.at[c]) for c in range(self.count)]
        self.items = []
        self.started = 0
        self.window = 2
        for c in range(self.count):
            for k in range(1, hi):
                self.items.append((c, k))
        self.arrived = [False] * self.count

    def start_own(self, c):
        for j in range(1, self.lo):
            self.xc[c, 0, j].start()
        self.lc[c].start()

    def start_z(self, c):
        if c in self.late:
            self.late[c]()
            self.start_own(c)
        for k in range(1, self.hi):
            self.zc[c, k].start()

    def begin(self):
        for c in range(self.count):
            if c < self.window:
                self.start_z(c)
            if c not in self.late:
                self.start_own(c)
        self.started = min(self.window, self.count)

    def step(self, n=1):
        for _ in range(n):
            if not self.items:
                return
            c, k = self.items.pop(0)
            self.zc[c, k].wait_recv()
            for j in range(1, self.lo):
                self.xc[c, k, j].start()
            if k == self.hi - 1 and self.started < self.count:
                self.start_z(self.started)
                self.started += 1

    def arrive(self, c):
        if self.arrived[c]:
            return
        while any(i[0] <= c for i in self.items):
            self.step()
        self.lc[c].wait()
        for k in range(self.hi):
            for j in range(1, self.lo):
                self.xc[c, k, j].wait_recv()
        self.arrived[c] = True

    def finish(self):
        for c in range(self.count):
            self.arrive(c)
        for c in range(self.count):
            for k in range(1, self.hi):
                self.zc[c, k].wait_send()
            for k in range(self.hi):
                for j in range(1, self.lo):
                    self.xc[c, k, j].wait_send()


class LineGather(Gather):
    def __init__(self, shapes, splits, dp, first):
        super().__init__(shapes, (0,) * len(shapes), splits, dp)
        self.first = first

    def scratch(self):
        c, hi, lo = self.count, self.hi, self.lo
        return [
            DMA((c, lo, hi)),
            DMA((c, lo, hi)),
            DMA((c, lo, hi)),
            DMA((c, hi)),
            DMA((c, hi)),
            DMA((c,)),
        ]

    def bind(self, place, ins, outs, sems):
        us, ds, zr, xs, xr, ls = sems
        hi, lo = self.hi, self.lo
        self.h = place.h

        def slot(c, j, k):
            i, at, step = self.chunks[c]
            r = j * hi + k
            return outs[i].at[pl.ds(r * self.shapes[i][0] + at, step)]

        def src(c, j, k):
            i, at, step = self.chunks[c]
            return slot(c, j, k) if j or k else ins[i].at[pl.ds(at, step)]

        self.rows_of = [range(lo) if c in self.first else range(1) for c in range(self.count)]
        each = [(c, j, k) for c in range(self.count) for j in self.rows_of[c] for k in range(hi)]
        self.up = {
            (c, j, k): remote(
                src(c, j, k), slot(c, j, k + 1), us.at[c, j, k], zr.at[c, j, k + 1], place.z(1)
            )
            for c, j, k in each
            if k < hi - 1
        }
        self.down = {
            (c, j, k): remote(
                src(c, j, k),
                slot(c, j, (k - 1) % hi),
                ds.at[c, j, k],
                zr.at[c, j, (k - 1) % hi],
                place.z(-1),
            )
            for c, j, k in each
            if k != 1
        }
        self.into = {
            (c, j, k): remote(
                slot(c, j, k), slot(c, j, k), us.at[c, j, k - 1], zr.at[c, j, k], place.z(1)
            )
            for c, j, k in each
            if k
        }
        self.xc = {
            (c, k): remote(src(c, 0, k), slot(c, 1, k), xs.at[c, k], xr.at[c, k], place.x(1))
            for c in range(self.count)
            for k in range(1 if c in self.first else hi)
        }
        self.lc = [
            pltpu.make_async_copy(src(c, 0, 0), slot(c, 0, 0), ls.at[c]) for c in range(self.count)
        ]
        self.items = [
            (c, j, k) for c in range(self.count) for j in self.rows_of[c] for k in (1, 3, 2)
        ]
        self.window = 3
        self.arrived = [False] * self.count

    def passes(self, k):
        h, hi = self.h, self.hi
        if k == 0:
            return h < hi - 1, h > 0
        return (h >= k) & (h < hi - 1), (h < k) & (h > 0)

    def pass_on(self, key, act):
        c, j, k = key
        up, down = self.passes(k)
        if key in self.up:

            @pl.when(up)
            def _():
                act(self.up[key])

        if key in self.down:

            @pl.when(down)
            def _():
                act(self.down[key])

    def start_z(self, c):
        for j in self.rows_of[c]:
            if j:
                self.xc[c, 0].wait_recv()
            self.pass_on((c, j, 0), lambda copy: copy.start())

    def begin(self):
        for c in range(self.count):
            if c < self.window:
                self.start_z(c)
            self.xc[c, 0].start()
            self.lc[c].start()
        self.started = min(self.window, self.count)

    def step(self, n=1):
        for _ in range(n):
            if not self.items:
                return
            c, j, k = self.items.pop(0)
            self.into[c, j, k].wait_recv()
            self.pass_on((c, j, k), lambda copy: copy.start())
            if (c, k) in self.xc:
                self.xc[c, k].start()
            if (j, k) == (self.rows_of[c][-1], 2) and self.started < self.count:
                self.start_z(self.started)
                self.started += 1

    def arrive(self, c):
        if self.arrived[c]:
            return
        while any(i[0] <= c for i in self.items):
            self.step()
        self.lc[c].wait()
        for k in range(self.hi):
            if (c, k) in self.xc and c not in self.first:
                self.xc[c, k].wait_recv()
        self.arrived[c] = True

    def finish(self):
        for c in range(self.count):
            self.arrive(c)
        for c in range(self.count):
            for j in self.rows_of[c]:
                for k in range(self.hi):
                    self.pass_on((c, j, k), lambda copy: copy.wait_send())
        for copy in self.xc.values():
            copy.wait_send()


class RowSum:
    def __init__(self, rows, width, mp):
        self.mlo = 2 if mp % 2 == 0 else 1
        self.mhi = mp // self.mlo
        self.share, self.width = rows // mp, width
        self.tile = min(512, width)
        self.tiles = width // self.tile

    def scratch(self):
        h, t = self.mhi, self.tiles
        g = max(h - 1, 1)
        return [
            pltpu.VMEM((h, self.share, self.width), low_type),
            pltpu.VMEM((h, self.share, self.width), low_type),
            pltpu.VMEM((g, self.share, self.width), low_type),
            pltpu.VMEM((g, self.share, self.width), low_type),
            pltpu.VMEM((self.share, self.width), f32),
            DMA((h, t)),
            DMA((h, t)),
            DMA((g, t)),
            DMA((g, t)),
        ]

    def bind(self, place, refs):
        self.place = place
        (self.cs, self.cr, self.ys, self.yr, self.acc) = refs[:5]
        css, crs, yss, yrs = refs[5:]
        h = self.mhi

        def sl(ref, k, t):
            return ref.at[k, :, pl.ds(t * self.tile, self.tile)]

        other = {"mp": place.part(0, 1)}
        self.cc = {
            (k, t): remote(sl(self.cs, k, t), sl(self.cr, k, t), css.at[k, t], crs.at[k, t], other)
            for k in range(h)
            for t in range(self.tiles)
        }
        self.yc = {
            (k, t): remote(
                sl(self.ys, k - 1, t),
                sl(self.yr, k - 1, t),
                yss.at[k - 1, t],
                yrs.at[k - 1, t],
                {"mp": place.part(k, 0)},
            )
            for k in range(1, h)
            for t in range(self.tiles)
        }

    def start_of(self, k, i):
        return pl.multiple_of(self.place.part(k, i) * self.share, 8)

    def scatter(self, partial, before=lambda t: None, between=lambda: None):
        order = list(range(1, self.mhi)) + [0]
        for t in range(self.tiles):
            before(t)
            cols = pl.ds(t * self.tile, self.tile)
            if self.mlo > 1:
                for k in order:
                    v = partial(self.start_of(k, 1), self.share, t, self.tile)
                    self.cs[k, :, cols] = v.astype(low_type)
                    self.cc[k, t].start()
            for k in order:
                v = partial(self.start_of(k, 0), self.share, t, self.tile)
                if self.mlo > 1:
                    self.cc[k, t].wait_recv()
                    v += self.cr[k, :, cols].astype(f32)
                if k:
                    self.ys[k - 1, :, cols] = v.astype(low_type)
                    self.yc[k, t].start()
                else:
                    self.acc[:, cols] = v
            between()

    def arrive(self):
        for t in range(self.tiles):
            for k in range(1, self.mhi):
                self.yc[k, t].wait_recv()

        def read(at, count):
            v = self.acc[pl.ds(at, count), :]
            for k in range(1, self.mhi):
                v += self.yr[k - 1, pl.ds(at, count), :].astype(f32)
            return v

        return read

    def finish(self):
        for t in range(self.tiles):
            if self.mlo > 1:
                for k in range(self.mhi):
                    self.cc[k, t].wait_send()
            for k in range(1, self.mhi):
                self.yc[k, t].wait_send()

    def free(self, credit):
        for k in range(1, self.mhi):
            to = {"mp": self.place.part(k, 0)}
            pl.semaphore_signal(credit, inc=1, device_id=to, device_id_type=MESH_ID)
        for i in range(1, self.mlo):
            to = {"mp": self.place.part(0, i)}
            pl.semaphore_signal(credit, inc=1, device_id=to, device_id_type=MESH_ID)

    def freed(self, credit):
        pl.semaphore_wait(credit, self.mhi - 1 + self.mlo - 1)


class Spread:
    def __init__(self, rows, mp, parts):
        self.mlo = 2 if mp % 2 == 0 else 1
        self.mhi = mp // self.mlo
        self.share, self.parts = rows // mp, parts
        self.step = self.share // parts

    def scratch(self):
        h, p = self.mhi, self.parts
        g = max(h - 1, 1)
        return [DMA((g, p)), DMA((g, p)), DMA((h, p)), DMA((h, p))]

    def bind(self, place, refs, full, own=None):
        gys, gyr, gcs, gcr = refs
        h, p = self.mhi, self.parts
        other = {"mp": place.part(0, 1)}

        def rows_at(m, r):
            return full.at[pl.ds(pl.multiple_of(m * self.share + r * self.step, 8), self.step), :]

        def mine(r):
            if own is None:
                return rows_at(place.m, r)
            return own.at[pl.ds(r * self.step, self.step), :]

        self.gy = {
            (k, r): remote(
                mine(r),
                rows_at(place.m, r),
                gys.at[k - 1, r],
                gyr.at[k - 1, r],
                {"mp": place.part(k, 0)},
            )
            for k in range(1, h)
            for r in range(p)
        }
        self.gc = {
            (k, r): remote(
                rows_at(place.part((h - k) % h, 0), r) if k else mine(r),
                rows_at(place.part((h - k) % h, 0), r),
                gcs.at[k, r],
                gcr.at[k, r],
                other,
            )
            for k in range(h)
            for r in range(p)
        }

    def send(self, r):
        for k in range(1, self.mhi):
            self.gy[k, r].start()
        if self.mlo > 1:
            self.gc[0, r].start()

    def forward(self, r):
        for k in range(1, self.mhi):
            self.gy[k, r].wait_recv()
            if self.mlo > 1:
                self.gc[k, r].start()

    def finish(self):
        for r in range(self.parts):
            if self.mlo > 1:
                for k in range(self.mhi):
                    self.gc[k, r].wait()
            for k in range(1, self.mhi):
                self.gy[k, r].wait_send()


def sequence_length(seg, rows):
    top = jnp.max(jnp.max(seg, axis=1, keepdims=True), axis=0, keepdims=True)
    return jnp.where(top == 0, rows, jnp.where(top == 1, rows // 2, rows // 4))


def attention_bias(length, start, count, keys):
    row = start + lax.broadcasted_iota(jnp.int32, (count, 1), 0)
    first = row - (row & (length - 1))
    col = lax.broadcasted_iota(jnp.int32, (count, keys), 1)
    return jnp.where((col <= row) & (col >= first), 0.0, -1e30)


def small_rows(total, step, fn):
    @pl.loop(0, total // step)
    def _(t):
        fn(pl.multiple_of(t * step, step))


def forward_call(attn, wo, x_own, gain, gate, up, down, dp, mp, cid, eps):
    rows, width = attn.shape[0], x_own.shape[1]
    ff = gate.shape[1]
    shapes = [gate.shape, up.shape, down.shape]
    if split_dp(dp) == (4, 2):
        gather = LineGather(shapes, (2, 2, 2), dp, (5,))
    else:
        gather = Gather(shapes, (0, 0, 0), (2, 2, 2), dp)
    rsum, spread = RowSum(rows, width, mp), Spread(rows, mp, 2)
    share = rsum.share
    n_g, n_r = len(gather.scratch()), len(rsum.scratch())
    tile = 128

    def kernel(attn_r, wo_r, x_r, gains_r, gate_r, up_r, down_r, *refs):
        gain_r = gains_r.at[pl.ds(1, 1), :]
        wg_o, wu_o, wd_o, h_o, inv_o, act_o = refs[:6]
        saved = refs[6:9]
        hid_v, ga_v, ub_v, wg_v, wu_v, wsem, ssem = refs[9:16]
        g_s = refs[16 : 16 + n_g]
        r_s = refs[16 + n_g : 16 + n_g + n_r]
        place = Place(dp, mp)
        place.barrier()
        gather.bind(place, (gate_r, up_r, down_r), (wg_o, wu_o, wd_o), g_s)
        rsum.bind(place, r_s)
        spread.bind(place, refs[16 + n_g + n_r :], act_o)
        gather.begin()

        def partial(start, count, t, n):
            return jnp.dot(
                attn_r[pl.ds(start, count), :],
                wo_r[:, pl.ds(t * n, n)],
                preferred_element_type=f32,
            )

        rsum.scatter(partial)
        gather.step(2)
        read = rsum.arrive()
        for r in range(spread.parts):
            base = r * spread.step
            own = place.m * share

            def norm(at):
                v = x_r[pl.ds(base + at, 32), :].astype(f32) + read(base + at, 32)
                h_o[pl.ds(base + at, 32), :] = v
                inv = lax.rsqrt(jnp.mean(v * v, axis=-1, keepdims=True) + eps)
                inv_o[pl.ds(base + at, 32), :] = jnp.broadcast_to(inv, (32, 128))
                act_o[pl.ds(pl.multiple_of(own + base + at, 32), 32), :] = (
                    v * inv * gain_r[...]
                ).astype(low_type)

            small_rows(spread.step, 32, norm)
            spread.send(r)
            gather.step(1)
        for r in range(spread.parts):
            spread.forward(r)
            gather.step(1)
        spread.finish()
        rsum.finish()
        for c in range(2):
            gather.arrive(c)
        cg = pltpu.make_async_copy(wg_o, wg_v, wsem.at[0])
        cg.start()
        for c in range(2, 4):
            gather.arrive(c)
        cu = pltpu.make_async_copy(wu_o, wu_v, wsem.at[1])
        cu.start()
        cg.wait()
        cu.wait()
        groups = 4
        per = rows // tile // groups
        stores = []
        for q in range(groups):

            @pl.loop(q * per, (q + 1) * per)
            def _(t):
                rs = pl.ds(pl.multiple_of(t * tile, tile), tile)
                a = act_o[rs, :]
                gp = jnp.dot(a, wg_v[...], preferred_element_type=f32)
                upv = jnp.dot(a, wu_v[...], preferred_element_type=f32)
                sg = jax.nn.sigmoid(gp)
                sw = gp * sg
                hid_v[rs, :] = (sw * upv).astype(low_type)
                ga_v[rs, :] = (upv * sg * (1.0 + gp * (1.0 - sg))).astype(low_type)
                ub_v[rs, :] = sw.astype(low_type)

            rs = pl.ds(q * per * tile, per * tile)
            for n, (v, o) in enumerate(zip((hid_v, ga_v, ub_v), saved)):
                c = pltpu.make_async_copy(v.at[rs, :], o.at[rs, :], ssem.at[q, n])
                c.start()
                stores.append(c)
            gather.step(3)
        gather.finish()
        for c in stores:
            c.wait()

    sds = jax.ShapeDtypeStruct
    act_shape = sds((rows, ff), low_type)
    return pl.pallas_call(
        kernel,
        name="forward_mlp",
        out_shape=gather.out_shapes()
        + [
            sds((share, width), f32),
            sds((share, 128), f32),
            sds((rows, width), low_type),
            act_shape,
            act_shape,
            act_shape,
        ],
        in_specs=[VM] * 4 + [HBM] * 3,
        out_specs=[HBM] * 3 + [VM] * 3 + [HBM] * 3,
        scratch_shapes=[pltpu.VMEM((rows, ff), low_type)] * 3
        + [
            pltpu.VMEM((width, ff), low_type),
            pltpu.VMEM((width, ff), low_type),
            DMA((2,)),
            DMA((4, 3)),
        ]
        + gather.scratch()
        + rsum.scratch()
        + spread.scratch(),
        compiler_params=big(cid),
        cost_estimate=cost(2e10, 1e8),
    )(attn, wo, x_own, gain, gate, up, down)


def fold_order(hi):
    return sorted(range(1, hi), key=lambda k: -min(k, hi - k)) + [0]


class Fold:
    def __init__(self, rows, cols, dp, sub):
        self.hi, self.lo = split_dp(dp)
        self.rows, self.cols, self.sub = rows, cols, sub
        self.step = rows // sub
        self.order = fold_order(self.hi)

    def scratch(self):
        hi, lo, s = self.hi, self.lo, self.sub
        j = max(lo - 1, 1)
        return [
            pltpu.VMEM((lo * hi, self.rows, self.cols), low_type),
            pltpu.VMEM((j * hi, self.rows, self.cols), low_type),
            pltpu.VMEM((hi - 1, self.rows, self.cols), low_type),
            DMA((j, hi, s)),
            DMA((j, hi, s)),
            DMA((hi - 1, s)),
            DMA((hi - 1, s)),
        ]

    def out_shapes(self):
        return [
            jax.ShapeDtypeStruct((self.rows, self.cols), f32),
            jax.ShapeDtypeStruct((8, self.cols), f32),
        ]

    def bind(self, place, refs):
        self.g, self.xb, self.zb, xs, xr, zs, zr = refs
        hi, lo = self.hi, self.lo

        def part(s):
            return pl.ds(s * self.step, self.step)

        self.part = part
        self.xc = {
            (k, j, s): remote(
                self.g.at[j * hi + k, part(s), :],
                self.xb.at[(j - 1) * hi + k, part(s), :],
                xs.at[j - 1, k, s],
                xr.at[j - 1, k, s],
                place.x(-j),
            )
            for k in range(hi)
            for j in range(1, lo)
            for s in range(self.sub)
        }
        self.zc = {
            (k, s): remote(
                self.g.at[k, part(s), :],
                self.zb.at[k - 1, part(s), :],
                zs.at[k - 1, s],
                zr.at[k - 1, s],
                place.z(-k),
            )
            for k in range(1, hi)
            for s in range(self.sub)
        }
        self.items = [(k, s) for k in self.order for s in range(self.sub)]
        self.blocks = [(j, k) for j in range(1, lo) for k in self.order]
        self.blocks += [(0, k) for k in self.order]
        self.small = next(n for n in (64, 32, 16, 8) if self.step % n == 0)

    def tiles(self, s, fn):
        @pl.loop(0, self.step // self.small)
        def _(t):
            fn(pl.ds(pl.multiple_of(s * self.step + t * self.small, self.small), self.small))

    def send_x(self, k, s):
        for j in range(1, self.lo):
            self.xc[k, j, s].start()

    def add_and_send(self, k, s):
        for j in range(1, self.lo):
            self.xc[k, j, s].wait_recv()
        if k:

            def add(rs):
                v = self.g[k, rs, :].astype(f32)
                for j in range(1, self.lo):
                    v += self.xb[(j - 1) * self.hi + k, rs, :].astype(f32)
                self.g[k, rs, :] = v.astype(low_type)

            self.tiles(s, add)
            self.zc[k, s].start()

    def finish(self, out, squares):
        squares[...] = jnp.zeros_like(squares)
        for s in range(self.sub):
            for k in range(1, self.hi):
                self.zc[k, s].wait_recv()

            def add(rs):
                v = self.g[0, rs, :].astype(f32)
                for j in range(1, self.lo):
                    v += self.xb[(j - 1) * self.hi, rs, :].astype(f32)
                for k in range(1, self.hi):
                    v += self.zb[k - 1, rs, :].astype(f32)
                out[rs, :] = v
                squares[...] += jnp.sum((v * v).reshape(self.small // 8, 8, self.cols), axis=0)

            self.tiles(s, add)
        for c in self.xc.values():
            c.wait_send()
        for c in self.zc.values():
            c.wait_send()


class FoldQueue:
    def __init__(self, folds, window=WINDOW):
        self.order = [(f, k, s) for f in folds for k, s in f.items]
        self.have = set()
        self.window, self.started, self.done = window, 0, 0

    def ready(self, fold, j, k):
        self.have.add((id(fold), j, k))
        self.pump()

    def pump(self):
        while self.started < min(len(self.order), self.done + self.window):
            f, k, s = self.order[self.started]
            if any((id(f), j, k) not in self.have for j in range(1, f.lo)):
                return
            f.send_x(k, s)
            self.started += 1

    def advance(self, n=1):
        for _ in range(n):
            if self.done == self.started:
                return
            f, k, s = self.order[self.done]
            if (id(f), 0, k) not in self.have:
                return
            f.add_and_send(k, s)
            self.done += 1
            self.pump()

    def finish(self):
        self.advance(len(self.order))
        assert self.done == len(self.order)


def big(cid, remote_kernel=True):
    extra = {"collective_id": cid, "has_side_effects": True} if remote_kernel else {}
    return pltpu.CompilerParams(vmem_limit_bytes=62 * 2**20, **extra)


def cost(flops, bytes_accessed):
    return pl.CostEstimate(
        flops=int(flops), bytes_accessed=int(bytes_accessed), transcendentals=10**6
    )


def attention_call(
    tokens, out_grad, wq, wkv, wo, gains, gateup, down, segment, rates,
    heads, kv_heads, dp, mp, cid, eps
):
    rows, width = tokens.shape
    hd = rates.shape[1]
    blk, qcols = wq.shape
    kv_rows = wkv.shape[1]
    ff = down.shape[0]
    block = min(256, rows)
    scale = hd**-0.5
    share = rows // mp
    cols = qcols + 2 * hd
    late = {}
    gather = Gather(
        [(16, blk), wq.shape, (blk, 2 * hd), wo.shape], (0, 0, 0, 1), (1, 2, 1, 2), dp, late
    )
    n_g = len(gather.scratch())

    def kernel(tok_r, og_r, q_f, kv_f, wo_f, gn_f, gu_h, dn_h, sg_r, rt_r, *refs):
        (wqkv_o, wo_o, gain_o, og_h, x_o, a_h, inv_o, qo, ko, vo, ob_o, lse_o, gl_h, ul_h, dl_h) = (
            refs[:15]
        )
        c_r, s_r = refs[15:17]
        kvx, gall, xv, wv, bias, q_r, kv_r, wo_r, gn_r, ks, kr, cs_, ws = refs[17:30]
        og_o, a_o, gl_o, ul_o, dl_o, gu_r, dn_r, io = refs[30:38]
        g_s = refs[38:]
        loads = [
            pltpu.make_async_copy(gu_h, gu_r, io.at[0]),
            pltpu.make_async_copy(dn_h, dn_r, io.at[1]),
        ]
        for c in loads:
            c.start()
        stores = []

        def store(src, dst):
            c = pltpu.make_async_copy(src, dst, io.at[2 + len(stores)])
            c.start()
            stores.append(c)

        place = Place(dp, mp)
        copies = []
        for j in range(place.lo):
            for k in range(place.hi):
                r = j * place.hi + k
                at = pl.ds(pl.multiple_of(place.owner(j, k) * blk, 128), blk)
                to = pl.ds(r * blk, blk)
                copies.append(pltpu.make_async_copy(tok_r.at[:, at], xv.at[:, to], cs_.at[0, r]))
                copies.append(
                    pltpu.make_async_copy(og_r.at[:, at], og_o.at[:, to], cs_.at[1, r])
                )
        for c in copies:
            c.start()
        gn_r[...] = jnp.zeros_like(gn_r)
        gn_r[:2, :] = gn_f[...].astype(low_type)
        q_r[...] = q_f[...].astype(low_type)
        for n in range(kv_heads):
            for i in range(2):
                kv_r[:, (2 * n + i) * hd : (2 * n + i + 1) * hd] = kv_f[
                    i, :, n * hd : (n + 1) * hd
                ].astype(low_type)
        wo_r[...] = wo_f[...].astype(low_type)
        place.barrier()
        here = pl.ds(pl.multiple_of(place.m * kv_rows, kv_rows), kv_rows)
        swaps = []
        for n, m in place.others_mp():
            head = m * kv_heads // mp
            c = remote(
                kv_r.at[:, pl.ds(pl.multiple_of(head * 2 * hd, 128), 2 * hd)],
                kvx.at[here],
                ks.at[n],
                kr.at[n],
                {"mp": m},
            )
            c.start()
            swaps.append(c)
        head = place.m * kv_heads // mp
        mine = pltpu.make_async_copy(
            kv_r.at[:, pl.ds(pl.multiple_of(head * 2 * hd, 128), 2 * hd)], kvx.at[here], ks.at[0]
        )
        mine.start()

        def swapped():
            mine.wait()
            for c in swaps:
                c.wait_recv()

        late[3] = swapped
        late[4] = late[5] = lambda: None
        gather.bind(
            place,
            (gn_r, q_r, kvx, wo_r),
            (gall, wqkv_o.at[:, pl.ds(0, qcols)], wqkv_o.at[:, pl.ds(qcols, 2 * hd)], wo_o),
            g_s,
        )
        gather.begin()
        for c in loads:
            c.wait()

        @pl.loop(0, blk // 32)
        def _(t):
            rs = pl.ds(pl.multiple_of(t * 32, 32), 32)
            gl_o[rs, :] = gu_r[0, rs, :].astype(low_type)
            ul_o[rs, :] = gu_r[1, rs, :].astype(low_type)

        dl_o[...] = dn_r[...].T.astype(low_type)
        store(gl_o, gl_h)
        store(ul_o, ul_h)
        store(dl_o, dl_h)
        gather.step(2 * (gather.hi - 1))
        length = sequence_length(sg_r[...], rows)

        @pl.loop(0, rows // 128)
        def _(t):
            at = pl.multiple_of(t * 128, 128)
            row = at + lax.broadcasted_iota(jnp.int32, (128, 1), 0)
            angle = (row & (length - 1)).astype(f32) * rt_r[...]
            lane = lax.broadcasted_iota(jnp.int32, (128, hd), 1)
            c_r[pl.ds(at, 128), :] = jnp.cos(angle)
            sn = jnp.sin(angle)
            s_r[pl.ds(at, 128), :] = jnp.where(lane < hd // 2, -sn, sn)

        for c in copies:
            c.wait()
        store(og_o, og_h)
        own = place.m * share

        @pl.loop(0, share // 32)
        def _(t):
            at = pl.multiple_of(t * 32, 32)
            v = xv[pl.ds(pl.multiple_of(own + at, 32), 32), :]
            x_o[pl.ds(at, 32), :] = v
            v = v.astype(f32)
            inv = lax.rsqrt(jnp.mean(v * v, axis=-1, keepdims=True) + eps)
            inv_o[pl.ds(at, 32), :] = jnp.broadcast_to(inv, (32, 128))

        gather.arrive(0)
        for c in (1, 2, 3):
            gather.arrive(c)
        wcopy = pltpu.make_async_copy(wqkv_o, wv, ws.at[0])
        wcopy.start()
        for r in range(dp):
            at = r * 16
            gain_o[:, r * blk : (r + 1) * blk] = gall[at : at + 8, :].astype(f32)
        wcopy.wait()
        gain = gain_o[:1, :]
        half = rows // 128 // 2
        for q in range(2):

            @pl.loop(q * half, (q + 1) * half)
            def _(t):
                rs = pl.ds(pl.multiple_of(t * 128, 128), 128)
                v = xv[rs, :].astype(f32)
                inv = lax.rsqrt(jnp.mean(v * v, axis=-1, keepdims=True) + eps)
                a = (v * inv * gain).astype(low_type)
                a_o[rs, :] = a
                raw = jnp.dot(a, wv[...], preferred_element_type=f32)
                cs, sn = c_r[rs, :], s_r[rs, :]
                for n in range(heads):
                    u = raw[:, n * hd : (n + 1) * hd]
                    qo[rs, n * hd : (n + 1) * hd] = (
                        u * cs + pltpu.roll(u, hd // 2, 1) * sn
                    ).astype(low_type)
                u = raw[:, qcols : qcols + hd]
                ko[rs, :] = (u * cs + pltpu.roll(u, hd // 2, 1) * sn).astype(low_type)
                vo[rs, :] = raw[:, qcols + hd :].astype(low_type)

            done = pl.ds(q * half * 128, half * 128)
            store(a_o.at[done, :], a_h.at[done, :])
            gather.step(1)

        for q in range(rows // block):
            rs = pl.ds(q * block, block)
            keys = (q + 1) * block
            bias[:, :keys] = attention_bias(length, q * block, block, keys)
            lane = lax.broadcasted_iota(jnp.int32, (block, 128), 1)
            lse = jnp.zeros((block, 128), f32)
            for n in range(heads):
                hs = slice(n * hd, (n + 1) * hd)
                s = lax.dot_general(qo[rs, hs], ko[:keys, :], NT, preferred_element_type=f32)
                s = s * scale + bias[:, :keys]
                top = jnp.max(s, axis=-1, keepdims=True)
                e = jnp.exp(s - top)
                total = jnp.sum(e, axis=-1, keepdims=True)
                p = (e * (1.0 / total)).astype(low_type)
                ob_o[rs, hs] = jnp.dot(p, vo[:keys, :], preferred_element_type=f32).astype(
                    low_type
                )
                lse = jnp.where(lane == n, top + jnp.log(total), lse)
            lse_o[rs, :] = lse
            gather.step(1)
        gather.finish()
        for c in swaps:
            c.wait_send()
        for c in stores:
            c.wait()

    sds = jax.ShapeDtypeStruct
    return pl.pallas_call(
        kernel,
        name="attention_forward",
        out_shape=[
            sds((width, cols), low_type),
            sds((qcols, width), low_type),
            sds((8, width), f32),
            sds((rows, width), low_type),
            sds((share, width), low_type),
            sds((rows, width), low_type),
            sds((share, 128), f32),
            sds((rows, qcols), low_type),
            sds((rows, hd), low_type),
            sds((rows, hd), low_type),
            sds((rows, qcols), low_type),
            sds((rows, 128), f32),
            sds((blk, ff), low_type),
            sds((blk, ff), low_type),
            sds((blk, ff), low_type),
            sds((rows, hd), f32),
            sds((rows, hd), f32),
        ],
        in_specs=[HBM] * 2 + [VM] * 4 + [HBM] * 2 + [VM] * 2,
        out_specs=[HBM, HBM, VM, HBM, VM, HBM] + [VM] * 6 + [HBM] * 3 + [VM] * 2,
        scratch_shapes=[
            pltpu.VMEM((blk, 2 * hd), low_type),
            pltpu.VMEM((16 * dp, blk), low_type),
            pltpu.VMEM((rows, width), low_type),
            pltpu.VMEM((width, cols), low_type),
            pltpu.VMEM((block, rows), f32),
            pltpu.VMEM((blk, qcols), low_type),
            pltpu.VMEM((kv_rows, kv_heads * 2 * hd), low_type),
            pltpu.VMEM(wo.shape, low_type),
            pltpu.VMEM((16, blk), low_type),
            DMA((mp,)),
            DMA((mp,)),
            DMA((2, dp)),
            DMA((1,)),
            pltpu.VMEM((rows, width), low_type),
            pltpu.VMEM((rows, width), low_type),
            pltpu.VMEM((blk, ff), low_type),
            pltpu.VMEM((blk, ff), low_type),
            pltpu.VMEM((blk, ff), low_type),
            pltpu.VMEM(gateup.shape, f32),
            pltpu.VMEM(down.shape, f32),
            DMA((8,)),
        ]
        + gather.scratch(),
        compiler_params=big(cid),
        cost_estimate=cost(6e9, 2e7),
    )(tokens, out_grad, wq, wkv, wo, gains, gateup, down, segment, rates)


def put_natural(place, ref, rows, value, blk):
    for j in range(place.lo):
        for k in range(place.hi):
            owner = place.owner(j, k)
            r = j * place.hi + k
            ref[rows, pl.ds(pl.multiple_of(owner * blk, 128), blk)] = value[
                :, r * blk : (r + 1) * blk
            ]


def mlp_back_call(hid, og, act, ga, ub, wd, wg, wu, h_own, inv_own, gain, dp, mp, cid):
    rows, ff = hid.shape
    width = og.shape[1]
    blk = width // dp
    folds = [Fold(blk, ff, dp, 2), Fold(blk, ff, dp, 2)]
    rsum, spread = RowSum(rows, width, mp), Spread(rows, mp, 2)
    share, tile = rsum.share, rsum.tile
    n_f, n_r = len(folds[0].scratch()), len(rsum.scratch())

    def kernel(
        hid_r, og_r, act_r, ga_r, ub_r, wd_r, wg_r, wu_r, h_r, inv_r, gn_r, *refs
    ):
        g_r = gn_r.at[pl.ds(1, 1), :]
        (down_o, dsq_o, gate_o, gsq_o, du_o, dh_h, dhb_h, gg_o) = refs[:8]
        pb, ogx, dg, du, wbuf, dh_o, dhb_o, ls, ws, wd_s = refs[8:18]
        at = 18
        for f in folds:
            f_refs = refs[at : at + n_f]
            at += n_f
            f.refs = f_refs
        r_s = refs[at : at + n_r]
        p_s = refs[at + n_r :]
        place = Place(dp, mp)
        own = pl.multiple_of(place.m * share, 8)
        load_og = pltpu.make_async_copy(og_r, pb, ls.at[0])
        load_hid = pltpu.make_async_copy(hid_r, dg, ls.at[1])
        load_ub = pltpu.make_async_copy(ub_r, du, ls.at[2])
        load_own = pltpu.make_async_copy(og_r.at[pl.ds(own, share), :], ogx, ls.at[3])
        load_ga = pltpu.make_async_copy(ga_r, dg, ls.at[4])
        load_act = pltpu.make_async_copy(act_r, pb, ls.at[5])
        store_du = pltpu.make_async_copy(du, du_o, ls.at[6])
        tiles = rsum.tiles
        load_wd = [
            pltpu.make_async_copy(
                wd_r.at[pl.ds(t * tile, tile), :], wbuf.at[t // 2, t % 2], wd_s.at[t]
            )
            for t in range(tiles)
        ]

        def fetch(t):
            rs = pl.ds(t * tile, tile)
            return [
                pltpu.make_async_copy(w.at[rs, :], wbuf.at[t % 2, i], ws.at[t, i])
                for i, w in enumerate((wg_r, wu_r))
            ]

        for c in [load_og, load_hid, load_ub, load_own] + load_wd:
            c.start()
        place.barrier()
        for f in folds:
            f.bind(place, f.refs)
        rsum.bind(place, r_s)
        spread.bind(place, p_s, dhb_o)
        load_og.wait()
        load_hid.wait()
        first, second = folds
        queue = FoldQueue(folds)
        for j, k in first.blocks:
            r = j * first.hi + k
            first.g[r] = jnp.dot(
                pb[:, r * blk : (r + 1) * blk].T, dg[...], preferred_element_type=f32
            ).astype(low_type)
            queue.ready(first, j, k)
        load_ga.start()
        for c in load_wd + [load_ub, load_ga]:
            c.wait()
        groups = 4
        per = rows // 128 // groups
        for q in range(groups):

            @pl.loop(q * per, (q + 1) * per)
            def _(n):
                rs = pl.ds(pl.multiple_of(n * 128, 128), 128)
                d = jnp.dot(pb[rs, :tile], wbuf[0, 0], preferred_element_type=f32)
                for t in range(1, tiles):
                    d += jnp.dot(
                        pb[rs, t * tile : (t + 1) * tile],
                        wbuf[t // 2, t % 2],
                        preferred_element_type=f32,
                    )
                dg[rs, :] = (d * dg[rs, :].astype(f32)).astype(low_type)
                du[rs, :] = (d * du[rs, :].astype(f32)).astype(low_type)

            if q > 0:
                queue.advance()
        store_du.start()
        load_act.start()
        for c in fetch(0):
            c.start()

        def before(t):
            for c in fetch(t):
                c.wait()
            if t + 1 < tiles:
                for c in fetch(t + 1):
                    c.start()

        def partial(start, count, t, n):
            rs = pl.ds(start, count)
            return lax.dot_general(
                dg[rs, :], wbuf[t % 2, 0], NT, preferred_element_type=f32
            ) + lax.dot_general(du[rs, :], wbuf[t % 2, 1], NT, preferred_element_type=f32)

        rsum.scatter(partial, before, queue.advance)
        load_act.wait()
        for n, (j, k) in enumerate(second.blocks):
            r = j * second.hi + k
            second.g[r] = jnp.dot(
                pb[:, r * blk : (r + 1) * blk].T, dg[...], preferred_element_type=f32
            ).astype(low_type)
            queue.ready(second, j, k)
        load_own.wait()
        read = rsum.arrive()
        gg_o[...] = jnp.zeros_like(gg_o)
        for r in range(spread.parts):

            @pl.loop(0, spread.step // 32)
            def _(t):
                at = pl.multiple_of(r * spread.step + t * 32, 32)
                rs = pl.ds(at, 32)
                v, h = read(at, 32), h_r[rs, :]
                inv = inv_r[rs, :1]
                weighted = v * g_r[...]
                mean = jnp.mean(weighted * h, axis=-1, keepdims=True)
                dh = ogx[rs, :].astype(f32) + inv * weighted - h * (inv * inv * inv * mean)
                dh_o[rs, :] = dh
                dhb_o[pl.ds(pl.multiple_of(own + at, 32), 32), :] = dh.astype(low_type)
                gg_o[...] += jnp.sum((v * h * inv).reshape(4, 8, width), axis=0)

            spread.send(r)
            queue.advance()
        store_dh = pltpu.make_async_copy(dh_o, dh_h, ls.at[7])
        store_dh.start()
        for r in range(spread.parts):
            spread.forward(r)
            queue.advance()
        spread.finish()
        store_dhb = pltpu.make_async_copy(dhb_o, dhb_h, ls.at[8])
        store_dhb.start()
        queue.advance(len(first.items) + len(second.items) // 2 - queue.done)
        first.finish(gate_o, dsq_o)
        down_o[...] = gate_o[...].T
        queue.finish()
        second.finish(gate_o, gsq_o)
        rsum.finish()
        for c in (store_du, store_dh, store_dhb):
            c.wait()

    sds = jax.ShapeDtypeStruct
    square = sds((8, ff), f32)
    return pl.pallas_call(
        kernel,
        name="mlp_backward",
        out_shape=[
            sds((ff, blk), f32),
            square,
            sds((blk, ff), f32),
            square,
            sds((rows, ff), low_type),
            sds((share, width), f32),
            sds((rows, width), low_type),
            sds((8, width), f32),
        ],
        in_specs=[HBM] * 8 + [VM] * 3,
        out_specs=[VM] * 4 + [HBM] * 3 + [VM],
        scratch_shapes=[
            pltpu.VMEM((rows, width), low_type),
            pltpu.VMEM((share, width), low_type),
            pltpu.VMEM((rows, ff), low_type),
            pltpu.VMEM((rows, ff), low_type),
            pltpu.VMEM((2, 2, tile, ff), low_type),
            pltpu.VMEM((share, width), f32),
            pltpu.VMEM((rows, width), low_type),
            DMA((9,)),
            DMA((rsum.tiles, 2)),
            DMA((rsum.tiles,)),
        ]
        + folds[0].scratch()
        + folds[1].scratch()
        + rsum.scratch()
        + spread.scratch(),
        compiler_params=big(cid),
        cost_estimate=cost(4e10, 1e8),
    )(hid, og, act, ga, ub, wd, wg, wu, h_own, inv_own, gain)


def attention_back_call(
    act, du, hid, wd, dhb, wqkv, a1, h_own, wo, q, k, v, lse, cosine, sine, segment,
    ob, x_own, inv_own, dh_own, gain, gain_two, squares, heads, kv_heads, dp, mp, cid
):
    rows, width = act.shape
    ff = du.shape[1]
    hd = cosine.shape[1]
    qcols, cols = heads * hd, wqkv.shape[1]
    blk = width // dp
    kv_rows, wide = blk // mp, cols - qcols
    block = min(256, rows)
    scale = hd**-0.5
    folds = [Fold(blk, ff, dp, 2), Fold(qcols, blk, dp, 2), Fold(blk, cols, dp, 2)]
    rsum = RowSum(rows, width, mp)
    spreads = [Spread(rows, mp, 2), Spread(rows, mp, 2)]
    share, tile, tiles = rsum.share, rsum.tile, rsum.tiles
    n_f, n_r, n_s = len(folds[0].scratch()), len(rsum.scratch()), len(spreads[0].scratch())
    n_sq = len(squares)
    local = [m * kv_heads // mp for m in range(mp)]
    shared = mp > kv_heads

    def kernel(
        act_r, du_r, hid_r, wd_r, dhb_r, wqkv_r, a_r, h_h, wo_h, q_r, k_r, v_r, l_h, c_h, s_h,
        sg_r, ob_h, x_h, inv_r, dh_h, gn_r, g2_r, *refs
    ):
        sq_r, refs = refs[:n_sq], refs[n_sq:]
        staged, refs = refs[-9:], refs[:-9]
        h_r, wo_r, l_r, c_r, s_r, ob_r, x_r, dh_r, st = staged
        g_r = gn_r.at[pl.ds(0, 1), :]
        stage = [
            pltpu.make_async_copy(a, b, st.at[n])
            for n, (a, b) in enumerate(
                zip((h_h, wo_h, l_h, c_h, s_h, ob_h, x_h, dh_h), staged[:8])
            )
        ]
        up_o, q_o, wo_o, kv_o, y_o, in_o, gain_o, tot_o = refs[:8]
        (pb, db, wbuf, bias, dk, dv, out, y_own, in_own, sq0, sq1, sq2, obt) = refs[8:21]
        (gg, mine, got, sent, got2, t1, t2, ls, ws, gm, gd, ts, credit) = refs[21:34]
        at = 34
        place = Place(dp, mp)
        me_dp, me_mp = lax.axis_index("dp"), place.m
        own = pl.multiple_of(place.m * share, 8)
        load_act = pltpu.make_async_copy(act_r, pb, ls.at[0])
        load_du = pltpu.make_async_copy(du_r, db, ls.at[1])
        load_dhb = pltpu.make_async_copy(dhb_r, pb, ls.at[2])
        load_hid = pltpu.make_async_copy(hid_r, db, ls.at[3])
        load_a = pltpu.make_async_copy(a_r, pb, ls.at[4])
        keeps = [
            pltpu.make_async_copy(o, full.at[pl.ds(own, share), :], ls.at[5 + n])
            for n, (o, full) in enumerate(((y_own, y_o), (in_own, in_o)))
        ]

        def fetch(t):
            return pltpu.make_async_copy(
                wd_r.at[pl.ds(t * tile, tile), :], wbuf.at[t % 2], ws.at[0, t]
            )

        def fetch_qkv(t):
            return pltpu.make_async_copy(
                wqkv_r.at[pl.ds(t * tile, tile), :],
                wbuf.at[t % 2, :, pl.ds(0, cols)],
                ws.at[1, t],
            )

        load_act.start()
        load_du.start()
        fetch(0).start()
        for c in stage:
            c.start()
        place.barrier()
        for f in folds:
            f.bind(place, refs[at : at + n_f])
            at += n_f
        rsum.bind(place, refs[at : at + n_r])
        at += n_r
        for p, o, full in zip(spreads, (y_own, in_own), (y_o, in_o)):
            p.bind(place, refs[at : at + n_s], full, o)
            at += n_s
        up, wof, qkvf = folds
        spread_y, spread_in = spreads
        queue = FoldQueue(folds)
        advance = queue.advance

        load_act.wait()
        load_du.wait()
        for j, kk in up.blocks:
            r = j * up.hi + kk
            up.g[r] = jnp.dot(
                pb[:, r * blk : (r + 1) * blk].T, db[...], preferred_element_type=f32
            ).astype(low_type)
            queue.ready(up, j, kk)
        load_hid.start()
        load_dhb.start()
        for c in stage:
            c.wait()
        load_hid.wait()

        def before(t):
            fetch(t).wait()
            if t + 1 < tiles:
                fetch(t + 1).start()

        def partial_y(start, count, t, n):
            return lax.dot_general(
                db[pl.ds(start, count), :], wbuf[t % 2], NT, preferred_element_type=f32
            )

        rsum.scatter(partial_y, before)
        fetch_qkv(0).start()
        advance()
        for n in range(qcols // 128):
            obt[n * 128 : (n + 1) * 128, :] = ob_r[:, n * 128 : (n + 1) * 128].T
        load_dhb.wait()
        for j, kk in wof.blocks:
            r = j * wof.hi + kk
            wof.g[r] = jnp.dot(
                obt[...], pb[:, r * blk : (r + 1) * blk], preferred_element_type=f32
            ).astype(low_type)
            queue.ready(wof, j, kk)
        advance()
        dk[...] = jnp.zeros_like(dk)
        dv[...] = jnp.zeros_like(dv)
        length = sequence_length(sg_r[...], rows)
        count = rows // block
        for b in range(count):
            rs = pl.ds(b * block, block)
            keys = (b + 1) * block
            ks = slice(0, keys)
            bias[:, ks] = attention_bias(length, b * block, block, keys)
            do = lax.dot_general(pb[rs, :], wo_r[...], NT, preferred_element_type=f32).astype(
                low_type
            )
            cs, sn = c_r[rs, :], s_r[rs, :]
            for n in range(heads):
                hs = slice(n * hd, (n + 1) * hd)
                qb = q_r[rs, hs]
                s = lax.dot_general(qb, k_r[ks, :], NT, preferred_element_type=f32)
                p = jnp.exp(s * scale + bias[:, ks] - l_r[rs, n : n + 1])
                dpr = lax.dot_general(do[:, hs], v_r[ks, :], NT, preferred_element_type=f32)
                centre = jnp.sum(p * dpr, axis=-1, keepdims=True)
                ds = (p * (dpr - centre)).astype(low_type)
                u = jnp.dot(ds, k_r[ks, :], preferred_element_type=f32) * scale
                out[rs, hs] = (u * cs - pltpu.roll(u, hd // 2, 1) * sn).astype(low_type)
                dk[ks, :] += lax.dot_general(ds, qb, TN, preferred_element_type=f32)
                dv[ks, :] += lax.dot_general(
                    p.astype(low_type), do[:, hs], TN, preferred_element_type=f32
                )
            if b == count // 2:
                read_y = rsum.arrive()

                @pl.loop(0, share // 32)
                def _(t):
                    rt = pl.ds(pl.multiple_of(t * 32, 32), 32)
                    y = (h_r[rt, :] + read_y(t * 32, 32)).astype(low_type)
                    put_natural(place, y_own, rt, y, blk)

                for r in range(spread_y.parts):
                    spread_y.send(r)
                keeps[0].start()
                rsum.finish()
                rsum.free(credit)
            advance()
        load_a.start()
        u = dk[...] * scale
        out[:, qcols : qcols + hd] = (
            u * c_r[...] - pltpu.roll(u, hd // 2, 1) * s_r[...]
        ).astype(low_type)
        out[:, qcols + hd :] = dv[...].astype(low_type)

        def before_in(t):
            fetch_qkv(t).wait()
            if t + 1 < tiles:
                fetch_qkv(t + 1).start()

        def partial_in(start, count, t, n):
            return lax.dot_general(
                out[pl.ds(start, count), :],
                wbuf[t % 2, :, :cols],
                NT,
                preferred_element_type=f32,
            )

        rsum.freed(credit)
        rsum.scatter(partial_in, before_in)
        advance()
        load_a.wait()
        for n, (j, kk) in enumerate(qkvf.blocks):
            r = j * qkvf.hi + kk
            qkvf.g[r] = jnp.dot(
                pb[:, r * blk : (r + 1) * blk].T, out[...], preferred_element_type=f32
            ).astype(low_type)
            queue.ready(qkvf, j, kk)
            if n % 4 == 3:
                advance()
        for r in range(spread_y.parts):
            spread_y.forward(r)
            advance(2)
        advance(2)
        read = rsum.arrive()
        gg[...] = jnp.zeros_like(gg)

        @pl.loop(0, share // 32)
        def _(t):
            rs = pl.ds(pl.multiple_of(t * 32, 32), 32)
            g, x = read(t * 32, 32), x_r[rs, :].astype(f32)
            inv = inv_r[rs, :1]
            weighted = g * g_r[...]
            mean = jnp.mean(weighted * x, axis=-1, keepdims=True)
            d = dh_r[rs, :] + inv * weighted - x * (inv * inv * inv * mean)
            put_natural(place, in_own, rs, d.astype(low_type), blk)
            gg[...] += jnp.sum((g * x * inv).reshape(4, 8, width), axis=0)

        mine[...] = jnp.zeros_like(mine)
        mine[0:1, :] = jnp.sum(gg[...], axis=0, keepdims=True)
        mine[1:2, :] = jnp.sum(g2_r[...], axis=0, keepdims=True)
        got[place.m] = mine[...]
        gains_mp = []
        for n, m in place.others_mp():
            c = remote(mine, got.at[place.m], gm.at[0, n], gm.at[1, n], {"mp": m})
            c.start()
            gains_mp.append(c)
        for r in range(spread_in.parts):
            spread_in.send(r)
        keeps[1].start()
        advance(4)
        for c in gains_mp:
            c.wait()
        g = got[0]
        for n in range(1, mp):
            g += got[n]
        for r in range(dp):
            sent[r] = g[:, r * blk : (r + 1) * blk]
        gains_dp = []
        for r, d in place.others_dp():
            c = remote(sent.at[r], got2.at[r], gd.at[0, r], gd.at[1, r], {"dp": d})
            c.start()
            gains_dp.append(c)
        advance(2)
        for r in range(spread_in.parts):
            spread_in.forward(r)
            advance(1)
        advance(len(up.items) + len(wof.items) + len(qkvf.items) // 2 - queue.done)
        up.finish(up_o, sq0)
        queue.finish()
        for c in gains_dp:
            c.wait()
        g = sent[0]
        for r in range(1, dp):
            g += got2[r]
        gain_o[...] = g
        g = whole(g * g)
        total = jnp.where(me_mp == 0, g, jnp.zeros_like(g))
        for a in sq_r:
            total += whole(a[...])
        wof.finish(wo_o, sq1)
        total += whole(sq0[...]) + whole(sq1[...])
        qkv = rsum.acc.at[pl.ds(0, blk), pl.ds(0, cols)]
        qkvf.finish(qkv, sq2)
        swaps = []
        for n, m in place.others_mp():
            c = remote(
                qkv.at[pl.ds(pl.multiple_of(m * kv_rows, 8), kv_rows), pl.ds(qcols, wide)],
                kv_o.at[me_mp],
                ts.at[0, n],
                ts.at[1, n],
                {"mp": m},
            )
            c.start()
            swaps.append(c)
        kv_o[me_mp] = qkv[pl.ds(pl.multiple_of(me_mp * kv_rows, 8), kv_rows), qcols:]
        if shared:
            total += whole(sq2[:, :qcols])
            for c in swaps:
                c.wait_recv()
            for h in range(kv_heads):
                of = [m for m in range(mp) if local[m] == h]
                g = kv_o[of[0]]
                for m in of[1:]:
                    g += kv_o[m]
                total += whole(g * g)
        else:
            total += whole(sq2[...])
        for peers, table, me, base in (
            ([(n, {"mp": m}) for n, m in place.others_mp()], t1, me_mp, 2),
            ([(n, {"dp": d}) for n, d in place.others_dp()], t2, me_dp, 4),
        ):
            table[me] = jnp.broadcast_to(total, (8, 128))
            waits = []
            for n, to in peers:
                c = remote(table.at[me], table.at[me], ts.at[base, n], ts.at[base + 1, n], to)
                c.start()
                waits.append(c)
            if base == 2:
                q_o[...] = qkv[:, :qcols]
            for c in waits:
                c.wait()
            total = table[0]
            for n in range(1, len(peers) + 1):
                total += table[n]
        tot_o[...] = total
        for c in swaps:
            if shared:
                c.wait_send()
            else:
                c.wait()
        rsum.finish()
        for p, c in zip(spreads, keeps):
            p.finish()
            c.wait()

    sds = jax.ShapeDtypeStruct
    scratch = []
    for part in folds + [rsum] + spreads:
        scratch += part.scratch()
    staged = (h_own, wo, lse, cosine, sine, ob, x_own, dh_own)
    scratch += [pltpu.VMEM(a.shape, a.dtype) for a in staged] + [DMA((len(staged),))]
    return pl.pallas_call(
        kernel,
        name="attention_backward",
        out_shape=[
            sds((blk, ff), f32),
            sds((blk, qcols), f32),
            sds((qcols, blk), f32),
            sds((mp, kv_rows, wide), f32),
            sds((rows, width), low_type),
            sds((rows, width), low_type),
            sds((8, blk), f32),
            sds((8, 128), f32),
        ],
        in_specs=[HBM] * 9
        + [VM] * 3
        + [HBM] * 3
        + [VM]
        + [HBM] * 2
        + [VM, HBM]
        + [VM] * (2 + n_sq),
        out_specs=[VM] * 4 + [HBM] * 2 + [VM] * 2,
        scratch_shapes=[
            pltpu.VMEM((rows, width), low_type),
            pltpu.VMEM((rows, ff), low_type),
            pltpu.VMEM((2, tile, max(ff, cols)), low_type),
            pltpu.VMEM((block, rows), f32),
            pltpu.VMEM((rows, hd), f32),
            pltpu.VMEM((rows, hd), f32),
            pltpu.VMEM((rows, cols), low_type),
            pltpu.VMEM((share, width), low_type),
            pltpu.VMEM((share, width), low_type),
            pltpu.VMEM((8, ff), f32),
            pltpu.VMEM((8, blk), f32),
            pltpu.VMEM((8, cols), f32),
            pltpu.VMEM((qcols, rows), low_type),
            pltpu.VMEM((8, width), f32),
            pltpu.VMEM((8, width), f32),
            pltpu.VMEM((mp, 8, width), f32),
            pltpu.VMEM((dp, 8, blk), f32),
            pltpu.VMEM((dp, 8, blk), f32),
            pltpu.VMEM((mp, 8, 128), f32),
            pltpu.VMEM((dp, 8, 128), f32),
            DMA((7,)),
            DMA((2, tiles)),
            DMA((2, mp)),
            DMA((2, dp)),
            DMA((6, max(dp, mp))),
            pltpu.SemaphoreType.REGULAR,
        ]
        + scratch,
        compiler_params=big(cid),
        cost_estimate=cost(4e10, 1e8),
    )(
        act, du, hid, wd, dhb, wqkv, a1, h_own, wo, q, k, v, lse, cosine, sine, segment,
        ob, x_own, inv_own, dh_own, gain, gain_two, *squares
    )


def whole(v):
    return jnp.sum(jnp.sum(v, axis=0, keepdims=True), axis=1, keepdims=True)


def update_call(total, widen, keep, groups):
    steps = 4
    count = len(groups)

    def split(shape):
        return shape[-2] % (steps * 8) == 0 and shape[-2] >= 128

    def spec(shape, cut):
        lead = len(shape) - 2
        rows = shape[-2] // steps if cut else shape[-2]
        return pl.BlockSpec(
            shape[:-2] + (rows, shape[-1]), lambda i: (0,) * lead + (i if cut else 0, 0)
        )

    ins, in_specs, outs, out_specs, kinds = [], [], [], [], []
    for weight, moment, square, grads, rate, decay in groups:
        cut = split(weight.shape)
        ins += [weight, moment, square] + grads
        in_specs += [spec(weight.shape, cut)] * 3 + [spec(g.shape, cut) for g in grads]
        outs += [jax.ShapeDtypeStruct(weight.shape, f32)] * 3
        out_specs += [spec(weight.shape, cut)] * 3
        kinds.append((len(grads), rate, decay))

    wide_spec = pl.BlockSpec((widen.shape[0] // steps, widen.shape[1]), lambda i: (i, 0))
    outs += [
        jax.ShapeDtypeStruct((1, 1), f32),
        jax.ShapeDtypeStruct(keep.shape, keep.dtype),
        jax.ShapeDtypeStruct(widen.shape, f32),
    ]
    out_specs += [pl.BlockSpec((1, 1), lambda i: (0, 0)), wide_spec, wide_spec]

    def kernel(tot_r, wide_r, keep_r, *refs):
        out_refs = refs[len(ins) :]
        out_refs[-1][...] = wide_r[...].astype(f32)
        out_refs[-2][...] = keep_r[...]
        norm = jnp.sqrt(tot_r[:1, :1])
        out_refs[-3][...] = norm
        factor = jnp.minimum(1.0, clip_limit / (norm + 1e-06))
        at = 0
        for n, (parts, rate, decay) in enumerate(kinds):
            w_r, m_r, s_r = refs[at : at + 3]
            g_rs = refs[at + 3 : at + 3 + parts]
            at += 3 + parts
            w_o, m_o, s_o = out_refs[3 * n : 3 * n + 3]

            def one(index, gradient):
                new = adam_update(
                    w_r[index], m_r[index], s_r[index], gradient, factor, rate, decay
                )
                w_o[index], m_o[index], s_o[index] = new

            if parts == 1 and g_rs[0].shape == w_r.shape:
                one(..., g_rs[0][...])
            elif parts == 1 and g_rs[0].ndim == 3:
                copies, _, wide = g_rs[0].shape
                hd = wide // 2
                heads = w_r.shape[2] // hd
                for h in range(heads):
                    v = None
                    for m in range(copies):
                        if m * heads // copies == h:
                            v = g_rs[0][m] if v is None else v + g_rs[0][m]
                    for i in range(2):
                        index = (i, slice(None), slice(h * hd, (h + 1) * hd))
                        one(index, v[:, i * hd : (i + 1) * hd])
            elif parts == 1:
                one(..., g_rs[0][: w_r.shape[0], :])
            else:
                for i in range(parts):
                    one(i, g_rs[i][...])

    return pl.pallas_call(
        kernel,
        name="update",
        grid=(steps,),
        out_shape=outs,
        in_specs=[pl.BlockSpec((8, 128), lambda i: (0, 0)), wide_spec, wide_spec] + in_specs,
        out_specs=out_specs,
        compiler_params=pltpu.CompilerParams(vmem_limit_bytes=61 * 2**20),
        cost_estimate=cost(3e7, 4e7),
    )(total, widen, keep, *ins)


def body(
    tokens,
    segment_ids,
    out_grad,
    query_weight,
    keyval_weight,
    output_weight,
    gateup_weight,
    down_weight,
    norm_gains,
    query_moment,
    keyval_moment,
    output_moment,
    gateup_moment,
    down_moment,
    gains_moment,
    query_square,
    keyval_square,
    output_square,
    gateup_square,
    down_square,
    gains_square,
):
    dp = lax.axis_size("dp")
    mp = lax.axis_size("mp")
    heads = H // mp
    rows = tokens.shape[0]
    blk = D // dp
    qcols = query_weight.shape[1]

    half = np.arange(HD // 2, dtype=np.float64) * 2.0 / HD
    rates = jnp.asarray(np.tile(rope_base**-half, 2)[None].astype(np.float32))
    segment = segment_ids.reshape(-1, 128)
    (
        wqkv, wo, gains, og, x_own, act_one, inv_one, q, k, v, attn, lse, gate_low, up_low, down_low,
        cosine, sine,
    ) = attention_call(
        tokens, out_grad, query_weight, keyval_weight, output_weight, norm_gains,
        gateup_weight, down_weight, segment, rates, heads, KV, dp, mp, 0, norm_eps,
    )
    wg, wu, wd, h_own, inv_two, act_two, hid, ga, ub = forward_call(
        attn, wo, x_own, gains, gate_low, up_low, down_low, dp, mp, 1, norm_eps
    )
    down_share, down_sq, gate_share, gate_sq, du, dh_own, dhb, gain_two_part = mlp_back_call(
        hid, og, act_two, ga, ub, wd, wg, wu, h_own, inv_two, gains, dp, mp, 2
    )
    (
        up_share, query_share, output_share, kv_parts, layer_out, in_low, gains_share, total
    ) = attention_back_call(
        act_two, du, hid, wd, dhb, wqkv, act_one, h_own, wo, q, k, v, lse, cosine, sine, segment,
        attn, x_own, inv_one, dh_own, gains, gain_two_part, [down_sq, gate_sq],
        heads, KV, dp, mp, 3,
    )
    output_rate = matrix_rate * (TOK_DEV * D / (16.0 * H * HD)) ** 0.5
    *news, grad_norm, layer_out, input_grad = update_call(
        total,
        in_low,
        layer_out,
        [
            (query_weight, query_moment, query_square, [query_share], matrix_rate, weight_decay),
            (keyval_weight, keyval_moment, keyval_square, [kv_parts], matrix_rate, weight_decay),
            (
                output_weight, output_moment, output_square, [output_share],
                output_rate, weight_decay,
            ),
            (
                gateup_weight, gateup_moment, gateup_square, [gate_share, up_share],
                matrix_rate, weight_decay,
            ),
            (down_weight, down_moment, down_square, [down_share], matrix_rate, weight_decay),
            (norm_gains, gains_moment, gains_square, [gains_share], gain_rate, 0.0),
        ],
    )
    return (layer_out, input_grad, grad_norm.reshape(())) + tuple(news[0::3] + news[1::3] + news[2::3])


def solution(mesh):
    params = (
        P("dp", "mp"),
        P(None, ("dp", "mp"), None),
        P("mp", "dp"),
        P(None, "dp", "mp"),
        P("mp", "dp"),
        P(None, "dp"),
    )
    rows = P("dp", None)
    return jax.shard_map(
        body,
        mesh=mesh,
        in_specs=(rows, P("dp"), rows) + params * 3,
        out_specs=(rows, rows, P()) + params * 3,
        check_vma=False,
    )
```
